32 devices in a mesh: rep: 8 (over z, y), col: 4 (over x, core).
Axes of the slice: x: 2, y: 2, z: 4, core: 2. Of those that a mesh axis runs over, the one named last changes fastest.
Arguments:
- momentum: float32 [8, 288, 8192], P('rep', None, 'col'), may hold values from -6 to 6
- grads: bfloat16 [2, 8, 288, 8192], P(None, 'rep', None, 'col'), may hold values from -3 to 3
- weights: float32 [288, 8192], P(None, 'col'), may hold values from -6 to 6
- right_factor: float32 [8192, 256], P('col'), may hold values from -0.0625 to 0.0625
Outputs:
- new_weights: float32 [288, 8192], P(None, 'col')
- new_momentum: float32 [8, 288, 8192], P('rep', None, 'col')
- new_right: float32 [8192, 256], P('col')
The draws below stay inside these ranges and needn't reach their ends.
All inputs are finite; a program needn't handle non-finite values.
Results may differ from the reference program's by a relative error of at most 0.0003.
Values sent between devices are 32-bit elements; how exact they have to be, the bound alone decides.
No kernel may reach another device: no remote copies, remote signals or barrier semaphores. Data moves between devices by JAX's collectives and lax.ppermute only.
A program may use at most 64 MiB of HBM per device.

```python
import math
import jax
import jax.numpy as jnp
from jax import lax

ROWS = 288
N = 8192
R = 256
STEPS = 2
REPLICAS = 8
N_REP = 8


def draw_momentum(key, part):
    shared_key = jax.random.fold_in(key, 11)
    private_key = jax.random.fold_in(key, 12)
    shared = jax.random.truncated_normal(shared_key, -3.0, 3.0, (ROWS, N), jnp.float32)
    private = 0.3 * jax.random.truncated_normal(private_key, -3.0, 3.0, (N_REP, ROWS, N), jnp.float32)
    return shared[None] + private


def level_of(key, shape, cuts, smallest, largest):
    def one(dim, shards_of):
        draws = jax.random.uniform(jax.random.fold_in(jax.random.fold_in(key, 6), dim), (shards_of,), jnp.float32, smallest / len(cuts), largest / len(cuts))
        return jnp.repeat(jnp.exp(draws), shape[dim] // shards_of).reshape((-1,) + (1,) * (len(shape) - dim - 1))

    level = one(*cuts[0])
    for cut in cuts[1:]:
        level = level * one(*cut)
    return level


def scatter_about(own_key, shape, scale, bound, split=(), kind=jnp.bfloat16):
    result = scale * jax.random.normal(own_key, shape, jnp.float32)
    if split:
        result = result * level_of(own_key, shape, split, -0.22, 0.18)
    return jnp.clip(result, -bound, bound).astype(kind)


def setup_inputs(seed: int = 0) -> dict:
    key_of = jax.random.split(jax.random.key(seed), 5)
    momentum = draw_momentum(jax.random.fold_in(key_of[4], 71), 0)
    grads = scatter_about(key_of[1], (STEPS, REPLICAS, ROWS, N), 0.5, 3.0, ((1, 8), (3, 4)))
    weights = scatter_about(key_of[2], (ROWS, N), 1.0, 6.0, ((1, 4),), jnp.float32)
    right_factor = scatter_about(key_of[3], (N, R), N ** -0.5, 0.0625, ((0, 4),), jnp.float32)
    return dict(momentum=momentum, grads=grads, weights=weights, right_factor=right_factor)


precise = lax.Precision.HIGHEST
damping = 0.1
rate_base = 0.2
epsilon = 1e-06

def reference(momentum, grads, weights, right_factor):
    moment = momentum
    weight_now = weights
    step_size = rate_base * math.sqrt(ROWS * N / R)
    for section_index in range(STEPS):
        combined = moment + grads[section_index].astype(jnp.float32)
        averaged = lax.optimization_barrier(jnp.mean(combined, axis=0))
        left_raw = jnp.dot(averaged, right_factor, precision=precise)
        gram_matrix = jnp.dot(left_raw.T, left_raw, precision=precise)
        lower_factor = jnp.linalg.cholesky(gram_matrix)
        left_factor = jax.scipy.linalg.solve_triangular(lower_factor, left_raw.T, lower=True).T
        right_raw = jnp.dot(averaged.T, left_factor, precision=precise)
        correction = jnp.dot(left_factor, right_raw.T, precision=precise)
        moment = combined - damping * correction[None]
        totals = lax.optimization_barrier(jnp.sum(right_raw * right_raw, axis=0))
        right_factor = right_raw / jnp.sqrt(totals + epsilon)
        weight_now = weight_now - step_size * jnp.dot(left_factor, right_factor.T, precision=precise)
    return (weight_now, moment, right_factor)
```

```python
import functools
import math

import jax
import jax.numpy as jnp
from jax import lax
from jax.experimental import pallas as pl
from jax.experimental.pallas import tpu as pltpu
from jax.sharding import PartitionSpec as P

STEPS = 2
DAMPING = 0.1
RATE = 0.2
EPS = 1e-06
LANES = 128
GROUP = 8

precise = lax.Precision.HIGHEST
VMEM = pl.BlockSpec(memory_space=pltpu.VMEM)
SMEM = pl.BlockSpec(memory_space=pltpu.SMEM)
F32 = jnp.float32
BF16 = jnp.bfloat16


def dot(a, b, ca=1, cb=0):
    return lax.dot_general(
        a, b, (((ca,), (cb,)), ((), ())), precision=precise, preferred_element_type=F32
    )


def halves(x):
    high = x.astype(BF16)
    return high, (x - high.astype(F32)).astype(BF16)


def dot3(a, b, ca=1, cb=0):
    def one(x, y):
        return lax.dot_general(x, y, (((ca,), (cb,)), ((), ())), preferred_element_type=F32)

    return one(a[0], b[0]) + (one(a[0], b[1]) + one(a[1], b[0]))


def cost(flops, moved):
    return pl.CostEstimate(flops=int(flops), bytes_accessed=int(moved), transcendentals=0)


def eliminate(rows, group):
    count, n = len(rows), len(rows) * 8
    lane = lax.broadcasted_iota(jnp.int32, (8, n), 1)
    sub = lax.broadcasted_iota(jnp.int32, (8, n), 0)
    rows = list(rows)
    for j in range(0, n, group):
        rb, s = j // 8, j % 8

        def across(x, k):
            return jnp.broadcast_to(x[:, k : k + 1], (8, n))

        def down(x, k):
            return jnp.broadcast_to(x[k : k + 1, :], (8, n))

        column = [{i: across(rows[i], j + k) for i in range(rb, count)} for k in range(group)]
        unit = [[None] * group for _ in range(group)]
        scaled = [[None] * group for _ in range(group)]
        inverse = [None] * group
        for a in range(group):
            for b in range(a + 1):
                v = down(column[b][rb], s + a)
                for e in range(b):
                    v = v - unit[a][e] * scaled[b][e]
                scaled[a][b] = v
                if b < a:
                    unit[a][b] = v * inverse[b]
            inverse[a] = 1.0 / scaled[a][a]
        inside = (lane >= j) & (lane < j + group)
        pivot_rows = []
        for k in range(group):
            r = jnp.where(lane == j + k, 1.0, jnp.where(inside, 0.0, down(rows[rb], s + k)))
            for e in range(k):
                r = r - unit[k][e] * pivot_rows[e]
            pivot_rows.append(r)
        for i in range(rb, count):
            if i == rb and s + group == 8 and s == 0:
                out = rows[i]
                for k in range(group):
                    r = jnp.where(lane == j + k, scaled[k][k], pivot_rows[k])
                    out = jnp.where(sub == k, r, out)
                rows[i] = out
                continue
            left = []
            for k in range(group):
                v = column[k][i]
                for e in range(k):
                    v = v - unit[k][e] * left[e]
                left.append(v)
            y = jnp.where(inside, 0.0, rows[i])
            for k in range(group):
                m = left[k] * inverse[k]
                if i == rb:
                    m = jnp.where(sub > s + k, m, 0.0)
                y = y - m * pivot_rows[k]
            if i == rb:
                out = jnp.where(sub < s, rows[i], y)
                for k in range(group):
                    r = jnp.where(lane == j + k, scaled[k][k], pivot_rows[k])
                    out = jnp.where(sub == s + k, r, out)
                y = out
            rows[i] = y
    return rows


def inverse_factor(matrix):
    n = matrix.shape[0]
    rows = eliminate([matrix[8 * i : 8 * i + 8, :] for i in range(n // 8)], GROUP)
    rows = jnp.concatenate(rows, axis=0)
    lane = lax.broadcasted_iota(jnp.int32, (n, n), 1)
    sub = lax.broadcasted_iota(jnp.int32, (n, n), 0)
    pivots = jnp.sum(jnp.where(lane == sub, rows, 0.0), axis=1, keepdims=True)
    unit = jnp.where(lane < sub, rows, jnp.where(lane == sub, 1.0, 0.0))
    return unit / jnp.sqrt(pivots)


def orthonormal_columns(left_raw):
    width = left_raw.shape[1]
    blocks = [left_raw[:, i : i + LANES] for i in range(0, width, LANES)]
    done = []
    for block in blocks:
        for q in done:
            block = block - dot(q, dot(q, block, 0, 0))
        done.append(dot(block, inverse_factor(dot(block, block, 0, 0)), 1, 1))
    return jnp.concatenate(done, axis=1)


def orth_kernel(scaled, half, core_ref, mine_ref, other_ref, left_ref, leftt_ref, *norm_ref):
    first = core_ref[0] == 0
    mine, other = mine_ref[...], other_ref[...]
    top = jnp.where(first, mine, other)
    bottom = jnp.where(first, other, mine)
    left_raw = jnp.concatenate([top[:half], bottom[:half]], axis=0)
    if scaled:
        norm = jnp.sqrt(top[half : half + 1] + EPS)
        norm_ref[0][...] = norm
        left_raw = left_raw / norm
    left = orthonormal_columns(left_raw)
    left_ref[...] = left
    leftt_ref[...] = left.T


def orth(core, mine, other, half, scaled):
    rank = mine.shape[1]
    shapes = [
        jax.ShapeDtypeStruct((2 * half, rank), F32),
        jax.ShapeDtypeStruct((rank, 2 * half), F32),
    ]
    if scaled:
        shapes.append(jax.ShapeDtypeStruct((1, rank), F32))
    return pl.pallas_call(
        functools.partial(orth_kernel, scaled, half),
        out_shape=shapes,
        in_specs=[SMEM, VMEM, VMEM],
        out_specs=[VMEM] * len(shapes),
        cost_estimate=cost(1.5e10, 1e6),
        name="orth",
    )(core, mine, other)


def combine_kernel(half, inv, core_ref, mom_ref, grads_ref, right_ref, up_ref, dn_ref, keep_ref, send_ref, acc_ref):
    k = pl.program_id(0)
    rows = mom_ref.shape[1]
    total = mom_ref[0] + grads_ref[0, 0].astype(F32)
    later = grads_ref[1, 0].astype(F32)
    w = total.shape[1] // 2
    up_ref[0, :rows] = total[:, :w]
    dn_ref[0, :rows] = total[:, w:]
    up_ref[0, rows:] = later[:, :w]
    dn_ref[0, rows:] = later[:, w:]
    part = dot(total, right_ref[...])

    @pl.when(k == 0)
    def _():
        acc_ref[...] = part

    @pl.when(k > 0)
    def _():
        acc_ref[...] += part

    @pl.when(k == pl.num_programs(0) - 1)
    def _():
        first = core_ref[0] == 0
        whole = acc_ref[...] * inv
        top, bottom = whole[:half], whole[half:]
        keep_ref[...] = jnp.where(first, top, bottom)
        send_ref[...] = jnp.where(first, bottom, top)


def combine(core, momentum, grads, right_factor, n):
    _, rows, cols = momentum.shape
    rank = right_factor.shape[1]
    half, w = rows // 2, cols // n
    chunks = jax.ShapeDtypeStruct((n, 2 * rows, w // 2), F32)
    part = jax.ShapeDtypeStruct((half, rank), F32)
    return pl.pallas_call(
        functools.partial(combine_kernel, half, 1.0 / n),
        out_shape=[chunks, chunks, part, part],
        grid=(n,),
        in_specs=[
            SMEM,
            pl.BlockSpec((1, rows, w), lambda k: (0, 0, k)),
            pl.BlockSpec((2, 1, rows, w), lambda k: (0, 0, 0, k)),
            pl.BlockSpec((w, rank), lambda k: (k, 0)),
        ],
        out_specs=[
            pl.BlockSpec((1, 2 * rows, w // 2), lambda k: (k, 0, 0)),
            pl.BlockSpec((1, 2 * rows, w // 2), lambda k: (k, 0, 0)),
            pl.BlockSpec((half, rank), lambda k: (0, 0)),
            pl.BlockSpec((half, rank), lambda k: (0, 0)),
        ],
        scratch_shapes=[pltpu.VMEM((rows, rank), F32)],
        cost_estimate=cost(12 * rows * cols * rank, 16 * rows * cols),
        name="combine",
    )(core, momentum, grads, right_factor)


def middle_kernel(half, inv, core_ref, up_ref, dn_ref, left_ref, leftt_ref, keep_ref, send_ref):
    rows = 2 * half
    mean = jnp.concatenate([up_ref[...], dn_ref[...]], axis=1) * inv
    averaged, later = mean[:rows], mean[rows:]
    right_raw = dot(averaged, left_ref[...], 0, 0)
    averaged = averaged - DAMPING * dot(left_ref[...], right_raw, 1, 1) + later
    part = dot(averaged, right_raw)
    squares = jnp.sum(right_raw * right_raw, axis=0, keepdims=True)
    squares = jnp.broadcast_to(squares, (8, squares.shape[1]))
    first = core_ref[0] == 0
    top, bottom = part[:half], part[half:]
    keep_ref[:half] = jnp.where(first, top, bottom)
    send_ref[:half] = jnp.where(first, bottom, top)
    keep_ref[half:] = squares
    send_ref[half:] = squares


def middle(core, up, dn, left, leftt, n):
    rows, rank = left.shape
    part = jax.ShapeDtypeStruct((rows // 2 + 8, rank), F32)
    return pl.pallas_call(
        functools.partial(middle_kernel, rows // 2, 1.0 / n),
        out_shape=[part, part],
        in_specs=[SMEM] + [VMEM] * 4,
        out_specs=[VMEM] * 2,
        cost_estimate=cost(36 * rows * rank * rank, 4e6),
        name="middle",
    )(core, up, dn, left, leftt)


def update_kernel(n, inv, rate, order_ref, *refs):
    ups, dns = refs[:n], refs[n : 2 * n]
    mom_ref, grads_ref, w_ref, l1_ref, l1t_ref, l2_ref, l2t_ref, norm_ref = refs[2 * n : 2 * n + 8]
    mom_out, w_out, right_out, sq_out = refs[2 * n + 8 : 2 * n + 12]
    buf, sem, split = refs[2 * n + 12], refs[2 * n + 13], refs[2 * n + 14 :]
    k = pl.program_id(0)
    rows = mom_ref.shape[1]
    w = buf.shape[2] // 2

    def copies(i, slot):
        return (
            pltpu.make_async_copy(ups[i], buf.at[slot, :, pl.ds(0, w)], sem.at[slot, 0]),
            pltpu.make_async_copy(dns[(n - i) % n], buf.at[slot, :, pl.ds(w, w)], sem.at[slot, 1]),
        )

    def start(i):
        for c in copies(i, i % 2):
            c.start()

    @pl.when(k == 0)
    def _():
        start(0)
        for ref, src in zip(split, (l1_ref[...], l1t_ref[...], l2_ref[...], l2t_ref[...], l1_ref[...] / norm_ref[...])):
            ref[0], ref[1] = halves(src)

    for i in range(1, n):

        @pl.when(k == i - 1)
        def _():
            start(i)

    slot = lax.rem(k, 2)
    for c in copies(0, slot):
        c.wait()
    l1, l1t, l2, l2t, l1n = [(ref[0], ref[1]) for ref in split]
    mean = buf[slot] * inv
    averaged, later = mean[:rows], mean[rows:]
    y1 = halves(dot3(l1t, halves(averaged)))
    correction = DAMPING * dot3(l1, y1)
    averaged = averaged - correction + later
    y2 = dot3(l2t, halves(averaged))
    moment = mom_ref[0] + grads_ref[0, 0].astype(F32) - correction + grads_ref[1, 0].astype(F32)
    mom_out[0] = moment - DAMPING * dot3(l2, halves(y2))
    w_out[...] = w_ref[...] - rate * dot3(l1n, y1)
    right = y2.T
    right_out[...] = right
    squares = jnp.sum(right * right, axis=0, keepdims=True)

    @pl.when(k == 0)
    def _():
        sq_out[...] = squares

    @pl.when(k > 0)
    def _():
        sq_out[...] += squares


def update(order, ups, dns, momentum, grads, weights, l1, l1t, l2, l2t, norm, rate):
    n = len(ups)
    _, rows, cols = momentum.shape
    rank = l1.shape[1]
    w = cols // n
    any_space = pl.BlockSpec(memory_space=pl.ANY)

    def whole(shape):
        return pl.BlockSpec(shape, lambda k, order: (0,) * len(shape))

    return pl.pallas_call(
        functools.partial(update_kernel, n, 1.0 / n, rate),
        out_shape=[
            jax.ShapeDtypeStruct(momentum.shape, F32),
            jax.ShapeDtypeStruct(weights.shape, F32),
            jax.ShapeDtypeStruct((cols, rank), F32),
            jax.ShapeDtypeStruct((1, rank), F32),
        ],
        grid_spec=pltpu.PrefetchScalarGridSpec(
            num_scalar_prefetch=1,
            grid=(n,),
            in_specs=[any_space] * (2 * n)
            + [
                pl.BlockSpec((1, rows, w), lambda k, order: (0, 0, order[k])),
                pl.BlockSpec((2, 1, rows, w), lambda k, order: (0, 0, 0, order[k])),
                pl.BlockSpec((rows, w), lambda k, order: (0, order[k])),
                whole((rows, rank)),
                whole((rank, rows)),
                whole((rows, rank)),
                whole((rank, rows)),
                whole((1, rank)),
            ],
            out_specs=[
                pl.BlockSpec((1, rows, w), lambda k, order: (0, 0, order[k])),
                pl.BlockSpec((rows, w), lambda k, order: (0, order[k])),
                pl.BlockSpec((w, rank), lambda k, order: (order[k], 0)),
                whole((1, rank)),
            ],
            scratch_shapes=[
                pltpu.VMEM((2, 2 * rows, w), F32),
                pltpu.SemaphoreType.DMA((2, 2)),
                pltpu.VMEM((2, rows, rank), BF16),
                pltpu.VMEM((2, rank, rows), BF16),
                pltpu.VMEM((2, rows, rank), BF16),
                pltpu.VMEM((2, rank, rows), BF16),
                pltpu.VMEM((2, rows, rank), BF16),
            ],
        ),
        cost_estimate=cost(30 * rows * cols * rank, 32 * rows * cols),
        name="update",
    )(order, *ups, *dns, momentum, grads, weights, l1, l1t, l2, l2t, norm)


def finish_kernel(rate, right_ref, w_ref, l2_ref, total_ref, right_out, w_out):
    right = right_ref[...] / jnp.sqrt(total_ref[...] + EPS)
    right_out[...] = right
    w_out[...] = w_ref[...] - rate * dot3(halves(l2_ref[...]), halves(right), 1, 1)


def finish(right_raw, weights, l2, totals, rate, n):
    cols, rank = right_raw.shape
    rows = weights.shape[0]
    w = cols // n
    return pl.pallas_call(
        functools.partial(finish_kernel, rate),
        out_shape=[
            jax.ShapeDtypeStruct((cols, rank), F32),
            jax.ShapeDtypeStruct((rows, cols), F32),
        ],
        grid=(n,),
        in_specs=[
            pl.BlockSpec((w, rank), lambda k: (k, 0)),
            pl.BlockSpec((rows, w), lambda k: (0, k)),
            pl.BlockSpec((rows, rank), lambda k: (0, 0)),
            pl.BlockSpec((1, rank), lambda k: (0, 0)),
        ],
        out_specs=[
            pl.BlockSpec((w, rank), lambda k: (k, 0)),
            pl.BlockSpec((rows, w), lambda k: (0, k)),
        ],
        input_output_aliases={0: 0, 1: 1},
        cost_estimate=cost(6 * rows * cols * rank, 16 * rows * cols),
        name="finish",
    )(right_raw, weights, l2, totals)


def flip(x, axis, bit):
    size = lax.axis_size(axis)
    return lax.ppermute(x, axis, [(i, i ^ bit) for i in range(size)])


def bits(size):
    return [1 << b for b in range(size.bit_length() - 1)]


def all_sum(keep, send):
    x = keep + flip(send, "col", 1)
    for bit in bits(lax.axis_size("col"))[1:]:
        x = x + flip(x, "col", bit)
    for bit in bits(lax.axis_size("rep")):
        x = x + flip(x, "rep", bit)
    return x, flip(x, "col", 1)


def ring_shards(rate, momentum, grads, weights, right_factor):
    n = lax.axis_size("rep")
    half = momentum.shape[1] // 2
    ring = list(range(0, n, 2)) + list(range(n - 1, 0, -2))
    place = jnp.array([ring.index(i) for i in range(n)], jnp.int32)[lax.axis_index("rep")]
    ahead = [(ring[i], ring[(i + 1) % n]) for i in range(n)]
    back = [(b, a) for a, b in ahead]
    core = (lax.axis_index("col") & 1).astype(jnp.int32)[None]

    up_all, dn_all, keep, send = combine(core, momentum, grads, right_factor, n)

    def chunk(x, k):
        return lax.dynamic_index_in_dim(x, lax.rem(place + k + n, n), 0, keepdims=False)

    left = orth(core, *all_sum(keep, send), half, False)
    up, dn = chunk(up_all, -1), chunk(dn_all, 1)
    for k in range(1, n):
        up = lax.ppermute(up, "rep", ahead) + chunk(up_all, -1 - k + n)
        dn = lax.ppermute(dn, "rep", back) + chunk(dn_all, 1 + k)
    ups, dns = [up], [dn]
    for k in range(1, n):
        ups.append(lax.ppermute(ups[-1], "rep", ahead))
        dns.append(lax.ppermute(dns[-1], "rep", back))
    l1, l1t = left
    keep, send = middle(core, up, dn, l1, l1t, n)
    l2, l2t, norm = orth(core, *all_sum(keep, send), half, True)
    order = lax.rem(place - jnp.arange(n, dtype=jnp.int32) + n, n)
    new_momentum, weights, right_raw, squares = update(
        order, ups, dns, momentum, grads, weights, l1, l1t, l2, l2t, norm, rate
    )
    for bit in bits(lax.axis_size("col")):
        squares = squares + flip(squares, "col", bit)
    new_right, weights = finish(right_raw, weights, l2, squares, rate, n)
    return weights, new_momentum, new_right


def plain_orthonormal(left_raw):
    half = left_raw.shape[0] // 2
    zero = jnp.zeros((1,), jnp.int32)
    return orth(zero, left_raw[:half], left_raw[half:], half, False)[0]


def plain_shards(rate, momentum, grads, weights, right_factor):
    n = lax.axis_size("rep")
    moment = momentum[0]
    combined = moment + grads[0, 0].astype(F32)
    averaged, later = lax.psum((combined / n, grads[1, 0].astype(F32) / n), "rep")
    for step in range(STEPS):
        if step > 0:
            combined = moment + grads[step, 0].astype(F32)
            averaged = averaged + later
        left = plain_orthonormal(lax.psum(dot(averaged, right_factor), "col"))
        right_raw = dot(averaged, left, 0, 0)
        correction = DAMPING * dot(left, right_raw, 1, 1)
        moment = combined - correction
        averaged = averaged - correction
        totals = lax.psum(jnp.sum(right_raw * right_raw, axis=0), "col")
        right_factor = right_raw / jnp.sqrt(totals + EPS)
        weights = weights - rate * dot(left, right_factor, 1, 1)
    return weights, moment[None], right_factor


def solution(mesh):
    def body(momentum, grads, weights, right_factor):
        rep, col = mesh.shape["rep"], mesh.shape["col"]
        _, rows, cols = momentum.shape
        rank = right_factor.shape[1]
        rate = RATE * math.sqrt(rows * cols / rank)
        powers = rep & (rep - 1) == 0 and col & (col - 1) == 0 and col > 1
        ring = powers and 2 < rep <= 16 and cols % (2 * LANES * rep * col) == 0 and rows % 16 == 0
        shards = ring_shards if ring else plain_shards
        return jax.shard_map(
            functools.partial(shards, rate),
            mesh=mesh,
            in_specs=(
                P("rep", None, "col"),
                P(None, "rep", None, "col"),
                P(None, "col"),
                P("col", None),
            ),
            out_specs=(P(None, "col"), P("rep", None, "col"), P("col", None)),
            check_vma=False,
        )(momentum, grads, weights, right_factor)

    return body
```

```python
import functools
import math

import jax
import jax.numpy as jnp
from jax import lax
from jax.experimental import pallas as pl
from jax.experimental.pallas import tpu as pltpu
from jax.sharding import PartitionSpec as P

STEPS = 2
DAMPING = 0.1
RATE = 0.2
EPS = 1e-06
LANES = 128
GROUP = 8

precise = lax.Precision.HIGHEST
VMEM = pl.BlockSpec(memory_space=pltpu.VMEM)
SMEM = pl.BlockSpec(memory_space=pltpu.SMEM)
F32 = jnp.float32
BF16 = jnp.bfloat16


def dot(a, b, ca=1, cb=0):
    return lax.dot_general(
        a, b, (((ca,), (cb,)), ((), ())), precision=precise, preferred_element_type=F32
    )


def halves(x):
    high = x.astype(BF16)
    return high, (x - high.astype(F32)).astype(BF16)


def dot3(a, b, ca=1, cb=0):
    def one(x, y):
        return lax.dot_general(x, y, (((ca,), (cb,)), ((), ())), preferred_element_type=F32)

    return one(a[0], b[0]) + (one(a[0], b[1]) + one(a[1], b[0]))


def cost(flops, moved):
    return pl.CostEstimate(flops=int(flops), bytes_accessed=int(moved), transcendentals=0)


def eliminate(rows, group):
    count, n = len(rows), len(rows) * 8
    lane = lax.broadcasted_iota(jnp.int32, (8, n), 1)
    sub = lax.broadcasted_iota(jnp.int32, (8, n), 0)
    rows = list(rows)
    for j in range(0, n, group):
        rb, s = j // 8, j % 8

        def across(x, k):
            return jnp.broadcast_to(x[:, k : k + 1], (8, n))

        def down(x, k):
            return jnp.broadcast_to(x[k : k + 1, :], (8, n))

        column = [{i: across(rows[i], j + k) for i in range(rb, count)} for k in range(group)]
        unit = [[None] * group for _ in range(group)]
        scaled = [[None] * group for _ in range(group)]
        inverse = [None] * group
        for a in range(group):
            for b in range(a + 1):
                v = down(column[b][rb], s + a)
                for e in range(b):
                    v = v - unit[a][e] * scaled[b][e]
                scaled[a][b] = v
                if b < a:
                    unit[a][b] = v * inverse[b]
            inverse[a] = 1.0 / scaled[a][a]
        inside = (lane >= j) & (lane < j + group)
        pivot_rows = []
        for k in range(group):
            r = jnp.where(lane == j + k, 1.0, jnp.where(inside, 0.0, down(rows[rb], s + k)))
            for e in range(k):
                r = r - unit[k][e] * pivot_rows[e]
            pivot_rows.append(r)
        for i in range(rb, count):
            if i == rb and s + group == 8 and s == 0:
                out = rows[i]
                for k in range(group):
                    r = jnp.where(lane == j + k, scaled[k][k], pivot_rows[k])
                    out = jnp.where(sub == k, r, out)
                rows[i] = out
                continue
            left = []
            for k in range(group):
                v = column[k][i]
                for e in range(k):
                    v = v - unit[k][e] * left[e]
                left.append(v)
            y = jnp.where(inside, 0.0, rows[i])
            for k in range(group):
                m = left[k] * inverse[k]
                if i == rb:
                    m = jnp.where(sub > s + k, m, 0.0)
                y = y - m * pivot_rows[k]
            if i == rb:
                out = jnp.where(sub < s, rows[i], y)
                for k in range(group):
                    r = jnp.where(lane == j + k, scaled[k][k], pivot_rows[k])
                    out = jnp.where(sub == s + k, r, out)
                y = out
            rows[i] = y
    return rows


def inverse_factor(matrix):
    n = matrix.shape[0]
    rows = eliminate([matrix[8 * i : 8 * i + 8, :] for i in range(n // 8)], GROUP)
    rows = jnp.concatenate(rows, axis=0)
    lane = lax.broadcasted_iota(jnp.int32, (n, n), 1)
    sub = lax.broadcasted_iota(jnp.int32, (n, n), 0)
    pivots = jnp.sum(jnp.where(lane == sub, rows, 0.0), axis=1, keepdims=True)
    unit = jnp.where(lane < sub, rows, jnp.where(lane == sub, 1.0, 0.0))
    return unit / jnp.sqrt(pivots)


def orthonormal_blocks(blocks, done):
    out = []
    for block in blocks:
        for q in out:
            block = block - dot(q, dot(q, block, 0, 0))
        out.append(dot(block, inverse_factor(dot(block, block, 0, 0)), 1, 1))
    return out


def column_blocks(x):
    return [x[:, i : i + LANES] for i in range(0, x.shape[1], LANES)]


def first_kernel(scaled, me_ref, *refs):
    count = len(refs) - 3 - scaled
    parts, (left_ref, rest_ref), raw = refs[:count], refs[count : count + 2], refs[-1]
    rows = raw.shape[0] // count
    for d in range(count):
        at = pl.multiple_of((me_ref[0] ^ d) * rows, 8)
        raw[pl.ds(at, rows), :] = parts[d][:rows]
    left_raw = raw[...]
    if scaled:
        norm = jnp.sqrt(parts[0][rows : rows + 1] + EPS)
        refs[count + 2][...] = norm
        left_raw = left_raw / norm
    blocks = column_blocks(left_raw)
    middle = len(blocks) // 2
    done = orthonormal_blocks(blocks[:middle], [])
    left_ref[...] = jnp.concatenate(done, axis=1)
    rest = blocks[middle:]
    for q in done:
        rest = [block - dot(q, dot(q, block, 0, 0)) for block in rest]
    rest_ref[...] = jnp.concatenate(rest, axis=1)


def second_kernel(left_ref, rest_ref, out_ref, outt_ref):
    done = orthonormal_blocks(column_blocks(rest_ref[...]), [])
    left = jnp.concatenate([left_ref[...]] + done, axis=1)
    out_ref[...] = left
    outt_ref[...] = left.T


def orth_first(me, parts, rows, scaled):
    rank = parts[0].shape[1]
    part = jax.ShapeDtypeStruct((rows, rank // 2), F32)
    shapes = [part, part] + [jax.ShapeDtypeStruct((1, rank), F32)] * scaled
    return pl.pallas_call(
        functools.partial(first_kernel, scaled),
        out_shape=shapes,
        in_specs=[SMEM] + [VMEM] * len(parts),
        out_specs=[VMEM] * len(shapes),
        scratch_shapes=[pltpu.VMEM((rows, rank), F32)],
        cost_estimate=cost(6e9, 1e6),
        name="orth_first",
    )(me, *parts)


def orth_second(left, rest):
    rows, rank = left.shape[0], left.shape[1] + rest.shape[1]
    return pl.pallas_call(
        second_kernel,
        out_shape=[
            jax.ShapeDtypeStruct((rows, rank), F32),
            jax.ShapeDtypeStruct((rank, rows), F32),
        ],
        in_specs=[VMEM] * 2,
        out_specs=[VMEM] * 2,
        cost_estimate=cost(6e9, 1e6),
        name="orth_second",
    )(left, rest)


def combine_kernel(count, inv, me_ref, mom_ref, grads_ref, right_ref, up_ref, dn_ref, *refs):
    parts, acc_ref = refs[:count], refs[count]
    k = pl.program_id(0)
    rows = mom_ref.shape[1]
    total = mom_ref[0] + grads_ref[0, 0].astype(F32)
    later = grads_ref[1, 0].astype(F32)
    w = total.shape[1] // 2
    up_ref[0, :rows] = total[:, :w]
    dn_ref[0, :rows] = total[:, w:]
    up_ref[0, rows:] = later[:, :w]
    dn_ref[0, rows:] = later[:, w:]
    part = dot(total, right_ref[...])

    @pl.when(k == 0)
    def _():
        acc_ref[...] = part

    @pl.when(k > 0)
    def _():
        acc_ref[...] += part

    @pl.when(k == pl.num_programs(0) - 1)
    def _():
        acc_ref[...] *= inv
        block = rows // count
        for d in range(count):
            at = pl.multiple_of((me_ref[0] ^ d) * block, 8)
            parts[d][...] = acc_ref[pl.ds(at, block), :]


def combine(me, momentum, grads, right_factor, n, count):
    _, rows, cols = momentum.shape
    rank = right_factor.shape[1]
    w = cols // n
    chunks = jax.ShapeDtypeStruct((n, 2 * rows, w // 2), F32)
    part = jax.ShapeDtypeStruct((rows // count, rank), F32)
    out = pl.pallas_call(
        functools.partial(combine_kernel, count, 1.0 / n),
        out_shape=[chunks, chunks] + [part] * count,
        grid=(n,),
        in_specs=[
            SMEM,
            pl.BlockSpec((1, rows, w), lambda k: (0, 0, k)),
            pl.BlockSpec((2, 1, rows, w), lambda k: (0, 0, 0, k)),
            pl.BlockSpec((w, rank), lambda k: (k, 0)),
        ],
        out_specs=[
            pl.BlockSpec((1, 2 * rows, w // 2), lambda k: (k, 0, 0)),
            pl.BlockSpec((1, 2 * rows, w // 2), lambda k: (k, 0, 0)),
        ]
        + [pl.BlockSpec((rows // count, rank), lambda k: (0, 0))] * count,
        scratch_shapes=[pltpu.VMEM((rows, rank), F32)],
        cost_estimate=cost(12 * rows * cols * rank, 16 * rows * cols),
        name="combine",
    )(me, momentum, grads, right_factor)
    return out[0], out[1], out[2:]


def middle_kernel(inv, me_ref, up_ref, dn_ref, left_ref, leftt_ref, up_out, dn_out, *refs):
    parts, scratch = refs[:-1], refs[-1]
    rows, rank = left_ref.shape
    w = up_ref.shape[1]
    mean = jnp.concatenate([up_ref[...], dn_ref[...]], axis=1) * inv
    averaged, later = mean[:rows], mean[rows:]
    right = dot(leftt_ref[...], averaged)
    averaged = averaged - DAMPING * dot(left_ref[...], right) + later
    up_out[:rank] = right[:, :w]
    dn_out[:rank] = right[:, w:]
    up_out[rank:] = averaged[:, :w]
    dn_out[rank:] = averaged[:, w:]
    scratch[...] = dot(averaged, right, 1, 1)
    squares = dot(jnp.ones((8, 2 * w), F32), right * right, 1, 1)
    block = rows // len(parts)
    for d, ref in enumerate(parts):
        at = pl.multiple_of((me_ref[0] ^ d) * block, 8)
        ref[:block] = scratch[pl.ds(at, block), :]
        ref[block:] = squares


def middle(me, up, dn, left, leftt, n, count):
    rows, rank = left.shape
    w = up.shape[1]
    part = jax.ShapeDtypeStruct((rows // count + 8, rank), F32)
    ring = jax.ShapeDtypeStruct((rank + rows, w), F32)
    out = pl.pallas_call(
        functools.partial(middle_kernel, 1.0 / n),
        out_shape=[ring, ring] + [part] * count,
        in_specs=[SMEM] + [VMEM] * 4,
        out_specs=[VMEM] * (2 + count),
        scratch_shapes=[pltpu.VMEM((rows, rank), F32)],
        cost_estimate=cost(36 * rows * rank * rank, 4e6),
        name="middle",
    )(me, up, dn, left, leftt)
    return out[0], out[1], out[2:]


def fetcher(n, ups, dns, buf, sem, first, count):
    k = pl.program_id(0)
    w = buf.shape[2] // 2

    def copies(i, slot):
        at = pl.ds(first, count)
        return (
            pltpu.make_async_copy(ups[i].at[at, :], buf.at[slot, :, pl.ds(0, w)], sem.at[slot, 0]),
            pltpu.make_async_copy(dns[(n - i) % n].at[at, :], buf.at[slot, :, pl.ds(w, w)], sem.at[slot, 1]),
        )

    @pl.when(k == 0)
    def _():
        for c in copies(0, 0):
            c.start()

    for i in range(1, n):

        @pl.when(k == i - 1)
        def _():
            for c in copies(i, i % 2):
                c.start()

    slot = lax.rem(k, 2)
    for c in copies(0, slot):
        c.wait()
    return buf[slot]


def project_kernel(n, rank, order_ref, *refs):
    ups, dns, (leftt_ref, y_out, sq_out, buf, sem, split) = refs[:n], refs[n : 2 * n], refs[2 * n :]
    k = pl.program_id(0)

    @pl.when(k == 0)
    def _():
        split[0], split[1] = halves(leftt_ref[...])

    averaged = fetcher(n, ups, dns, buf, sem, rank, leftt_ref.shape[1])
    y = dot3((split[0], split[1]), halves(averaged))
    y_out[0] = y
    squares = dot(jnp.ones((8, y.shape[1]), F32), y * y, 1, 1)

    @pl.when(k == 0)
    def _():
        sq_out[...] = squares

    @pl.when(k > 0)
    def _():
        sq_out[...] += squares


def moment_kernel(n, rank, order_ref, *refs):
    ups, dns = refs[:n], refs[n : 2 * n]
    mom_ref, grads_ref, y_ref, l1_ref, l2_ref, mom_out, buf, sem, split = refs[2 * n :]

    @pl.when(pl.program_id(0) == 0)
    def _():
        split[0], split[1] = halves(jnp.concatenate([l1_ref[...], l2_ref[...]], axis=1))

    y1 = fetcher(n, ups, dns, buf, sem, 0, rank)
    y = jnp.concatenate([y1, y_ref[0]], axis=0)
    moment = mom_ref[0] + grads_ref[0, 0].astype(F32) + grads_ref[1, 0].astype(F32)
    mom_out[0] = moment - DAMPING * dot3((split[0], split[1]), halves(y))


def weight_kernel(n, rank, rate, order_ref, *refs):
    ups, dns = refs[:n], refs[n : 2 * n]
    w_ref, y_ref, l1_ref, l2_ref, norm_ref, total_ref, w_out, right_out, buf, sem, split = refs[2 * n :]
    norm = jnp.sqrt(total_ref[0:1] + EPS)

    @pl.when(pl.program_id(0) == 0)
    def _():
        left = jnp.concatenate([l1_ref[...] / norm_ref[...], l2_ref[...] / norm], axis=1)
        split[0], split[1] = halves(left)

    y1 = fetcher(n, ups, dns, buf, sem, 0, rank)
    y = jnp.concatenate([y1, y_ref[0]], axis=0)
    w_out[...] = w_ref[...] - rate * dot3((split[0], split[1]), halves(y))
    right_out[...] = y_ref[0].T / norm


def chunked(kernel, name, n, order, rings, extra, extra_specs, outs, out_specs, count, split, flops, moved):
    w = 2 * rings[0].shape[1]
    return pl.pallas_call(
        kernel,
        out_shape=outs,
        grid_spec=pltpu.PrefetchScalarGridSpec(
            num_scalar_prefetch=1,
            grid=(n,),
            in_specs=[pl.BlockSpec(memory_space=pl.ANY)] * len(rings) + extra_specs,
            out_specs=out_specs,
            scratch_shapes=[
                pltpu.VMEM((2, count, w), F32),
                pltpu.SemaphoreType.DMA((2, 2)),
                pltpu.VMEM((2,) + split, BF16),
            ],
        ),
        cost_estimate=cost(flops, moved),
        name=name,
    )(order, *rings, *extra)


def whole(shape):
    return pl.BlockSpec(shape, lambda k, order: (0,) * len(shape))


def flip(x, axis, bits):
    size = lax.axis_size(axis)
    return lax.ppermute(x, axis, [(i, i ^ bits) for i in range(size)])


def all_sum_stages(box):
    cols, reps = lax.axis_size("col"), lax.axis_size("rep")

    def scatter():
        x = box["parts"][0]
        for d in range(1, cols):
            x = x + flip(box["parts"][d], "col", d)
        box["x"] = x

    def exchange(masks):
        def stage():
            x = box["x"]
            got = [flip(x, "rep", m) for m in masks]
            if len(got) == 3:
                x = (x + got[0]) + (got[1] + got[2])
            else:
                x = x + got[0]
            box["x"] = x

        return stage

    def gather():
        x = box["x"]
        box["parts"] = [x] + [flip(x, "col", d) for d in range(1, cols)]

    masks = [[1 << b] for b in range(reps.bit_length() - 1)]
    return [scatter] + [exchange(m) for m in masks] + [gather]


def ring_shards(rate, momentum, grads, weights, right_factor):
    n, count = lax.axis_size("rep"), lax.axis_size("col")
    _, rows, cols = momentum.shape
    rank = right_factor.shape[1]
    ring = list(range(0, n, 2)) + list(range(n - 1, 0, -2))
    rep = lax.axis_index("rep")
    place = jnp.where(rep % 2 == 0, rep // 2, n - 1 - rep // 2).astype(jnp.int32)
    ahead = [(ring[i], ring[(i + 1) % n]) for i in range(n)]
    back = [(b, a) for a, b in ahead]
    me = lax.axis_index("col").astype(jnp.int32)[None]
    order = lax.rem(place - jnp.arange(n, dtype=jnp.int32) + n, n)

    def chunk(x, k):
        return lax.dynamic_index_in_dim(x, lax.rem(place + k + 2 * n, n), 0, keepdims=False)

    def tie(box, *arrays):
        keys = list(box)
        tied = lax.optimization_barrier(([box[k] for k in keys], list(arrays)))
        box.update(zip(keys, tied[0]))
        return tied[1]

    def windows(box, scaled):
        stages = all_sum_stages(box)

        def first():
            out = orth_first(me, box.pop("parts"), rows, scaled)
            box.pop("x")
            box["left"], box["rest"] = out[:2]
            if scaled:
                box["norm"] = out[2]

        def second():
            box["left"], box["leftt"] = orth_second(box.pop("left"), box.pop("rest"))

        work = [stages[i : i + 2] for i in range(0, len(stages), 2)]
        work[-1].append(first)
        return work + [[second]]

    up_all, dn_all, parts = combine(me, momentum, grads, right_factor, n, count)
    box = {"parts": list(parts)}
    work = windows(box, False)
    up, dn = chunk(up_all, -1), chunk(dn_all, 1)
    for k in range(1, n):
        up, dn = lax.ppermute(up, "rep", ahead), lax.ppermute(dn, "rep", back)
        if work:
            for stage in work.pop(0):
                stage()
            up, dn = tie(box, up, dn)
        up, dn = up + chunk(up_all, -1 - k), dn + chunk(dn_all, 1 + k)
    for stage in sum(work, []):
        stage()
    l1 = box["left"]
    up, dn, parts = middle(me, up, dn, l1, box["leftt"], n, count)

    box = {"parts": list(parts)}
    work = windows(box, True)
    ups, dns = [up], [dn]
    for k in range(1, n):
        up, dn = lax.ppermute(up, "rep", ahead), lax.ppermute(dn, "rep", back)
        if work:
            for stage in work.pop(0):
                stage()
            up, dn = tie(box, up, dn)
        ups.append(up)
        dns.append(dn)
    for stage in sum(work, []):
        stage()
    l2, l2t, norm = box["left"], box["leftt"], box["norm"]

    w = cols // n
    rings = ups + dns
    unit = 2 * rows * cols * rank
    y_spec = pl.BlockSpec((1, rank, w), lambda k, order: (k, 0, 0))
    block = pl.BlockSpec((rows, w), lambda k, order: (0, order[k]))
    moment_block = pl.BlockSpec((1, rows, w), lambda k, order: (0, 0, order[k]))
    grads_block = pl.BlockSpec((2, 1, rows, w), lambda k, order: (0, 0, 0, order[k]))
    y, squares = chunked(
        functools.partial(project_kernel, n, rank), "project", n, order, rings, [l2t], [whole((rank, rows))],
        [jax.ShapeDtypeStruct((n, rank, w), F32), jax.ShapeDtypeStruct((8, rank), F32)],
        [y_spec, whole((8, rank))], rows, (rank, rows), 3 * unit, 8 * rows * cols,
    )
    (new_momentum,) = chunked(
        functools.partial(moment_kernel, n, rank), "moment", n, order, rings, [momentum, grads, y, l1, l2],
        [moment_block, grads_block, y_spec, whole((rows, rank)), whole((rows, rank))],
        [jax.ShapeDtypeStruct(momentum.shape, F32)], [moment_block],
        rank, (rows, 2 * rank), 6 * unit, 20 * rows * cols,
    )
    for bit in range(count.bit_length() - 1):
        squares = squares + flip(squares, "col", 1 << bit)
    new_weights, new_right = chunked(
        functools.partial(weight_kernel, n, rank, rate), "weight", n, order, rings,
        [weights, y, l1, l2, norm, squares],
        [block, y_spec, whole((rows, rank)), whole((rows, rank)), whole((1, rank)), whole((8, rank))],
        [jax.ShapeDtypeStruct(weights.shape, F32), jax.ShapeDtypeStruct((cols, rank), F32)],
        [block, pl.BlockSpec((w, rank), lambda k, order: (order[k], 0))],
        rank, (rows, 2 * rank), 6 * unit, 20 * rows * cols,
    )
    return new_weights, new_momentum, new_right


def plain_orthonormal(left_raw):
    zero = jnp.zeros((1,), jnp.int32)
    left, rest = orth_first(zero, [left_raw], left_raw.shape[0], False)
    return orth_second(left, rest)[0]


def plain_shards(rate, momentum, grads, weights, right_factor):
    n = lax.axis_size("rep")
    moment = momentum[0]
    combined = moment + grads[0, 0].astype(F32)
    averaged, later = lax.psum((combined / n, grads[1, 0].astype(F32) / n), "rep")
    for step in range(STEPS):
        if step > 0:
            combined = moment + grads[step, 0].astype(F32)
            averaged = averaged + later
        left = plain_orthonormal(lax.psum(dot(averaged, right_factor), "col"))
        right_raw = dot(averaged, left, 0, 0)
        correction = DAMPING * dot(left, right_raw, 1, 1)
        moment = combined - correction
        averaged = averaged - correction
        totals = lax.psum(jnp.sum(right_raw * right_raw, axis=0), "col")
        right_factor = right_raw / jnp.sqrt(totals + EPS)
        weights = weights - rate * dot(left, right_factor, 1, 1)
    return weights, moment[None], right_factor


def solution(mesh):
    def body(momentum, grads, weights, right_factor):
        rep, col = mesh.shape["rep"], mesh.shape["col"]
        _, rows, cols = momentum.shape
        rank = right_factor.shape[1]
        rate = RATE * math.sqrt(rows * cols / rank)
        powers = rep & (rep - 1) == 0 and col & (col - 1) == 0 and col > 1
        fits = cols % (2 * LANES * rep * col) == 0 and rows % (8 * col) == 0
        ring = powers and 2 < rep <= 16 and col <= 8 and fits
        shards = ring_shards if ring else plain_shards
        return jax.shard_map(
            functools.partial(shards, rate),
            mesh=mesh,
            in_specs=(
                P("rep", None, "col"),
                P(None, "rep", None, "col"),
                P(None, "col"),
                P("col", None),
            ),
            out_specs=(P(None, "col"), P("rep", None, "col"), P("col", None)),
            check_vma=False,
        )(momentum, grads, weights, right_factor)

    return body
```

```python
import functools
import math

import jax
import jax.numpy as jnp
from jax import lax
from jax.experimental import pallas as pl
from jax.experimental.pallas import tpu as pltpu
from jax.sharding import PartitionSpec as P


STEPS = 2
DAMPING = 0.1
RATE = 0.2
EPS = 1e-06
LANES = 128
GROUP = 8

precise = lax.Precision.HIGHEST
VMEM = pl.BlockSpec(memory_space=pltpu.VMEM)
SMEM = pl.BlockSpec(memory_space=pltpu.SMEM)
F32 = jnp.float32
BF16 = jnp.bfloat16


def dot(a, b, ca=1, cb=0):
    return lax.dot_general(
        a, b, (((ca,), (cb,)), ((), ())), precision=precise, preferred_element_type=F32
    )


def halves(x):
    high = x.astype(BF16)
    return high, (x - high.astype(F32)).astype(BF16)


def dot3(a, b, ca=1, cb=0):
    def one(x, y):
        return lax.dot_general(x, y, (((ca,), (cb,)), ((), ())), preferred_element_type=F32)

    return one(a[0], b[0]) + (one(a[0], b[1]) + one(a[1], b[0]))


def cost(flops, moved):
    return pl.CostEstimate(flops=int(flops), bytes_accessed=int(moved), transcendentals=0)


def eliminate(rows, group):
    count, n = len(rows), len(rows) * 8
    lane = lax.broadcasted_iota(jnp.int32, (8, n), 1)
    sub = lax.broadcasted_iota(jnp.int32, (8, n), 0)
    rows = list(rows)
    for j in range(0, n, group):
        rb, s = j // 8, j % 8

        def across(x, k):
            return jnp.broadcast_to(x[:, k : k + 1], (8, n))

        def down(x, k):
            return jnp.broadcast_to(x[k : k + 1, :], (8, n))

        column = [{i: across(rows[i], j + k) for i in range(rb, count)} for k in range(group)]
        unit = [[None] * group for _ in range(group)]
        scaled = [[None] * group for _ in range(group)]
        inverse = [None] * group
        for a in range(group):
            for b in range(a + 1):
                v = down(column[b][rb], s + a)
                for e in range(b):
                    v = v - unit[a][e] * scaled[b][e]
                scaled[a][b] = v
                if b < a:
                    unit[a][b] = v * inverse[b]
            inverse[a] = 1.0 / scaled[a][a]
        inside = (lane >= j) & (lane < j + group)
        pivot_rows = []
        for k in range(group):
            r = jnp.where(lane == j + k, 1.0, jnp.where(inside, 0.0, down(rows[rb], s + k)))
            for e in range(k):
                r = r - unit[k][e] * pivot_rows[e]
            pivot_rows.append(r)
        for i in range(rb, count):
            if i == rb and s + group == 8 and s == 0:
                out = rows[i]
                for k in range(group):
                    r = jnp.where(lane == j + k, scaled[k][k], pivot_rows[k])
                    out = jnp.where(sub == k, r, out)
                rows[i] = out
                continue
            left = []
            for k in range(group):
                v = column[k][i]
                for e in range(k):
                    v = v - unit[k][e] * left[e]
                left.append(v)
            y = jnp.where(inside, 0.0, rows[i])
            for k in range(group):
                m = left[k] * inverse[k]
                if i == rb:
                    m = jnp.where(sub > s + k, m, 0.0)
                y = y - m * pivot_rows[k]
            if i == rb:
                out = jnp.where(sub < s, rows[i], y)
                for k in range(group):
                    r = jnp.where(lane == j + k, scaled[k][k], pivot_rows[k])
                    out = jnp.where(sub == s + k, r, out)
                y = out
            rows[i] = y
    return rows


def inverse_factor(matrix):
    n = matrix.shape[0]
    rows = eliminate([matrix[8 * i : 8 * i + 8, :] for i in range(n // 8)], GROUP)
    rows = jnp.concatenate(rows, axis=0)
    lane = lax.broadcasted_iota(jnp.int32, (n, n), 1)
    sub = lax.broadcasted_iota(jnp.int32, (n, n), 0)
    pivots = jnp.sum(jnp.where(lane == sub, rows, 0.0), axis=1, keepdims=True)
    unit = jnp.where(lane < sub, rows, jnp.where(lane == sub, 1.0, 0.0))
    return unit / jnp.sqrt(pivots)


def orthonormal_blocks(blocks):
    out = []
    for block in blocks:
        for q in out:
            block = block - dot(q, dot(q, block, 0, 0))
        out.append(dot(block, inverse_factor(dot(block, block, 0, 0)), 1, 1))
    return out


def column_blocks(x):
    return [x[:, i : i + LANES] for i in range(0, x.shape[1], LANES)]


def first_kernel(scaled, me_ref, *refs):
    count = len(refs) - 3 - scaled
    parts, (left_ref, rest_ref), raw = refs[:count], refs[count : count + 2], refs[-1]
    rows = raw.shape[0] // count
    for d in range(count):
        at = pl.multiple_of((me_ref[0] ^ d) * rows, 8)
        raw[pl.ds(at, rows), :] = parts[d][:rows]
    left_raw = raw[...]
    if scaled:
        norm = jnp.sqrt(parts[0][rows : rows + 1] + EPS)
        refs[count + 2][...] = norm
        left_raw = left_raw / norm
    blocks = column_blocks(left_raw)
    middle = len(blocks) // 2
    done = orthonormal_blocks(blocks[:middle])
    left_ref[...] = jnp.concatenate(done, axis=1)
    rest = blocks[middle:]
    for q in done:
        rest = [block - dot(q, dot(q, block, 0, 0)) for block in rest]
    rest_ref[...] = jnp.concatenate(rest, axis=1)


def second_kernel(left_ref, rest_ref, out_ref, outt_ref):
    done = orthonormal_blocks(column_blocks(rest_ref[...]))
    left = jnp.concatenate([left_ref[...]] + done, axis=1)
    out_ref[...] = left
    outt_ref[...] = left.T


def orth_first(me, parts, rows, scaled):
    rank = parts[0].shape[1]
    part = jax.ShapeDtypeStruct((rows, rank // 2), F32)
    shapes = [part, part] + [jax.ShapeDtypeStruct((1, rank), F32)] * scaled
    return pl.pallas_call(
        functools.partial(first_kernel, scaled),
        out_shape=shapes,
        in_specs=[SMEM] + [VMEM] * len(parts),
        out_specs=[VMEM] * len(shapes),
        scratch_shapes=[pltpu.VMEM((rows, rank), F32)],
        cost_estimate=cost(6e9, 1e6),
        name="orth_first",
    )(me, *parts)


def orth_second(left, rest):
    rows, rank = left.shape[0], left.shape[1] + rest.shape[1]
    return pl.pallas_call(
        second_kernel,
        out_shape=[
            jax.ShapeDtypeStruct((rows, rank), F32),
            jax.ShapeDtypeStruct((rank, rows), F32),
        ],
        in_specs=[VMEM] * 2,
        out_specs=[VMEM] * 2,
        cost_estimate=cost(6e9, 1e6),
        name="orth_second",
    )(left, rest)


def chunk_rows(mom, grads):
    return jnp.concatenate([mom[0] + grads[0, 0].astype(F32), grads[1, 0].astype(F32)], axis=0)


def lead_kernel(at_ref, mom_up, grads_up, mom_dn, grads_dn, up_ref, dn_ref):
    up_ref[...] = chunk_rows(mom_up[...], grads_up[...])
    dn_ref[...] = chunk_rows(mom_dn[...], grads_dn[...])


def lead(at, momentum, grads, n):
    _, rows, cols = momentum.shape
    w = cols // n // 2
    part = jax.ShapeDtypeStruct((2 * rows, w), F32)
    specs = []
    for side in range(2):
        specs.append(pl.BlockSpec((1, rows, w), lambda i, at, side=side: (0, 0, 2 * at[side] + side)))
        specs.append(pl.BlockSpec((2, 1, rows, w), lambda i, at, side=side: (0, 0, 0, 2 * at[side] + side)))
    return pl.pallas_call(
        lead_kernel,
        out_shape=[part, part],
        grid_spec=pltpu.PrefetchScalarGridSpec(
            num_scalar_prefetch=1,
            grid=(1,),
            in_specs=specs,
            out_specs=[whole((2 * rows, w))] * 2,
        ),
        cost_estimate=cost(4 * rows * w, 32 * rows * w),
        name="lead",
    )(at, momentum, grads, momentum, grads)


def combine_kernel(count, inv, me_ref, mom_ref, grads_ref, right_ref, up_ref, dn_ref, both_ref, *refs):
    parts, acc_ref = refs[:count], refs[count]
    k = pl.program_id(0)
    rows = mom_ref.shape[1]
    total = mom_ref[0] + grads_ref[0, 0].astype(F32)
    later = grads_ref[1, 0].astype(F32)
    both_ref[...] = total + later
    w = total.shape[1] // 2
    up_ref[0, :rows] = total[:, :w]
    dn_ref[0, :rows] = total[:, w:]
    up_ref[0, rows:] = later[:, :w]
    dn_ref[0, rows:] = later[:, w:]
    part = dot(total, right_ref[...])

    @pl.when(k == 0)
    def _():
        acc_ref[...] = part

    @pl.when(k > 0)
    def _():
        acc_ref[...] += part

    @pl.when(k == pl.num_programs(0) - 1)
    def _():
        acc_ref[...] *= inv
        block = rows // count
        for d in range(count):
            at = pl.multiple_of((me_ref[0] ^ d) * block, 8)
            parts[d][...] = acc_ref[pl.ds(at, block), :]


def combine(me, momentum, grads, right_factor, n, count):
    _, rows, cols = momentum.shape
    rank = right_factor.shape[1]
    w = cols // n
    chunks = jax.ShapeDtypeStruct((n, 2 * rows, w // 2), F32)
    part = jax.ShapeDtypeStruct((rows // count, rank), F32)
    out = pl.pallas_call(
        functools.partial(combine_kernel, count, 1.0 / n),
        out_shape=[chunks, chunks, jax.ShapeDtypeStruct((rows, cols), F32)] + [part] * count,
        grid=(n,),
        in_specs=[
            SMEM,
            pl.BlockSpec((1, rows, w), lambda k: (0, 0, k)),
            pl.BlockSpec((2, 1, rows, w), lambda k: (0, 0, 0, k)),
            pl.BlockSpec((w, rank), lambda k: (k, 0)),
        ],
        out_specs=[
            pl.BlockSpec((1, 2 * rows, w // 2), lambda k: (k, 0, 0)),
            pl.BlockSpec((1, 2 * rows, w // 2), lambda k: (k, 0, 0)),
            pl.BlockSpec((rows, w), lambda k: (0, k)),
        ]
        + [pl.BlockSpec((rows // count, rank), lambda k: (0, 0))] * count,
        scratch_shapes=[pltpu.VMEM((rows, rank), F32)],
        cost_estimate=cost(12 * rows * cols * rank, 16 * rows * cols),
        name="combine",
    )(me, momentum, grads, right_factor)
    return out[0], out[1], out[2], out[3:]


def reduced_kernel(inv, at_ref, up_ref, dn_ref, up_all, dn_all, left_ref, leftt_ref, up_out, dn_out):
    rows, rank = left_ref.shape
    w = up_ref.shape[1]
    up, dn = up_ref[...] + up_all[0], dn_ref[...] + dn_all[0]
    mean = jnp.concatenate([up, dn], axis=1) * inv
    averaged, later = mean[:rows], mean[rows:]
    right = dot(leftt_ref[...], averaged)
    averaged = averaged - DAMPING * dot(left_ref[...], right) + later
    up_out[:rank] = right[:, :w]
    dn_out[:rank] = right[:, w:]
    up_out[rank:] = averaged[:, :w]
    dn_out[rank:] = averaged[:, w:]


def reduced(place, up, dn, up_all, dn_all, left, leftt, n):
    rows, rank = left.shape
    w = up.shape[1]
    ring = jax.ShapeDtypeStruct((rank + rows, w), F32)
    mine = pl.BlockSpec((1, 2 * rows, w), lambda i, at: (at[0], 0, 0))
    return pl.pallas_call(
        functools.partial(reduced_kernel, 1.0 / n),
        out_shape=[ring, ring],
        grid_spec=pltpu.PrefetchScalarGridSpec(
            num_scalar_prefetch=1,
            grid=(1,),
            in_specs=[whole(up.shape), whole(dn.shape), mine, mine, whole((rows, rank)), whole((rank, rows))],
            out_specs=[whole(ring.shape)] * 2,
        ),
        cost_estimate=cost(24 * rows * rank * rank, 4e6),
        name="reduced",
    )(place, up, dn, up_all, dn_all, left, leftt)


def partial_kernel(rank, me_ref, up_ref, dn_ref, *refs):
    parts, scratch = refs[:-1], refs[-1]
    rows = up_ref.shape[0] - rank
    both = jnp.concatenate([up_ref[...], dn_ref[...]], axis=1)
    right, averaged = both[:rank], both[rank:]
    scratch[...] = dot(averaged, right, 1, 1)
    squares = dot(jnp.ones((8, both.shape[1]), F32), right * right, 1, 1)
    block = rows // len(parts)
    for d, ref in enumerate(parts):
        at = pl.multiple_of((me_ref[0] ^ d) * block, 8)
        ref[:block] = scratch[pl.ds(at, block), :]
        ref[block:] = squares


def partial_raw(me, up, dn, rank, count):
    rows = up.shape[0] - rank
    part = jax.ShapeDtypeStruct((rows // count + 8, rank), F32)
    return pl.pallas_call(
        functools.partial(partial_kernel, rank),
        out_shape=[part] * count,
        in_specs=[SMEM] + [VMEM] * 2,
        out_specs=[VMEM] * count,
        scratch_shapes=[pltpu.VMEM((rows, rank), F32)],
        cost_estimate=cost(12 * rows * rank * rank, 2e6),
        name="partial",
    )(me, up, dn)


def squares_kernel(rank, up_ref, dn_ref, leftt_ref, out_ref):
    averaged = jnp.concatenate([up_ref[rank:], dn_ref[rank:]], axis=1)
    right = dot(leftt_ref[...], averaged)
    out_ref[...] = dot(jnp.ones((8, right.shape[1]), F32), right * right, 1, 1)


def squares_of(up, dn, leftt):
    rank = leftt.shape[0]
    return pl.pallas_call(
        functools.partial(squares_kernel, rank),
        out_shape=jax.ShapeDtypeStruct((8, rank), F32),
        in_specs=[VMEM] * 3,
        out_specs=VMEM,
        cost_estimate=cost(12 * rank * rank * rank, 2e6),
        name="squares",
    )(up, dn, leftt)


def fetcher(n, ups, dns, buf, sem):
    k = pl.program_id(0)
    w = buf.shape[2] // 2

    def copies(i, slot):
        return (
            pltpu.make_async_copy(ups[i], buf.at[slot, :, pl.ds(0, w)], sem.at[slot, 0]),
            pltpu.make_async_copy(dns[(n - i) % n], buf.at[slot, :, pl.ds(w, w)], sem.at[slot, 1]),
        )

    @pl.when(k == 0)
    def _():
        for c in copies(0, 0):
            c.start()

    for i in range(1, n):

        @pl.when(k == i - 1)
        def _():
            for c in copies(i, i % 2):
                c.start()

    slot = lax.rem(k, 2)
    for c in copies(0, slot):
        c.wait()
    return buf[slot]


def finish_kernel(n, rate, order_ref, *refs):
    ups, dns = refs[:n], refs[n : 2 * n]
    both_ref, w_ref, l1_ref, l2_ref, l2t_ref, norm_ref, total_ref = refs[2 * n : 2 * n + 7]
    mom_out, w_out, right_out, buf, sem, project, update = refs[2 * n + 7 :]
    rows, rank = l1_ref.shape
    norm = jnp.sqrt(total_ref[0:1] + EPS)

    @pl.when(pl.program_id(0) == 0)
    def _():
        project[0], project[1] = halves(l2t_ref[...])
        l1, l2 = l1_ref[...], l2_ref[...]
        moment = DAMPING * jnp.concatenate([l1, l2], axis=1)
        weight = rate * jnp.concatenate([l1 / norm_ref[...], l2 / norm], axis=1)
        update[0], update[1] = halves(jnp.concatenate([moment, weight], axis=0))

    chunk = fetcher(n, ups, dns, buf, sem)
    y1, averaged = chunk[:rank], chunk[rank:]
    y2 = dot3((project[0], project[1]), halves(averaged))
    change = dot3((update[0], update[1]), halves(jnp.concatenate([y1, y2], axis=0)))
    mom_out[0] = both_ref[...] - change[:rows]
    w_out[...] = w_ref[...] - change[rows:]
    right_out[...] = y2.T / norm


def finish(order, rings, both, weights, l1, l2, l2t, norm, totals, rate):
    n = len(rings) // 2
    rows, cols = both.shape
    rank = l1.shape[1]
    w = cols // n
    block = pl.BlockSpec((rows, w), lambda k, order: (0, order[k]))
    return pl.pallas_call(
        functools.partial(finish_kernel, n, rate),
        out_shape=[
            jax.ShapeDtypeStruct((1, rows, cols), F32),
            jax.ShapeDtypeStruct((rows, cols), F32),
            jax.ShapeDtypeStruct((cols, rank), F32),
        ],
        grid_spec=pltpu.PrefetchScalarGridSpec(
            num_scalar_prefetch=1,
            grid=(n,),
            in_specs=[pl.BlockSpec(memory_space=pl.ANY)] * len(rings)
            + [block, block, whole((rows, rank)), whole((rows, rank)), whole((rank, rows))]
            + [whole((1, rank)), whole((8, rank))],
            out_specs=[
                pl.BlockSpec((1, rows, w), lambda k, order: (0, 0, order[k])),
                block,
                pl.BlockSpec((w, rank), lambda k, order: (order[k], 0)),
            ],
            scratch_shapes=[
                pltpu.VMEM((2, rank + rows, w), F32),
                pltpu.SemaphoreType.DMA((2, 2)),
                pltpu.VMEM((2, rank, rows), BF16),
                pltpu.VMEM((2, 2 * rows, 2 * rank), BF16),
            ],
        ),
        cost_estimate=cost(30 * rows * cols * rank, 32 * rows * cols),
        name="finish",
    )(order, *rings, both, weights, l1, l2, l2t, norm, totals)


def whole(shape):
    return pl.BlockSpec(shape, lambda k, order: (0,) * len(shape))


def flip(x, axis, bits):
    size = lax.axis_size(axis)
    return lax.ppermute(x, axis, [(i, i ^ bits) for i in range(size)])


def all_sum_stages(box):
    cols, reps = lax.axis_size("col"), lax.axis_size("rep")

    def scatter():
        got = [flip(box["parts"][d], "col", d) for d in range(1, cols)]
        x = box["parts"][0]
        for other in got:
            x = x + other
        box["x"] = x

    def exchange(bit):
        def stage():
            got = flip(box["x"], "rep", 1 << bit)
            box["x"] = box["x"] + got

        return stage

    def gather():
        box["parts"] = [box["x"]] + [flip(box["x"], "col", d) for d in range(1, cols)]

    return [scatter] + [exchange(b) for b in range(reps.bit_length() - 1)] + [gather]


def ring_shards(rate, momentum, grads, weights, right_factor):
    n, count = lax.axis_size("rep"), lax.axis_size("col")
    _, rows, _ = momentum.shape
    rank = right_factor.shape[1]
    ring = list(range(0, n, 2)) + list(range(n - 1, 0, -2))
    rep = lax.axis_index("rep")
    place = jnp.where(rep % 2 == 0, rep // 2, n - 1 - rep // 2).astype(jnp.int32)
    ahead = [(ring[i], ring[(i + 1) % n]) for i in range(n)]
    back = [(b, a) for a, b in ahead]
    me = lax.axis_index("col").astype(jnp.int32)[None]
    order = lax.rem(place - jnp.arange(n, dtype=jnp.int32) + n, n)

    def chunk(x, k):
        return lax.dynamic_index_in_dim(x, lax.rem(place + k + 2 * n, n), 0, keepdims=False)

    def tie(box, *arrays):
        keys = list(box)
        tied = lax.optimization_barrier(([box[k] for k in keys], list(arrays)))
        box.update(zip(keys, tied[0]))
        return tied[1]

    def step(up, dn):
        return lax.ppermute(up, "rep", ahead), lax.ppermute(dn, "rep", back)

    def windows(box, scaled):
        stages = all_sum_stages(box)

        def first():
            out = orth_first(me, box.pop("parts"), rows, scaled)
            box.pop("x")
            box["left"], box["rest"] = out[:2]
            if scaled:
                box["norm"] = out[2]

        def second():
            box["left"], box["leftt"] = orth_second(box.pop("left"), box.pop("rest"))

        return [stages[:2]] + [[s] for s in stages[2:-2]] + [stages[-2:], [first], [second]]

    box = {}

    def prepare():
        up_all, dn_all, both, parts = combine(me, momentum, grads, right_factor, n, count)
        box.update(up_all=up_all, dn_all=dn_all, both=both, parts=list(parts))

    work = [[prepare]] + windows(box, False)
    up, dn = lead(lax.rem(jnp.stack([place + n - 1, place + 1]), n), momentum, grads, n)
    for k in range(1, n):
        up, dn = step(up, dn)
        if work:
            for stage in work.pop(0):
                stage()
            up, dn = tie(box, up, dn)
        if k < n - 1:
            up, dn = up + chunk(box["up_all"], -1 - k), dn + chunk(box["dn_all"], 1 + k)
    for stage in sum(work, []):
        stage()
    l1 = box["left"]
    both = box["both"]
    up, dn = reduced(place[None], up, dn, box["up_all"], box["dn_all"], l1, box["leftt"], n)

    box = {}
    mine = (up, dn)

    def begin():
        box["parts"] = list(partial_raw(me, *mine, rank, count))

    def total_columns():
        x = squares_of(*mine, box["leftt"])
        got = [flip(x, "col", d) for d in range(1, count)]
        terms = [x] + got
        while len(terms) > 1:
            terms = [a + b for a, b in zip(terms[::2], terms[1::2])]
        box["total"] = terms[0]

    def total_bit(bit):
        def stage():
            got = flip(box["total"], "rep", 1 << bit)
            box["total"] = box["total"] + got

        return stage

    work = windows(box, True)
    work[0].insert(0, begin)
    bits = [total_bit(b) for b in range(n.bit_length() - 1)]
    work += [[total_columns, bits[0]], bits[1:]]
    ups, dns = [up], [dn]
    for _ in range(1, n):
        up, dn = step(up, dn)
        if work:
            for stage in work.pop(0):
                stage()
            up, dn = tie(box, up, dn)
        ups.append(up)
        dns.append(dn)
    for stage in sum(work, []):
        stage()
    new_momentum, new_weights, new_right = finish(
        order, ups + dns, both, weights, l1, box["left"], box["leftt"], box["norm"], box["total"], rate
    )
    return new_weights, new_momentum, new_right


def plain_orthonormal(left_raw):
    zero = jnp.zeros((1,), jnp.int32)
    left, rest = orth_first(zero, [left_raw], left_raw.shape[0], False)
    return orth_second(left, rest)[0]


def plain_shards(rate, momentum, grads, weights, right_factor):
    n = lax.axis_size("rep")
    moment = momentum[0]
    combined = moment + grads[0, 0].astype(F32)
    averaged, later = lax.psum((combined / n, grads[1, 0].astype(F32) / n), "rep")
    for step in range(STEPS):
        if step > 0:
            combined = moment + grads[step, 0].astype(F32)
            averaged = averaged + later
        left = plain_orthonormal(lax.psum(dot(averaged, right_factor), "col"))
        right_raw = dot(averaged, left, 0, 0)
        correction = DAMPING * dot(left, right_raw, 1, 1)
        moment = combined - correction
        averaged = averaged - correction
        totals = lax.psum(jnp.sum(right_raw * right_raw, axis=0), "col")
        right_factor = right_raw / jnp.sqrt(totals + EPS)
        weights = weights - rate * dot(left, right_factor, 1, 1)
    return weights, moment[None], right_factor


def solution(mesh):
    def body(momentum, grads, weights, right_factor):
        rep, col = mesh.shape["rep"], mesh.shape["col"]
        _, rows, cols = momentum.shape
        rank = right_factor.shape[1]
        rate = RATE * math.sqrt(rows * cols / rank)
        powers = rep & (rep - 1) == 0 and col & (col - 1) == 0 and col > 1
        fits = cols % (2 * LANES * rep * col) == 0 and rows % (8 * col) == 0
        ring = powers and 4 < rep <= 16 and col <= 8 and fits

        def shards(*args):
            return (ring_shards if ring else plain_shards)(rate, *args)

        step = jax.shard_map(
            shards,
            mesh=mesh,
            in_specs=(
                P("rep", None, "col"),
                P(None, "rep", None, "col"),
                P(None, "col"),
                P("col", None),
            ),
            out_specs=(P(None, "col"), P("rep", None, "col"), P("col", None)),
            check_vma=False,
        )
        return step(momentum, grads, weights, right_factor)

    return body
```

```python
import functools
import math

import jax
import jax.numpy as jnp
from jax import lax
from jax.experimental import pallas as pl
from jax.experimental.pallas import tpu as pltpu
from jax.sharding import PartitionSpec as P


STEPS = 2
DAMPING = 0.1
RATE = 0.2
EPS = 1e-06
LANES = 128
GROUP = 8

precise = lax.Precision.HIGHEST
VMEM = pl.BlockSpec(memory_space=pltpu.VMEM)
SMEM = pl.BlockSpec(memory_space=pltpu.SMEM)
F32 = jnp.float32
BF16 = jnp.bfloat16


def dot(a, b, ca=1, cb=0):
    return lax.dot_general(
        a, b, (((ca,), (cb,)), ((), ())), precision=precise, preferred_element_type=F32
    )


def halves(x):
    high = x.astype(BF16)
    return high, (x - high.astype(F32)).astype(BF16)


def dot3(a, b, ca=1, cb=0):
    def one(x, y):
        return lax.dot_general(x, y, (((ca,), (cb,)), ((), ())), preferred_element_type=F32)

    return one(a[0], b[0]) + (one(a[0], b[1]) + one(a[1], b[0]))


def grant(mib):
    return pltpu.CompilerParams(vmem_limit_bytes=mib << 20)


def cost(flops, moved):
    return pl.CostEstimate(flops=int(flops), bytes_accessed=int(moved), transcendentals=0)


def eliminate(rows, group):
    count, n = len(rows), len(rows) * 8
    lane = lax.broadcasted_iota(jnp.int32, (8, n), 1)
    sub = lax.broadcasted_iota(jnp.int32, (8, n), 0)
    rows = list(rows)
    for j in range(0, n, group):
        rb, s = j // 8, j % 8

        def across(x, k):
            return jnp.broadcast_to(x[:, k : k + 1], (8, n))

        def down(x, k):
            return jnp.broadcast_to(x[k : k + 1, :], (8, n))

        column = [{i: across(rows[i], j + k) for i in range(rb, count)} for k in range(group)]
        unit = [[None] * group for _ in range(group)]
        scaled = [[None] * group for _ in range(group)]
        inverse = [None] * group
        for a in range(group):
            for b in range(a + 1):
                v = down(column[b][rb], s + a)
                for e in range(b):
                    v = v - unit[a][e] * scaled[b][e]
                scaled[a][b] = v
                if b < a:
                    unit[a][b] = v * inverse[b]
            inverse[a] = 1.0 / scaled[a][a]
        inside = (lane >= j) & (lane < j + group)
        pivot_rows = []
        for k in range(group):
            r = jnp.where(lane == j + k, 1.0, jnp.where(inside, 0.0, down(rows[rb], s + k)))
            for e in range(k):
                r = r - unit[k][e] * pivot_rows[e]
            pivot_rows.append(r)
        for i in range(rb, count):
            if i == rb and s + group == 8 and s == 0:
                out = rows[i]
                for k in range(group):
                    r = jnp.where(lane == j + k, scaled[k][k], pivot_rows[k])
                    out = jnp.where(sub == k, r, out)
                rows[i] = out
                continue
            left = []
            for k in range(group):
                v = column[k][i]
                for e in range(k):
                    v = v - unit[k][e] * left[e]
                left.append(v)
            y = jnp.where(inside, 0.0, rows[i])
            for k in range(group):
                m = left[k] * inverse[k]
                if i == rb:
                    m = jnp.where(sub > s + k, m, 0.0)
                y = y - m * pivot_rows[k]
            if i == rb:
                out = jnp.where(sub < s, rows[i], y)
                for k in range(group):
                    r = jnp.where(lane == j + k, scaled[k][k], pivot_rows[k])
                    out = jnp.where(sub == s + k, r, out)
                y = out
            rows[i] = y
    return rows


def inverse_factor(matrix):
    n = matrix.shape[0]
    rows = eliminate([matrix[8 * i : 8 * i + 8, :] for i in range(n // 8)], GROUP)
    rows = jnp.concatenate(rows, axis=0)
    lane = lax.broadcasted_iota(jnp.int32, (n, n), 1)
    sub = lax.broadcasted_iota(jnp.int32, (n, n), 0)
    pivots = jnp.sum(jnp.where(lane == sub, rows, 0.0), axis=1, keepdims=True)
    unit = jnp.where(lane < sub, rows, jnp.where(lane == sub, 1.0, 0.0))
    return unit / jnp.sqrt(pivots)


def orthonormal_blocks(blocks):
    out = []
    for block in blocks:
        for q in out:
            block = block - dot(q, dot(q, block, 0, 0))
        out.append(dot(block, inverse_factor(dot(block, block, 0, 0)), 1, 1))
    return out


def column_blocks(x):
    return [x[:, i : i + LANES] for i in range(0, x.shape[1], LANES)]


def first_kernel(scaled, me_ref, *refs):
    count = len(refs) - 3 - scaled
    parts, (left_ref, rest_ref), raw = refs[:count], refs[count : count + 2], refs[-1]
    rows = raw.shape[0] // count
    for d in range(count):
        at = pl.multiple_of((me_ref[0] ^ d) * rows, 8)
        raw[pl.ds(at, rows), :] = parts[d][:rows]
    left_raw = raw[...]
    if scaled:
        norm = jnp.sqrt(parts[0][rows : rows + 1] + EPS)
        refs[count + 2][...] = norm
        left_raw = left_raw / norm
    blocks = column_blocks(left_raw)
    middle = len(blocks) // 2
    done = orthonormal_blocks(blocks[:middle])
    left_ref[...] = jnp.concatenate(done, axis=1)
    rest = blocks[middle:]
    for q in done:
        rest = [block - dot(q, dot(q, block, 0, 0)) for block in rest]
    rest_ref[...] = jnp.concatenate(rest, axis=1)


def second_kernel(left_ref, rest_ref, *refs):
    out_ref, outt_ref = refs[-2:] if len(refs) == 2 else refs[2:4]
    done = orthonormal_blocks(column_blocks(rest_ref[...]))
    left = jnp.concatenate([left_ref[...]] + done, axis=1)
    leftt = left.T
    out_ref[...] = left
    outt_ref[...] = leftt
    if len(refs) > 2:
        rank = leftt.shape[0]
        averaged = jnp.concatenate([refs[0][rank:], refs[1][rank:]], axis=1)
        right = dot(leftt, averaged)
        refs[4][...] = dot(jnp.ones((8, right.shape[1]), F32), right * right, 1, 1)


def orth_first(me, parts, rows, scaled):
    rank = parts[0].shape[1]
    part = jax.ShapeDtypeStruct((rows, rank // 2), F32)
    shapes = [part, part] + [jax.ShapeDtypeStruct((1, rank), F32)] * scaled
    return pl.pallas_call(
        functools.partial(first_kernel, scaled),
        out_shape=shapes,
        in_specs=[SMEM] + [VMEM] * len(parts),
        out_specs=[VMEM] * len(shapes),
        scratch_shapes=[pltpu.VMEM((rows, rank), F32)],
        cost_estimate=cost(6e9, 1e6),
        compiler_params=grant(12),
        name="orth_first",
    )(me, *parts)


def orth_second(left, rest, *mine):
    rows, rank = left.shape[0], left.shape[1] + rest.shape[1]
    shapes = [
        jax.ShapeDtypeStruct((rows, rank), F32),
        jax.ShapeDtypeStruct((rank, rows), F32),
    ]
    if mine:
        shapes.append(jax.ShapeDtypeStruct((8, rank), F32))
    return pl.pallas_call(
        second_kernel,
        out_shape=shapes,
        in_specs=[VMEM] * (2 + len(mine)),
        out_specs=[VMEM] * len(shapes),
        cost_estimate=cost(6e9, 1e6),
        compiler_params=grant(12),
        name="orth_second",
    )(left, rest, *mine)


def chunk_rows(mom, grads):
    return jnp.concatenate([mom[0] + grads[0, 0].astype(F32), grads[1, 0].astype(F32)], axis=0)


def lead_kernel(at_ref, mom_up, grads_up, mom_dn, grads_dn, up_ref, dn_ref):
    up_ref[...] = chunk_rows(mom_up[...], grads_up[...])
    dn_ref[...] = chunk_rows(mom_dn[...], grads_dn[...])


def lead(at, momentum, grads, n):
    _, rows, cols = momentum.shape
    w = cols // n // 2
    part = jax.ShapeDtypeStruct((2 * rows, w), F32)
    specs = []
    for side in range(2):
        specs.append(pl.BlockSpec((1, rows, w), lambda i, at, side=side: (0, 0, 2 * at[side] + side)))
        specs.append(pl.BlockSpec((2, 1, rows, w), lambda i, at, side=side: (0, 0, 0, 2 * at[side] + side)))
    return pl.pallas_call(
        lead_kernel,
        out_shape=[part, part],
        grid_spec=pltpu.PrefetchScalarGridSpec(
            num_scalar_prefetch=1,
            grid=(1,),
            in_specs=specs,
            out_specs=[whole((2 * rows, w))] * 2,
        ),
        cost_estimate=cost(4 * rows * w, 32 * rows * w),
        compiler_params=grant(58),
        name="lead",
    )(at, momentum, grads, momentum, grads)


def raw_kernel(count, inv, me_ref, mom_ref, grads_ref, right_ref, *refs):
    parts, acc_ref = refs[:count], refs[count]
    k = pl.program_id(0)
    rows = mom_ref.shape[1]
    part = dot(mom_ref[0] + grads_ref[0, 0].astype(F32), right_ref[...])

    @pl.when(k == 0)
    def _():
        acc_ref[...] = part

    @pl.when(k > 0)
    def _():
        acc_ref[...] += part

    @pl.when(k == pl.num_programs(0) - 1)
    def _():
        acc_ref[...] *= inv
        block = rows // count
        for d in range(count):
            at = pl.multiple_of((me_ref[0] ^ d) * block, 8)
            parts[d][...] = acc_ref[pl.ds(at, block), :]


def raw(me, momentum, grads, right_factor, n, count):
    _, rows, cols = momentum.shape
    rank = right_factor.shape[1]
    w = 2 * cols // n
    part = jax.ShapeDtypeStruct((rows // count, rank), F32)
    return pl.pallas_call(
        functools.partial(raw_kernel, count, 1.0 / n),
        out_shape=[part] * count,
        grid=(n // 2,),
        in_specs=[
            SMEM,
            pl.BlockSpec((1, rows, w), lambda k: (0, 0, k)),
            pl.BlockSpec((1, 1, rows, w), lambda k: (0, 0, 0, k)),
            pl.BlockSpec((w, rank), lambda k: (k, 0)),
        ],
        out_specs=[pl.BlockSpec((rows // count, rank), lambda k: (0, 0))] * count,
        scratch_shapes=[pltpu.VMEM((rows, rank), F32)],
        cost_estimate=cost(12 * rows * cols * rank, 8 * rows * cols),
        compiler_params=grant(16),
        name="raw",
    )(me, momentum, grads, right_factor)


def combine_kernel(mom_ref, grads_ref, after_ref, up_ref, dn_ref, both_ref):
    rows = mom_ref.shape[1]
    total = mom_ref[0] + grads_ref[0, 0].astype(F32)
    later = grads_ref[1, 0].astype(F32)
    both_ref[...] = total + later
    w = total.shape[1] // 2
    up_ref[0, :rows] = total[:, :w]
    dn_ref[0, :rows] = total[:, w:]
    up_ref[0, rows:] = later[:, :w]
    dn_ref[0, rows:] = later[:, w:]


def combine(momentum, grads, after, n):
    _, rows, cols = momentum.shape
    w = cols // n
    chunks = jax.ShapeDtypeStruct((n, 2 * rows, w // 2), F32)
    return pl.pallas_call(
        combine_kernel,
        out_shape=[chunks, chunks, jax.ShapeDtypeStruct((rows, cols), F32)],
        grid=(n,),
        in_specs=[
            pl.BlockSpec((1, rows, w), lambda k: (0, 0, k)),
            pl.BlockSpec((2, 1, rows, w), lambda k: (0, 0, 0, k)),
            pl.BlockSpec(memory_space=pl.ANY),
        ],
        out_specs=[
            pl.BlockSpec((1, 2 * rows, w // 2), lambda k: (k, 0, 0)),
            pl.BlockSpec((1, 2 * rows, w // 2), lambda k: (k, 0, 0)),
            pl.BlockSpec((rows, w), lambda k: (0, k)),
        ],
        cost_estimate=cost(3 * rows * cols, 20 * rows * cols),
        compiler_params=grant(16),
        name="combine",
    )(momentum, grads, after)


def reduced_kernel(inv, at_ref, up_ref, dn_ref, up_all, dn_all, left_ref, leftt_ref, up_out, dn_out):
    rows, rank = left_ref.shape
    w = up_ref.shape[1]
    up, dn = up_ref[...] + up_all[0], dn_ref[...] + dn_all[0]
    mean = jnp.concatenate([up, dn], axis=1) * inv
    averaged, later = mean[:rows], mean[rows:]
    right = dot(leftt_ref[...], averaged)
    averaged = averaged - DAMPING * dot(left_ref[...], right) + later
    up_out[:rank] = right[:, :w]
    dn_out[:rank] = right[:, w:]
    up_out[rank:] = averaged[:, :w]
    dn_out[rank:] = averaged[:, w:]


def reduced(place, up, dn, up_all, dn_all, left, leftt, n):
    rows, rank = left.shape
    w = up.shape[1]
    ring = jax.ShapeDtypeStruct((rank + rows, w), F32)
    mine = pl.BlockSpec((1, 2 * rows, w), lambda i, at: (at[0], 0, 0))
    return pl.pallas_call(
        functools.partial(reduced_kernel, 1.0 / n),
        out_shape=[ring, ring],
        grid_spec=pltpu.PrefetchScalarGridSpec(
            num_scalar_prefetch=1,
            grid=(1,),
            in_specs=[whole(up.shape), whole(dn.shape), mine, mine, whole((rows, rank)), whole((rank, rows))],
            out_specs=[whole(ring.shape)] * 2,
        ),
        cost_estimate=cost(24 * rows * rank * rank, 4e6),
        compiler_params=grant(12),
        name="reduced",
    )(place, up, dn, up_all, dn_all, left, leftt)


def partial_kernel(rank, me_ref, up_ref, dn_ref, *refs):
    parts, scratch = refs[:-1], refs[-1]
    rows = up_ref.shape[0] - rank
    both = jnp.concatenate([up_ref[...], dn_ref[...]], axis=1)
    right, averaged = both[:rank], both[rank:]
    scratch[...] = dot(averaged, right, 1, 1)
    squares = dot(jnp.ones((8, both.shape[1]), F32), right * right, 1, 1)
    block = rows // len(parts)
    for d, ref in enumerate(parts):
        at = pl.multiple_of((me_ref[0] ^ d) * block, 8)
        ref[:block] = scratch[pl.ds(at, block), :]
        ref[block:] = squares


def partial_raw(me, up, dn, rank, count):
    rows = up.shape[0] - rank
    part = jax.ShapeDtypeStruct((rows // count + 8, rank), F32)
    return pl.pallas_call(
        functools.partial(partial_kernel, rank),
        out_shape=[part] * count,
        in_specs=[SMEM] + [VMEM] * 2,
        out_specs=[VMEM] * count,
        scratch_shapes=[pltpu.VMEM((rows, rank), F32)],
        cost_estimate=cost(12 * rows * rank * rank, 2e6),
        compiler_params=grant(8),
        name="partial",
    )(me, up, dn)


def fetcher(n, ups, dns, buf, sem):
    k = pl.program_id(0)
    w = buf.shape[2] // 2

    def copies(i, slot):
        return (
            pltpu.make_async_copy(ups[i], buf.at[slot, :, pl.ds(0, w)], sem.at[slot, 0]),
            pltpu.make_async_copy(dns[(n - i) % n], buf.at[slot, :, pl.ds(w, w)], sem.at[slot, 1]),
        )

    @pl.when(k == 0)
    def _():
        for c in copies(0, 0):
            c.start()

    for i in range(1, n):

        @pl.when(k == i - 1)
        def _():
            for c in copies(i, i % 2):
                c.start()

    slot = lax.rem(k, 2)
    for c in copies(0, slot):
        c.wait()
    return buf[slot]


def finish_kernel(n, rate, order_ref, *refs):
    ups, dns = refs[:n], refs[n : 2 * n]
    both_ref, w_ref, l1_ref, l2_ref, l2t_ref, norm_ref, total_ref = refs[2 * n : 2 * n + 7]
    mom_out, w_out, right_out, buf, sem, project, update = refs[2 * n + 7 :]
    rows, rank = l1_ref.shape
    norm = jnp.sqrt(total_ref[0:1] + EPS)

    @pl.when(pl.program_id(0) == 0)
    def _():
        project[0], project[1] = halves(l2t_ref[...])
        l1, l2 = l1_ref[...], l2_ref[...]
        moment = DAMPING * jnp.concatenate([l1, l2], axis=1)
        weight = rate * jnp.concatenate([l1 / norm_ref[...], l2 / norm], axis=1)
        update[0], update[1] = halves(jnp.concatenate([moment, weight], axis=0))

    chunk = fetcher(n, ups, dns, buf, sem)
    y1, averaged = chunk[:rank], chunk[rank:]
    y2 = dot3((project[0], project[1]), halves(averaged))
    change = dot3((update[0], update[1]), halves(jnp.concatenate([y1, y2], axis=0)))
    mom_out[0] = both_ref[...] - change[:rows]
    w_out[...] = w_ref[...] - change[rows:]
    right_out[...] = y2.T / norm


def finish(order, rings, both, weights, l1, l2, l2t, norm, totals, rate):
    n = len(rings) // 2
    rows, cols = both.shape
    rank = l1.shape[1]
    w = cols // n
    block = pl.BlockSpec((rows, w), lambda k, order: (0, order[k]))
    return pl.pallas_call(
        functools.partial(finish_kernel, n, rate),
        out_shape=[
            jax.ShapeDtypeStruct((1, rows, cols), F32),
            jax.ShapeDtypeStruct((rows, cols), F32),
            jax.ShapeDtypeStruct((cols, rank), F32),
        ],
        grid_spec=pltpu.PrefetchScalarGridSpec(
            num_scalar_prefetch=1,
            grid=(n,),
            in_specs=[VMEM] * len(rings)
            + [block, block, whole((rows, rank)), whole((rows, rank)), whole((rank, rows))]
            + [whole((1, rank)), whole((8, rank))],
            out_specs=[
                pl.BlockSpec((1, rows, w), lambda k, order: (0, 0, order[k])),
                block,
                pl.BlockSpec((w, rank), lambda k, order: (order[k], 0)),
            ],
            scratch_shapes=[
                pltpu.VMEM((2, rank + rows, w), F32),
                pltpu.SemaphoreType.DMA((2, 2)),
                pltpu.VMEM((2, rank, rows), BF16),
                pltpu.VMEM((2, 2 * rows, 2 * rank), BF16),
            ],
        ),
        cost_estimate=cost(30 * rows * cols * rank, 32 * rows * cols),
        compiler_params=grant(28),
        name="finish",
    )(order, *rings, both, weights, l1, l2, l2t, norm, totals)


def whole(shape):
    return pl.BlockSpec(shape, lambda k, order: (0,) * len(shape))


def flip(x, axis, bits):
    size = lax.axis_size(axis)
    return lax.ppermute(x, axis, [(i, i ^ bits) for i in range(size)])


def all_sum_stages(box):
    cols, reps = lax.axis_size("col"), lax.axis_size("rep")

    def scatter():
        got = [flip(box["parts"][d], "col", d) for d in range(1, cols)]
        x = box["parts"][0]
        for other in got:
            x = x + other
        box["x"] = x

    def exchange(bit):
        def stage():
            got = flip(box["x"], "rep", 1 << bit)
            box["x"] = box["x"] + got

        return stage

    def gather():
        box["parts"] = [box["x"]] + [flip(box["x"], "col", d) for d in range(1, cols)]

    return [scatter] + [exchange(b) for b in range(reps.bit_length() - 1)] + [gather]


def ring_shards(rate, momentum, grads, weights, right_factor):
    n, count = lax.axis_size("rep"), lax.axis_size("col")
    _, rows, _ = momentum.shape
    rank = right_factor.shape[1]
    ring = list(range(0, n, 2)) + list(range(n - 1, 0, -2))
    rep = lax.axis_index("rep")
    place = jnp.where(rep % 2 == 0, rep // 2, n - 1 - rep // 2).astype(jnp.int32)
    ahead = [(ring[i], ring[(i + 1) % n]) for i in range(n)]
    back = [(b, a) for a, b in ahead]
    me = lax.axis_index("col").astype(jnp.int32)[None]
    order = lax.rem(place - jnp.arange(n, dtype=jnp.int32) + n, n)

    def chunk(x, k):
        return lax.dynamic_index_in_dim(x, lax.rem(place + k + 2 * n, n), 0, keepdims=False)

    def tie(box, *arrays):
        keys = list(box)
        tied = lax.optimization_barrier(([box[k] for k in keys], list(arrays)))
        box.update(zip(keys, tied[0]))
        return tied[1]

    def step(up, dn):
        return lax.ppermute(up, "rep", ahead), lax.ppermute(dn, "rep", back)

    def first(scaled):
        def stage():
            out = orth_first(me, box.pop("parts"), rows, scaled)
            box.pop("x")
            box["left"], box["rest"] = out[:2]
            if scaled:
                box["norm"] = out[2]

        return stage

    box = {}
    scatter, *bits, gather = all_sum_stages(box)

    def begin():
        box["parts"] = list(raw(me, momentum, grads, right_factor, n, count))

    def prepare():
        after = box["parts"][0]
        box["up_all"], box["dn_all"], box["both"] = combine(momentum, grads, after, n)

    def second():
        box["left"], box["leftt"] = orth_second(box.pop("left"), box.pop("rest"))

    work = [[begin, prepare, scatter]] + [[bit] for bit in bits] + [[first(False)], [second]]
    work[len(bits)].append(gather)
    up, dn = lead(lax.rem(jnp.stack([place + n - 1, place + 1]), n), momentum, grads, n)
    for k in range(1, n):
        up, dn = step(up, dn)
        if work:
            for stage in work.pop(0):
                stage()
            up, dn = tie(box, up, dn)
        if k < n - 1:
            up, dn = up + chunk(box["up_all"], -1 - k), dn + chunk(box["dn_all"], 1 + k)
    l1 = box["left"]
    both = box["both"]
    up, dn = reduced(place[None], up, dn, box["up_all"], box["dn_all"], l1, box["leftt"], n)

    box = {}
    mine = (up, dn)
    scatter, *bits, gather = all_sum_stages(box)

    def begin_again():
        box["parts"] = list(partial_raw(me, *mine, rank, count))

    def second_again():
        box["left"], box["leftt"], box["total"] = orth_second(box.pop("left"), box.pop("rest"), *mine)

    def total_columns():
        got = [flip(box["total"], "col", d) for d in range(1, count)]
        box["total"] = alike([box["total"]] + got)

    def total_bits(masks):
        def stage():
            got = [flip(box["total"], "rep", m) for m in masks]
            box["total"] = alike([box["total"]] + got)

        return stage

    work = [[begin_again, scatter, bits[0]]] + [[bit] for bit in bits[1:]]
    work[-1].append(gather)
    work += [[first(True)], [second_again, total_columns], [total_bits([1, 2, 3])]]
    work += [[total_bits([1 << b])] for b in range(2, n.bit_length() - 1)]
    ups, dns = [up], [dn]
    for _ in range(1, n):
        up, dn = step(up, dn)
        if work:
            for stage in work.pop(0):
                stage()
            up, dn = tie(box, up, dn)
        ups.append(up)
        dns.append(dn)
    new_momentum, new_weights, new_right = finish(
        order, ups + dns, both, weights, l1, box["left"], box["leftt"], box["norm"], box["total"], rate
    )
    return new_weights, new_momentum, new_right


def alike(terms):
    while len(terms) > 1:
        terms = [a + b for a, b in zip(terms[::2], terms[1::2])]
    return terms[0]


def plain_orthonormal(left_raw):
    zero = jnp.zeros((1,), jnp.int32)
    left, rest = orth_first(zero, [left_raw], left_raw.shape[0], False)
    return orth_second(left, rest)[0]


def plain_shards(rate, momentum, grads, weights, right_factor):
    n = lax.axis_size("rep")
    moment = momentum[0]
    combined = moment + grads[0, 0].astype(F32)
    averaged, later = lax.psum((combined / n, grads[1, 0].astype(F32) / n), "rep")
    for step in range(STEPS):
        if step > 0:
            combined = moment + grads[step, 0].astype(F32)
            averaged = averaged + later
        left = plain_orthonormal(lax.psum(dot(averaged, right_factor), "col"))
        right_raw = dot(averaged, left, 0, 0)
        correction = DAMPING * dot(left, right_raw, 1, 1)
        moment = combined - correction
        averaged = averaged - correction
        totals = lax.psum(jnp.sum(right_raw * right_raw, axis=0), "col")
        right_factor = right_raw / jnp.sqrt(totals + EPS)
        weights = weights - rate * dot(left, right_factor, 1, 1)
    return weights, moment[None], right_factor


def solution(mesh):
    def body(momentum, grads, weights, right_factor):
        rep, col = mesh.shape["rep"], mesh.shape["col"]
        _, rows, cols = momentum.shape
        rank = right_factor.shape[1]
        rate = RATE * math.sqrt(rows * cols / rank)
        powers = rep & (rep - 1) == 0 and col & (col - 1) == 0 and col > 1
        fits = cols % (2 * LANES * rep * col) == 0 and rows % (8 * col) == 0
        ring = powers and 4 < rep <= 16 and col <= 8 and fits

        def shards(*args):
            return (ring_shards if ring else plain_shards)(rate, *args)

        step = jax.shard_map(
            shards,
            mesh=mesh,
            in_specs=(
                P("rep", None, "col"),
                P(None, "rep", None, "col"),
                P(None, "col"),
                P("col", None),
            ),
            out_specs=(P(None, "col"), P("rep", None, "col"), P("col", None)),
            check_vma=False,
        )
        return step(momentum, grads, weights, right_factor)

    return body
```

```python
import functools
import math

import jax
import jax.numpy as jnp
from jax import lax
from jax.experimental import pallas as pl
from jax.experimental.pallas import tpu as pltpu
from jax.sharding import PartitionSpec as P


STEPS = 2
DAMPING = 0.1
RATE = 0.2
EPS = 1e-06
LANES = 128
GROUP = 8

precise = lax.Precision.HIGHEST
VMEM = pl.BlockSpec(memory_space=pltpu.VMEM)
SMEM = pl.BlockSpec(memory_space=pltpu.SMEM)
F32 = jnp.float32
BF16 = jnp.bfloat16


def dot(a, b, ca=1, cb=0):
    return lax.dot_general(
        a, b, (((ca,), (cb,)), ((), ())), precision=precise, preferred_element_type=F32
    )


def halves(x):
    high = x.astype(BF16)
    return high, (x - high.astype(F32)).astype(BF16)


def dot3(a, b, ca=1, cb=0):
    def one(x, y):
        return lax.dot_general(x, y, (((ca,), (cb,)), ((), ())), preferred_element_type=F32)

    return one(a[0], b[0]) + (one(a[0], b[1]) + one(a[1], b[0]))


def grant(mib):
    return pltpu.CompilerParams(vmem_limit_bytes=mib << 20)


def cost(flops, moved):
    return pl.CostEstimate(flops=int(flops), bytes_accessed=int(moved), transcendentals=0)


def eliminate(rows, group):
    count, n = len(rows), len(rows) * 8
    lane = lax.broadcasted_iota(jnp.int32, (8, n), 1)
    sub = lax.broadcasted_iota(jnp.int32, (8, n), 0)
    rows = list(rows)
    for j in range(0, n, group):
        rb, s = j // 8, j % 8

        def across(x, k):
            return jnp.broadcast_to(x[:, k : k + 1], (8, n))

        def down(x, k):
            return jnp.broadcast_to(x[k : k + 1, :], (8, n))

        column = [{i: across(rows[i], j + k) for i in range(rb, count)} for k in range(group)]
        unit = [[None] * group for _ in range(group)]
        scaled = [[None] * group for _ in range(group)]
        inverse = [None] * group
        for a in range(group):
            for b in range(a + 1):
                v = down(column[b][rb], s + a)
                for e in range(b):
                    v = v - unit[a][e] * scaled[b][e]
                scaled[a][b] = v
                if b < a:
                    unit[a][b] = v * inverse[b]
            inverse[a] = 1.0 / scaled[a][a]
        inside = (lane >= j) & (lane < j + group)
        pivot_rows = []
        for k in range(group):
            r = jnp.where(lane == j + k, 1.0, jnp.where(inside, 0.0, down(rows[rb], s + k)))
            for e in range(k):
                r = r - unit[k][e] * pivot_rows[e]
            pivot_rows.append(r)
        for i in range(rb, count):
            if i == rb and s + group == 8 and s == 0:
                out = rows[i]
                for k in range(group):
                    r = jnp.where(lane == j + k, scaled[k][k], pivot_rows[k])
                    out = jnp.where(sub == k, r, out)
                rows[i] = out
                continue
            left = []
            for k in range(group):
                v = column[k][i]
                for e in range(k):
                    v = v - unit[k][e] * left[e]
                left.append(v)
            y = jnp.where(inside, 0.0, rows[i])
            for k in range(group):
                m = left[k] * inverse[k]
                if i == rb:
                    m = jnp.where(sub > s + k, m, 0.0)
                y = y - m * pivot_rows[k]
            if i == rb:
                out = jnp.where(sub < s, rows[i], y)
                for k in range(group):
                    r = jnp.where(lane == j + k, scaled[k][k], pivot_rows[k])
                    out = jnp.where(sub == s + k, r, out)
                y = out
            rows[i] = y
    return rows


def inverse_factor(matrix):
    n = matrix.shape[0]
    rows = eliminate([matrix[8 * i : 8 * i + 8, :] for i in range(n // 8)], GROUP)
    rows = jnp.concatenate(rows, axis=0)
    lane = lax.broadcasted_iota(jnp.int32, (n, n), 1)
    sub = lax.broadcasted_iota(jnp.int32, (n, n), 0)
    pivots = jnp.sum(jnp.where(lane == sub, rows, 0.0), axis=1, keepdims=True)
    unit = jnp.where(lane < sub, rows, jnp.where(lane == sub, 1.0, 0.0))
    return unit / jnp.sqrt(pivots)


def orthonormal_blocks(blocks):
    out = []
    for block in blocks:
        for q in out:
            block = block - dot(q, dot(q, block, 0, 0))
        out.append(dot(block, inverse_factor(dot(block, block, 0, 0)), 1, 1))
    return out


def column_blocks(x):
    return [x[:, i : i + LANES] for i in range(0, x.shape[1], LANES)]


def first_kernel(scaled, me_ref, *refs):
    count = len(refs) - 3 - scaled
    parts, (left_ref, rest_ref), raw = refs[:count], refs[count : count + 2], refs[-1]
    rows = raw.shape[0] // count
    for d in range(count):
        at = pl.multiple_of((me_ref[0] ^ d) * rows, 8)
        raw[pl.ds(at, rows), :] = parts[d][:rows]
    left_raw = raw[...]
    if scaled:
        norm = jnp.sqrt(parts[0][rows : rows + 1] + EPS)
        refs[count + 2][...] = norm
        left_raw = left_raw / norm
    blocks = column_blocks(left_raw)
    middle = len(blocks) // 2
    done = orthonormal_blocks(blocks[:middle])
    left_ref[...] = jnp.concatenate(done, axis=1)
    rest = blocks[middle:]
    for q in done:
        rest = [block - dot(q, dot(q, block, 0, 0)) for block in rest]
    rest_ref[...] = jnp.concatenate(rest, axis=1)


def second_kernel(left_ref, rest_ref, out_ref, outt_ref):
    done = orthonormal_blocks(column_blocks(rest_ref[...]))
    left = jnp.concatenate([left_ref[...]] + done, axis=1)
    out_ref[...] = left
    outt_ref[...] = left.T


def orth_first(me, parts, rows, scaled):
    rank = parts[0].shape[1]
    part = jax.ShapeDtypeStruct((rows, rank // 2), F32)
    shapes = [part, part] + [jax.ShapeDtypeStruct((1, rank), F32)] * scaled
    return pl.pallas_call(
        functools.partial(first_kernel, scaled),
        out_shape=shapes,
        in_specs=[SMEM] + [VMEM] * len(parts),
        out_specs=[VMEM] * len(shapes),
        scratch_shapes=[pltpu.VMEM((rows, rank), F32)],
        cost_estimate=cost(6e9, 1e6),
        compiler_params=grant(12),
        name="orth_first",
    )(me, *parts)


def orth_second(left, rest):
    rows, rank = left.shape[0], left.shape[1] + rest.shape[1]
    return pl.pallas_call(
        second_kernel,
        out_shape=[
            jax.ShapeDtypeStruct((rows, rank), F32),
            jax.ShapeDtypeStruct((rank, rows), F32),
        ],
        in_specs=[VMEM] * 2,
        out_specs=[VMEM] * 2,
        cost_estimate=cost(6e9, 1e6),
        compiler_params=grant(12),
        name="orth_second",
    )(left, rest)


def chunk_rows(mom, grads):
    return jnp.concatenate([mom[0] + grads[0, 0].astype(F32), grads[1, 0].astype(F32)], axis=0)


def lead_kernel(at_ref, mom_up, grads_up, mom_dn, grads_dn, up_ref, dn_ref):
    up_ref[...] = chunk_rows(mom_up[...], grads_up[...])
    dn_ref[...] = chunk_rows(mom_dn[...], grads_dn[...])


def lead(place, momentum, grads, n):
    _, rows, cols = momentum.shape
    w = cols // n // 2
    part = jax.ShapeDtypeStruct((2 * rows, w), F32)
    specs = []
    for side, offset in enumerate((n - 1, 1)):

        def half(i, at, side=side, offset=offset):
            return 2 * lax.rem(at[0] + offset, n) + side

        specs.append(pl.BlockSpec((1, rows, w), lambda i, at, half=half: (0, 0, half(i, at))))
        specs.append(pl.BlockSpec((2, 1, rows, w), lambda i, at, half=half: (0, 0, 0, half(i, at))))
    return pl.pallas_call(
        lead_kernel,
        out_shape=[part, part],
        grid_spec=pltpu.PrefetchScalarGridSpec(
            num_scalar_prefetch=1,
            grid=(1,),
            in_specs=specs,
            out_specs=[whole((2 * rows, w))] * 2,
        ),
        cost_estimate=cost(4 * rows * w, 32 * rows * w),
        compiler_params=grant(58),
        name="lead",
    )(place, momentum, grads, momentum, grads)


def combine_kernel(count, inv, me_ref, mom_ref, grads_ref, right_ref, up_ref, dn_ref, both_ref, *refs):
    parts, acc_ref = refs[:count], refs[count]
    k = pl.program_id(0)
    rows = mom_ref.shape[1]
    chunks, _, w = up_ref.shape
    total = mom_ref[0] + grads_ref[0, 0].astype(F32)
    later = grads_ref[1, 0].astype(F32)
    both_ref[0] = total + later
    for c in range(chunks):
        for side, ref in enumerate((up_ref, dn_ref)):
            at = (2 * c + side) * w
            ref[c, :rows] = total[:, at : at + w]
            ref[c, rows:] = later[:, at : at + w]
    part = dot(total, right_ref[...])

    @pl.when(k == 0)
    def _():
        acc_ref[...] = part

    @pl.when(k > 0)
    def _():
        acc_ref[...] += part

    @pl.when(k == pl.num_programs(0) - 1)
    def _():
        acc_ref[...] *= inv
        block = rows // count
        for d in range(count):
            at = pl.multiple_of((me_ref[0] ^ d) * block, 8)
            parts[d][...] = acc_ref[pl.ds(at, block), :]


def combine(me, momentum, grads, right_factor, n, count):
    _, rows, cols = momentum.shape
    rank = right_factor.shape[1]
    steps = n // 2
    w = cols // steps
    chunks = jax.ShapeDtypeStruct((n, 2 * rows, w // 4), F32)
    part = jax.ShapeDtypeStruct((rows // count, rank), F32)
    out = pl.pallas_call(
        functools.partial(combine_kernel, count, 1.0 / n),
        out_shape=[chunks, chunks, jax.ShapeDtypeStruct((1, rows, cols), F32)] + [part] * count,
        grid=(steps,),
        in_specs=[
            SMEM,
            pl.BlockSpec((1, rows, w), lambda k: (0, 0, k)),
            pl.BlockSpec((2, 1, rows, w), lambda k: (0, 0, 0, k)),
            pl.BlockSpec((w, rank), lambda k: (k, 0)),
        ],
        out_specs=[
            pl.BlockSpec((2, 2 * rows, w // 4), lambda k: (k, 0, 0)),
            pl.BlockSpec((2, 2 * rows, w // 4), lambda k: (k, 0, 0)),
            pl.BlockSpec((1, rows, w), lambda k: (0, 0, k)),
        ]
        + [pl.BlockSpec((rows // count, rank), lambda k: (0, 0))] * count,
        scratch_shapes=[pltpu.VMEM((rows, rank), F32)],
        cost_estimate=cost(12 * rows * cols * rank, 28 * rows * cols),
        compiler_params=grant(20),
        name="combine",
    )(me, momentum, grads, right_factor)
    return out[0], out[1], out[2], out[3:]


def ring_add_kernel(at_ref, up_ref, dn_ref, up_all, dn_all, up_out, dn_out):
    up_out[...] = up_ref[...] + up_all[0]
    dn_out[...] = dn_ref[...] + dn_all[0]


def ring_add(place, step, up, dn, up_all, dn_all):
    n = up_all.shape[0]
    shape = jax.ShapeDtypeStruct(up.shape, F32)
    return pl.pallas_call(
        ring_add_kernel,
        out_shape=[shape, shape],
        grid_spec=pltpu.PrefetchScalarGridSpec(
            num_scalar_prefetch=1,
            grid=(1,),
            in_specs=[
                whole(up.shape),
                whole(dn.shape),
                pl.BlockSpec((1,) + up.shape, lambda i, at: (lax.rem(at[0] + n - 1 - step, n), 0, 0)),
                pl.BlockSpec((1,) + dn.shape, lambda i, at: (lax.rem(at[0] + 1 + step, n), 0, 0)),
            ],
            out_specs=[whole(up.shape), whole(dn.shape)],
        ),
        cost_estimate=cost(2 * up.size, 24 * up.size),
        compiler_params=grant(8),
        name="ring_add",
    )(place, up, dn, up_all, dn_all)


def alike_kernel(*refs):
    terms = [ref[...] for ref in refs[:-1]]
    while len(terms) > 1:
        terms = [a + b for a, b in zip(terms[::2], terms[1::2])]
    refs[-1][...] = terms[0]


def alike(terms):
    return pl.pallas_call(
        alike_kernel,
        out_shape=jax.ShapeDtypeStruct(terms[0].shape, F32),
        in_specs=[VMEM] * len(terms),
        out_specs=VMEM,
        cost_estimate=cost(len(terms) * terms[0].size, 4 * (len(terms) + 1) * terms[0].size),
        compiler_params=grant(4),
        name="alike",
    )(*terms)


def reduced_kernel(inv, at_ref, up_ref, dn_ref, up_all, dn_all, left_ref, leftt_ref, up_out, dn_out):
    rows, rank = left_ref.shape
    w = up_ref.shape[1]
    up, dn = up_ref[...] + up_all[0], dn_ref[...] + dn_all[0]
    mean = jnp.concatenate([up, dn], axis=1) * inv
    averaged, later = mean[:rows], mean[rows:]
    right = dot(leftt_ref[...], averaged)
    averaged = averaged - DAMPING * dot(left_ref[...], right) + later
    up_out[:rank] = right[:, :w]
    dn_out[:rank] = right[:, w:]
    up_out[rank:] = averaged[:, :w]
    dn_out[rank:] = averaged[:, w:]


def reduced(place, up, dn, up_all, dn_all, left, leftt, n):
    rows, rank = left.shape
    w = up.shape[1]
    ring = jax.ShapeDtypeStruct((rank + rows, w), F32)
    mine = pl.BlockSpec((1, 2 * rows, w), lambda i, at: (at[0], 0, 0))
    return pl.pallas_call(
        functools.partial(reduced_kernel, 1.0 / n),
        out_shape=[ring, ring],
        grid_spec=pltpu.PrefetchScalarGridSpec(
            num_scalar_prefetch=1,
            grid=(1,),
            in_specs=[whole(up.shape), whole(dn.shape), mine, mine, whole((rows, rank)), whole((rank, rows))],
            out_specs=[whole(ring.shape)] * 2,
        ),
        cost_estimate=cost(24 * rows * rank * rank, 4e6),
        compiler_params=grant(12),
        name="reduced",
    )(place, up, dn, up_all, dn_all, left, leftt)


def partial_kernel(rank, me_ref, up_ref, dn_ref, *refs):
    parts, scratch = refs[:-1], refs[-1]
    rows = up_ref.shape[0] - rank
    both = jnp.concatenate([up_ref[...], dn_ref[...]], axis=1)
    right, averaged = both[:rank], both[rank:]
    scratch[...] = dot(averaged, right, 1, 1)
    squares = dot(jnp.ones((8, both.shape[1]), F32), right * right, 1, 1)
    block = rows // len(parts)
    for d, ref in enumerate(parts):
        at = pl.multiple_of((me_ref[0] ^ d) * block, 8)
        ref[:block] = scratch[pl.ds(at, block), :]
        ref[block:] = squares


def partial_raw(me, up, dn, rank, count):
    rows = up.shape[0] - rank
    part = jax.ShapeDtypeStruct((rows // count + 8, rank), F32)
    return pl.pallas_call(
        functools.partial(partial_kernel, rank),
        out_shape=[part] * count,
        in_specs=[SMEM] + [VMEM] * 2,
        out_specs=[VMEM] * count,
        scratch_shapes=[pltpu.VMEM((rows, rank), F32)],
        cost_estimate=cost(12 * rows * rank * rank, 2e6),
        compiler_params=grant(8),
        name="partial",
    )(me, up, dn)


def fetcher(pieces, buf, sem):
    k = pl.program_id(0)

    def copies(i, slot):
        out = []
        for j, (ref, row, col) in enumerate(pieces[i]):
            at = buf.at[slot, pl.ds(row, ref.shape[0]), pl.ds(col, ref.shape[1])]
            out.append(pltpu.make_async_copy(ref, at, sem.at[slot, j]))
        return out

    @pl.when(k == 0)
    def _():
        for c in copies(0, 0):
            c.start()

    for i in range(1, len(pieces)):

        @pl.when(k == i - 1)
        def _():
            for c in copies(i, i % 2):
                c.start()

    slot = lax.rem(k, 2)
    for c in copies(0, slot):
        c.wait()
    return buf[slot]


def advance_kernel(m, order_ref, *refs):
    ups, dns = refs[:m], refs[m : 2 * m]
    both_ref, l1_ref, l2_ref, l2t_ref, mom_out, y_out, sq_out, buf, sem, project, update = refs[2 * m :]
    k = pl.program_id(0)
    rank = l2t_ref.shape[0]
    w = buf.shape[2] // 2

    @pl.when(k == 0)
    def _():
        project[0], project[1] = halves(l2t_ref[...])
        update[0], update[1] = halves(DAMPING * jnp.concatenate([l1_ref[...], l2_ref[...]], axis=1))

    chunk = fetcher([[(ups[i], 0, 0), (dns[i], 0, w)] for i in range(m)], buf, sem)
    y1, averaged = chunk[:rank], chunk[rank:]
    y2 = dot3((project[0], project[1]), halves(averaged))
    y_out[0] = y2
    y = halves(jnp.concatenate([y1, y2], axis=0))
    mom_out[0] = both_ref[0] - dot3((update[0], update[1]), y)
    squares = dot(jnp.ones((8, 2 * w), F32), y2 * y2, 1, 1)

    @pl.when(k == 0)
    def _():
        sq_out[...] = squares

    @pl.when(k > 0)
    def _():
        sq_out[...] += squares


def chunk_at(steps, n):
    def at(k, place):
        step = steps[0]
        for i in range(1, len(steps)):
            step = jnp.where(k == i, steps[i], step)
        return lax.rem(place[0] + n - step, n)

    return at


def advance(place, steps, n, ups, dns, both, l1, l2, l2t):
    m = len(ups)
    _, rows, _ = both.shape
    rank = l1.shape[1]
    w = 2 * ups[0].shape[1]
    at = chunk_at(steps, n)
    block = pl.BlockSpec((1, rows, w), lambda k, place: (0, 0, at(k, place)))
    return pl.pallas_call(
        functools.partial(advance_kernel, m),
        out_shape=[
            jax.ShapeDtypeStruct(both.shape, F32),
            jax.ShapeDtypeStruct((m, rank, w), F32),
            jax.ShapeDtypeStruct((8, rank), F32),
        ],
        grid_spec=pltpu.PrefetchScalarGridSpec(
            num_scalar_prefetch=1,
            grid=(m,),
            in_specs=[VMEM] * (2 * m) + [block, whole((rows, rank)), whole((rows, rank)), whole((rank, rows))],
            out_specs=[block, pl.BlockSpec((1, rank, w), lambda k, order: (k, 0, 0)), whole((8, rank))],
            scratch_shapes=[
                pltpu.VMEM((2, rank + rows, w), F32),
                pltpu.SemaphoreType.DMA((2, 2)),
                pltpu.VMEM((2, rank, rows), BF16),
                pltpu.VMEM((2, rows, 2 * rank), BF16),
            ],
        ),
        input_output_aliases={1 + 2 * m: 0},
        cost_estimate=cost(m * w * 30 * rows * rank, m * w * rows * 24),
        compiler_params=grant(14),
        name="advance",
    )(place, *ups, *dns, both, l1, l2, l2t)


def weights_kernel(n, groups, rate, order_ref, *refs):
    ups, dns, ys = refs[:n], refs[n : 2 * n], refs[2 * n : 2 * n + len(groups)]
    w_ref, l1_ref, l2_ref, norm_ref, *totals, w_out, right_out, buf, sem, update = refs[2 * n + len(groups) :]
    rank = right_out.shape[1]
    w = buf.shape[2] // 2
    total = totals[0][0:1]
    for ref in totals[1:]:
        total = total + ref[0:1]
    norm = jnp.sqrt(total + EPS)

    @pl.when(pl.program_id(0) == 0)
    def _():
        left = jnp.concatenate([l1_ref[...] / norm_ref[...], l2_ref[...] / norm], axis=1)
        update[0], update[1] = halves(rate * left)

    pieces = []
    for y_ref, group in zip(ys, groups):
        for j in range(group):
            i = len(pieces)
            rows = pl.ds(0, rank)
            pieces.append([(ups[i].at[rows, :], 0, 0), (dns[i].at[rows, :], 0, w), (y_ref.at[j], rank, 0)])
    y = fetcher(pieces, buf, sem)
    w_out[...] = w_ref[...] - dot3((update[0], update[1]), halves(y))
    right_out[...] = y[rank:].T / norm


def finish(place, steps, ups, dns, ys, weights, l1, l2, norm, totals, rate):
    n = len(ups)
    rows, cols = weights.shape
    rank = l1.shape[1]
    w = cols // n
    groups = tuple(y.shape[0] for y in ys)
    at = chunk_at(steps, n)
    block = pl.BlockSpec((rows, w), lambda k, place: (0, at(k, place)))
    return pl.pallas_call(
        functools.partial(weights_kernel, n, groups, rate),
        out_shape=[
            jax.ShapeDtypeStruct((rows, cols), F32),
            jax.ShapeDtypeStruct((cols, rank), F32),
        ],
        grid_spec=pltpu.PrefetchScalarGridSpec(
            num_scalar_prefetch=1,
            grid=(n,),
            in_specs=[VMEM] * (2 * n + len(ys))
            + [block, whole((rows, rank)), whole((rows, rank)), whole((1, rank))]
            + [whole((8, rank))] * len(totals),
            out_specs=[block, pl.BlockSpec((w, rank), lambda k, place: (at(k, place), 0))],
            scratch_shapes=[
                pltpu.VMEM((2, 2 * rank, w), F32),
                pltpu.SemaphoreType.DMA((2, 3)),
                pltpu.VMEM((2, rows, 2 * rank), BF16),
            ],
        ),
        cost_estimate=cost(12 * rows * cols * rank, 32 * rows * cols),
        compiler_params=grant(28),
        name="finish",
    )(place, *ups, *dns, *ys, weights, l1, l2, norm, *totals)


def whole(shape):
    return pl.BlockSpec(shape, lambda k, order: (0,) * len(shape))


def flip(x, axis, bits):
    size = lax.axis_size(axis)
    return lax.ppermute(x, axis, [(i, i ^ bits) for i in range(size)])


def all_sum_stages(box):
    cols, reps = lax.axis_size("col"), lax.axis_size("rep")

    def scatter():
        got = [flip(box["parts"][d], "col", d) for d in range(1, cols)]
        box["x"] = alike([box["parts"][0]] + got)

    def exchange(bit):
        def stage():
            got = flip(box["x"], "rep", 1 << bit)
            box["x"] = alike([box["x"], got])

        return stage

    def gather():
        box["parts"] = [box["x"]] + [flip(box["x"], "col", d) for d in range(1, cols)]

    return [scatter] + [exchange(b) for b in range(reps.bit_length() - 1)] + [gather]


def ring_shards(rate, momentum, grads, weights, right_factor):
    n, count = lax.axis_size("rep"), lax.axis_size("col")
    _, rows, _ = momentum.shape
    rank = right_factor.shape[1]
    ring = list(range(0, n, 2)) + list(range(n - 1, 0, -2))
    rep = lax.axis_index("rep")
    place = jnp.where(rep % 2 == 0, rep // 2, n - 1 - rep // 2).astype(jnp.int32)[None]
    ahead = [(ring[i], ring[(i + 1) % n]) for i in range(n)]
    back = [(b, a) for a, b in ahead]
    me = lax.axis_index("col").astype(jnp.int32)[None]

    def tie(box, *arrays):
        keys = list(box)
        tied = lax.optimization_barrier(([box[k] for k in keys], list(arrays)))
        box.update(zip(keys, tied[0]))
        return tied[1]

    def step(up, dn):
        return lax.ppermute(up, "rep", ahead), lax.ppermute(dn, "rep", back)

    def first(scaled):
        def stage():
            out = orth_first(me, box.pop("parts"), rows, scaled)
            box.pop("x")
            box["left"], box["rest"] = out[:2]
            if scaled:
                box["norm"] = out[2]

        return stage

    box = {}
    scatter, *bits, gather = all_sum_stages(box)

    def begin():
        out = combine(me, momentum, grads, right_factor, n, count)
        box["up_all"], box["dn_all"], box["both"] = out[:3]
        box["parts"] = list(out[3])

    def second():
        box["left"], box["leftt"] = orth_second(box.pop("left"), box.pop("rest"))

    work = [[begin, scatter]] + [[bit] for bit in bits] + [[first(False)], [second]]
    work[len(bits)].append(gather)
    up, dn = lead(place, momentum, grads, n)
    for k in range(1, n):
        up, dn = step(up, dn)
        if work:
            for stage in work.pop(0):
                stage()
            up, dn = tie(box, up, dn)
        if k < n - 1:
            up, dn = ring_add(place, k, up, dn, box["up_all"], box["dn_all"])
    l1 = box["left"]
    both = box["both"]
    up, dn = reduced(place, up, dn, box["up_all"], box["dn_all"], l1, box["leftt"], n)

    box = {}
    mine = (up, dn)
    scatter, *bits, gather = all_sum_stages(box)

    def begin_again():
        box["parts"] = list(partial_raw(me, *mine, rank, count))

    ups, dns = [up], [dn]
    ready, ys, totals = [], [], []

    def advance_ready():
        new = [c for c in range(n) if c not in ready and c < len(ups) and (n - c) % n < len(dns)]
        ready.extend(new)
        sides = ([ups[c] for c in new], [dns[(n - c) % n] for c in new])
        box["both"], y, squares = advance(place, new, n, *sides, box["both"], l1, box["left"], box["leftt"])
        ys.append(y)
        totals.append(squares)

    work = [[begin_again, scatter, bits[0]]] + [[bit] for bit in bits[1:]]
    work[-1].append(gather)
    work += [[first(True)], [second]]
    for _ in range(1, n):
        up, dn = step(up, dn)
        if work:
            for stage in work.pop(0):
                stage()
            up, dn = tie(box, up, dn)
        else:
            box.setdefault("both", both)
            advance_ready()
            up, dn = tie(box, up, dn)
        ups.append(up)
        dns.append(dn)
    box.setdefault("both", both)
    advance_ready()
    total = alike_total(totals, count)
    sides = ([ups[c] for c in ready], [dns[(n - c) % n] for c in ready])
    new_weights, new_right = finish(place, ready, *sides, ys, weights, l1, box["left"], box["norm"], [total], rate)
    return new_weights, box["both"], new_right


def alike_total(totals, count):
    total = totals[0]
    for other in totals[1:]:
        total = alike([total, other])
    got = [flip(total, "col", d) for d in range(1, count)]
    return alike([total] + got)


def plain_orthonormal(left_raw):
    zero = jnp.zeros((1,), jnp.int32)
    left, rest = orth_first(zero, [left_raw], left_raw.shape[0], False)
    return orth_second(left, rest)[0]


def plain_shards(rate, momentum, grads, weights, right_factor):
    n = lax.axis_size("rep")
    moment = momentum[0]
    combined = moment + grads[0, 0].astype(F32)
    averaged, later = lax.psum((combined / n, grads[1, 0].astype(F32) / n), "rep")
    for step in range(STEPS):
        if step > 0:
            combined = moment + grads[step, 0].astype(F32)
            averaged = averaged + later
        left = plain_orthonormal(lax.psum(dot(averaged, right_factor), "col"))
        right_raw = dot(averaged, left, 0, 0)
        correction = DAMPING * dot(left, right_raw, 1, 1)
        moment = combined - correction
        averaged = averaged - correction
        totals = lax.psum(jnp.sum(right_raw * right_raw, axis=0), "col")
        right_factor = right_raw / jnp.sqrt(totals + EPS)
        weights = weights - rate * dot(left, right_factor, 1, 1)
    return weights, moment[None], right_factor


def solution(mesh):
    def body(momentum, grads, weights, right_factor):
        rep, col = mesh.shape["rep"], mesh.shape["col"]
        _, rows, cols = momentum.shape
        rank = right_factor.shape[1]
        rate = RATE * math.sqrt(rows * cols / rank)
        powers = rep & (rep - 1) == 0 and col & (col - 1) == 0 and col > 1
        fits = cols % (2 * LANES * rep * col) == 0 and rows % (8 * col) == 0
        ring = powers and 4 < rep <= 16 and col <= 8 and fits

        def shards(*args):
            return (ring_shards if ring else plain_shards)(rate, *args)

        step = jax.shard_map(
            shards,
            mesh=mesh,
            in_specs=(
                P("rep", None, "col"),
                P(None, "rep", None, "col"),
                P(None, "col"),
                P("col", None),
            ),
            out_specs=(P(None, "col"), P("rep", None, "col"), P("col", None)),
            check_vma=False,
        )
        return step(momentum, grads, weights, right_factor)

    return body
```

```python
import functools
import math

import jax
import jax.numpy as jnp
from jax import lax
from jax.experimental import pallas as pl
from jax.experimental.pallas import tpu as pltpu
from jax.sharding import PartitionSpec as P


STEPS = 2
DAMPING = 0.1
RATE = 0.2
EPS = 1e-06
LANES = 128
GROUP = 8

precise = lax.Precision.HIGHEST
VMEM = pl.BlockSpec(memory_space=pltpu.VMEM)
SMEM = pl.BlockSpec(memory_space=pltpu.SMEM)
F32 = jnp.float32
BF16 = jnp.bfloat16


def dot(a, b, ca=1, cb=0):
    return lax.dot_general(
        a, b, (((ca,), (cb,)), ((), ())), precision=precise, preferred_element_type=F32
    )


def halves(x):
    high = x.astype(BF16)
    return high, (x - high.astype(F32)).astype(BF16)


def dot3(a, b, ca=1, cb=0):
    def one(x, y):
        return lax.dot_general(x, y, (((ca,), (cb,)), ((), ())), preferred_element_type=F32)

    return one(a[0], b[0]) + (one(a[0], b[1]) + one(a[1], b[0]))


def grant(mib):
    return pltpu.CompilerParams(vmem_limit_bytes=mib << 20)


def cost(flops, moved):
    return pl.CostEstimate(flops=int(flops), bytes_accessed=int(moved), transcendentals=0)


def eliminate(rows, group):
    count, n = len(rows), len(rows) * 8
    lane = lax.broadcasted_iota(jnp.int32, (8, n), 1)
    sub = lax.broadcasted_iota(jnp.int32, (8, n), 0)
    rows = list(rows)
    for j in range(0, n, group):
        rb, s = j // 8, j % 8

        def across(x, k):
            return jnp.broadcast_to(x[:, k : k + 1], (8, n))

        def down(x, k):
            return jnp.broadcast_to(x[k : k + 1, :], (8, n))

        column = [{i: across(rows[i], j + k) for i in range(rb, count)} for k in range(group)]
        unit = [[None] * group for _ in range(group)]
        scaled = [[None] * group for _ in range(group)]
        inverse = [None] * group
        for a in range(group):
            for b in range(a + 1):
                v = down(column[b][rb], s + a)
                for e in range(b):
                    v = v - unit[a][e] * scaled[b][e]
                scaled[a][b] = v
                if b < a:
                    unit[a][b] = v * inverse[b]
            inverse[a] = 1.0 / scaled[a][a]
        inside = (lane >= j) & (lane < j + group)
        pivot_rows = []
        for k in range(group):
            r = jnp.where(lane == j + k, 1.0, jnp.where(inside, 0.0, down(rows[rb], s + k)))
            for e in range(k):
                r = r - unit[k][e] * pivot_rows[e]
            pivot_rows.append(r)
        for i in range(rb, count):
            if i == rb and s + group == 8 and s == 0:
                out = rows[i]
                for k in range(group):
                    r = jnp.where(lane == j + k, scaled[k][k], pivot_rows[k])
                    out = jnp.where(sub == k, r, out)
                rows[i] = out
                continue
            left = []
            for k in range(group):
                v = column[k][i]
                for e in range(k):
                    v = v - unit[k][e] * left[e]
                left.append(v)
            y = jnp.where(inside, 0.0, rows[i])
            for k in range(group):
                m = left[k] * inverse[k]
                if i == rb:
                    m = jnp.where(sub > s + k, m, 0.0)
                y = y - m * pivot_rows[k]
            if i == rb:
                out = jnp.where(sub < s, rows[i], y)
                for k in range(group):
                    r = jnp.where(lane == j + k, scaled[k][k], pivot_rows[k])
                    out = jnp.where(sub == s + k, r, out)
                y = out
            rows[i] = y
    return rows


def inverse_factor(matrix):
    n = matrix.shape[0]
    rows = eliminate([matrix[8 * i : 8 * i + 8, :] for i in range(n // 8)], GROUP)
    rows = jnp.concatenate(rows, axis=0)
    lane = lax.broadcasted_iota(jnp.int32, (n, n), 1)
    sub = lax.broadcasted_iota(jnp.int32, (n, n), 0)
    pivots = jnp.sum(jnp.where(lane == sub, rows, 0.0), axis=1, keepdims=True)
    unit = jnp.where(lane < sub, rows, jnp.where(lane == sub, 1.0, 0.0))
    return unit / jnp.sqrt(pivots)


def orthonormal_blocks(blocks):
    out = []
    for block in blocks:
        for q in out:
            block = block - dot(q, dot(q, block, 0, 0))
        out.append(dot(block, inverse_factor(dot(block, block, 0, 0)), 1, 1))
    return out


def column_blocks(x):
    return [x[:, i : i + LANES] for i in range(0, x.shape[1], LANES)]


def first_kernel(scaled, me_ref, *refs):
    count = len(refs) - 3 - scaled
    parts, (left_ref, rest_ref), raw = refs[:count], refs[count : count + 2], refs[-1]
    rows = raw.shape[0] // count
    for d in range(count):
        at = pl.multiple_of((me_ref[0] ^ d) * rows, 8)
        raw[pl.ds(at, rows), :] = parts[d][:rows]
    left_raw = raw[...]
    if scaled:
        norm = jnp.sqrt(parts[0][rows : rows + 1] + EPS)
        refs[count + 2][...] = norm
        left_raw = left_raw / norm
    blocks = column_blocks(left_raw)
    middle = len(blocks) // 2
    done = orthonormal_blocks(blocks[:middle])
    left_ref[...] = jnp.concatenate(done, axis=1)
    rest = blocks[middle:]
    for q in done:
        rest = [block - dot(q, dot(q, block, 0, 0)) for block in rest]
    rest_ref[...] = jnp.concatenate(rest, axis=1)


def second_kernel(left_ref, rest_ref, out_ref, outt_ref):
    done = orthonormal_blocks(column_blocks(rest_ref[...]))
    left = jnp.concatenate([left_ref[...]] + done, axis=1)
    out_ref[...] = left
    outt_ref[...] = left.T


def orth_first(me, parts, rows, scaled):
    rank = parts[0].shape[1]
    part = jax.ShapeDtypeStruct((rows, rank // 2), F32)
    shapes = [part, part] + [jax.ShapeDtypeStruct((1, rank), F32)] * scaled
    return pl.pallas_call(
        functools.partial(first_kernel, scaled),
        out_shape=shapes,
        in_specs=[SMEM] + [VMEM] * len(parts),
        out_specs=[VMEM] * len(shapes),
        scratch_shapes=[pltpu.VMEM((rows, rank), F32)],
        cost_estimate=cost(6e9, 1e6),
        compiler_params=grant(12),
        name="orth_first",
    )(me, *parts)


def orth_second(left, rest):
    rows, rank = left.shape[0], left.shape[1] + rest.shape[1]
    return pl.pallas_call(
        second_kernel,
        out_shape=[
            jax.ShapeDtypeStruct((rows, rank), F32),
            jax.ShapeDtypeStruct((rank, rows), F32),
        ],
        in_specs=[VMEM] * 2,
        out_specs=[VMEM] * 2,
        cost_estimate=cost(6e9, 1e6),
        compiler_params=grant(12),
        name="orth_second",
    )(left, rest)


def chunk_rows(mom, grads):
    return jnp.concatenate([mom[0] + grads[0, 0].astype(F32), grads[1, 0].astype(F32)], axis=0)


def lead_kernel(n, place_ref, mom, grads, up_ref, dn_ref, mom_buf, grads_buf, sem):
    w = up_ref.shape[1]
    copies = []
    for side, offset in enumerate((n - 1, 1)):
        chunk = lax.rem(place_ref[0] + offset, n)
        at = pl.ds(pl.multiple_of((2 * chunk + side) * w, w), w)
        copies.append(
            (
                pltpu.make_async_copy(mom.at[:, :, at], mom_buf.at[side], sem.at[side, 0]),
                pltpu.make_async_copy(grads.at[:, :, :, at], grads_buf.at[side], sem.at[side, 1]),
            )
        )
    for pair in copies:
        for copy in pair:
            copy.start()
    for side, ref in enumerate((up_ref, dn_ref)):
        for copy in copies[side]:
            copy.wait()
        ref[...] = chunk_rows(mom_buf[side], grads_buf[side])


def lead(place, momentum, grads, n):
    _, rows, cols = momentum.shape
    w = cols // n // 2
    part = jax.ShapeDtypeStruct((2 * rows, w), F32)
    return pl.pallas_call(
        functools.partial(lead_kernel, n),
        out_shape=[part, part],
        in_specs=[SMEM, pl.BlockSpec(memory_space=pltpu.HBM), pl.BlockSpec(memory_space=pltpu.HBM)],
        out_specs=[VMEM] * 2,
        scratch_shapes=[
            pltpu.VMEM((2, 1, rows, w), F32),
            pltpu.VMEM((2, 2, 1, rows, w), BF16),
            pltpu.SemaphoreType.DMA((2, 2)),
        ],
        cost_estimate=cost(4 * rows * w, 32 * rows * w),
        compiler_params=grant(58),
        name="lead",
    )(place, momentum, grads)


def combine_kernel(count, inv, me_ref, mom_ref, grads_ref, right_ref, up_ref, dn_ref, both_ref, *refs):
    parts, acc_ref = refs[:count], refs[count]
    k = pl.program_id(0)
    rows = mom_ref.shape[1]
    chunks, _, w = up_ref.shape
    total = mom_ref[0] + grads_ref[0, 0].astype(F32)
    later = grads_ref[1, 0].astype(F32)
    both_ref[0] = total + later
    for c in range(chunks):
        for side, ref in enumerate((up_ref, dn_ref)):
            at = (2 * c + side) * w
            ref[c, :rows] = total[:, at : at + w]
            ref[c, rows:] = later[:, at : at + w]
    part = dot(total, right_ref[...])

    @pl.when(k == 0)
    def _():
        acc_ref[...] = part

    @pl.when(k > 0)
    def _():
        acc_ref[...] += part

    @pl.when(k == pl.num_programs(0) - 1)
    def _():
        acc_ref[...] *= inv
        block = rows // count
        for d in range(count):
            at = pl.multiple_of((me_ref[0] ^ d) * block, 8)
            parts[d][...] = acc_ref[pl.ds(at, block), :]


def combine(me, momentum, grads, right_factor, n, count):
    _, rows, cols = momentum.shape
    rank = right_factor.shape[1]
    steps = n // 2
    w = cols // steps
    chunks = jax.ShapeDtypeStruct((n, 2 * rows, w // 4), F32)
    part = jax.ShapeDtypeStruct((rows // count, rank), F32)
    out = pl.pallas_call(
        functools.partial(combine_kernel, count, 1.0 / n),
        out_shape=[chunks, chunks, jax.ShapeDtypeStruct((1, rows, cols), F32)] + [part] * count,
        grid=(steps,),
        in_specs=[
            SMEM,
            pl.BlockSpec((1, rows, w), lambda k: (0, 0, k)),
            pl.BlockSpec((2, 1, rows, w), lambda k: (0, 0, 0, k)),
            pl.BlockSpec((w, rank), lambda k: (k, 0)),
        ],
        out_specs=[
            pl.BlockSpec((2, 2 * rows, w // 4), lambda k: (k, 0, 0)),
            pl.BlockSpec((2, 2 * rows, w // 4), lambda k: (k, 0, 0)),
            pl.BlockSpec((1, rows, w), lambda k: (0, 0, k)),
        ]
        + [pl.BlockSpec((rows // count, rank), lambda k: (0, 0))] * count,
        scratch_shapes=[pltpu.VMEM((rows, rank), F32)],
        cost_estimate=cost(12 * rows * cols * rank, 28 * rows * cols),
        compiler_params=grant(20),
        name="combine",
    )(me, momentum, grads, right_factor)
    return out[0], out[1], out[2], out[3:]


def ring_add_kernel(at_ref, up_ref, dn_ref, up_all, dn_all, up_out, dn_out):
    up_out[...] = up_ref[...] + up_all[0]
    dn_out[...] = dn_ref[...] + dn_all[0]


def ring_add(place, step, up, dn, up_all, dn_all):
    n = up_all.shape[0]
    shape = jax.ShapeDtypeStruct(up.shape, F32)
    return pl.pallas_call(
        ring_add_kernel,
        out_shape=[shape, shape],
        grid_spec=pltpu.PrefetchScalarGridSpec(
            num_scalar_prefetch=1,
            grid=(1,),
            in_specs=[
                whole(up.shape),
                whole(dn.shape),
                pl.BlockSpec((1,) + up.shape, lambda i, at: (lax.rem(at[0] + n - 1 - step, n), 0, 0)),
                pl.BlockSpec((1,) + dn.shape, lambda i, at: (lax.rem(at[0] + 1 + step, n), 0, 0)),
            ],
            out_specs=[whole(up.shape), whole(dn.shape)],
        ),
        cost_estimate=cost(2 * up.size, 24 * up.size),
        compiler_params=grant(8),
        name="ring_add",
    )(place, up, dn, up_all, dn_all)


def alike_kernel(*refs):
    terms = [ref[...] for ref in refs[:-1]]
    while len(terms) > 1:
        terms = [a + b for a, b in zip(terms[::2], terms[1::2])]
    refs[-1][...] = terms[0]


def alike(terms):
    return pl.pallas_call(
        alike_kernel,
        out_shape=jax.ShapeDtypeStruct(terms[0].shape, F32),
        in_specs=[VMEM] * len(terms),
        out_specs=VMEM,
        cost_estimate=cost(len(terms) * terms[0].size, 4 * (len(terms) + 1) * terms[0].size),
        compiler_params=grant(4),
        name="alike",
    )(*terms)


def reduced_kernel(inv, at_ref, up_ref, dn_ref, up_all, dn_all, left_ref, leftt_ref, up_out, dn_out):
    rows, rank = left_ref.shape
    w = up_ref.shape[1]
    up, dn = up_ref[...] + up_all[0], dn_ref[...] + dn_all[0]
    mean = jnp.concatenate([up, dn], axis=1) * inv
    averaged, later = mean[:rows], mean[rows:]
    right = dot(leftt_ref[...], averaged)
    averaged = averaged - DAMPING * dot(left_ref[...], right) + later
    up_out[:rank] = right[:, :w]
    dn_out[:rank] = right[:, w:]
    up_out[rank:] = averaged[:, :w]
    dn_out[rank:] = averaged[:, w:]


def reduced(place, up, dn, up_all, dn_all, left, leftt, n):
    rows, rank = left.shape
    w = up.shape[1]
    ring = jax.ShapeDtypeStruct((rank + rows, w), F32)
    mine = pl.BlockSpec((1, 2 * rows, w), lambda i, at: (at[0], 0, 0))
    return pl.pallas_call(
        functools.partial(reduced_kernel, 1.0 / n),
        out_shape=[ring, ring],
        grid_spec=pltpu.PrefetchScalarGridSpec(
            num_scalar_prefetch=1,
            grid=(1,),
            in_specs=[whole(up.shape), whole(dn.shape), mine, mine, whole((rows, rank)), whole((rank, rows))],
            out_specs=[whole(ring.shape)] * 2,
        ),
        cost_estimate=cost(24 * rows * rank * rank, 4e6),
        compiler_params=grant(12),
        name="reduced",
    )(place, up, dn, up_all, dn_all, left, leftt)


def partial_kernel(rank, me_ref, up_ref, dn_ref, *refs):
    parts, scratch = refs[:-1], refs[-1]
    rows = up_ref.shape[0] - rank
    both = jnp.concatenate([up_ref[...], dn_ref[...]], axis=1)
    right, averaged = both[:rank], both[rank:]
    scratch[...] = dot(averaged, right, 1, 1)
    squares = dot(jnp.ones((8, both.shape[1]), F32), right * right, 1, 1)
    block = rows // len(parts)
    for d, ref in enumerate(parts):
        at = pl.multiple_of((me_ref[0] ^ d) * block, 8)
        ref[:block] = scratch[pl.ds(at, block), :]
        ref[block:] = squares


def partial_raw(me, up, dn, rank, count):
    rows = up.shape[0] - rank
    part = jax.ShapeDtypeStruct((rows // count + 8, rank), F32)
    return pl.pallas_call(
        functools.partial(partial_kernel, rank),
        out_shape=[part] * count,
        in_specs=[SMEM] + [VMEM] * 2,
        out_specs=[VMEM] * count,
        scratch_shapes=[pltpu.VMEM((rows, rank), F32)],
        cost_estimate=cost(12 * rows * rank * rank, 2e6),
        compiler_params=grant(8),
        name="partial",
    )(me, up, dn)


def fetcher(pieces, buf, sem):
    k = pl.program_id(0)

    def copies(i, slot):
        out = []
        for j, (ref, row, col) in enumerate(pieces[i]):
            at = buf.at[slot, pl.ds(row, ref.shape[0]), pl.ds(col, ref.shape[1])]
            out.append(pltpu.make_async_copy(ref, at, sem.at[slot, j]))
        return out

    @pl.when(k == 0)
    def _():
        for c in copies(0, 0):
            c.start()

    for i in range(1, len(pieces)):

        @pl.when(k == i - 1)
        def _():
            for c in copies(i, i % 2):
                c.start()

    slot = lax.rem(k, 2)
    for c in copies(0, slot):
        c.wait()
    return buf[slot]


def advance_kernel(m, order_ref, *refs):
    ups, dns = refs[:m], refs[m : 2 * m]
    both_ref, l1_ref, l2_ref, l2t_ref, mom_out, y_out, sq_out, buf, sem, project, update = refs[2 * m :]
    k = pl.program_id(0)
    rank = l2t_ref.shape[0]
    w = buf.shape[2] // 2

    @pl.when(k == 0)
    def _():
        project[0], project[1] = halves(l2t_ref[...])
        update[0], update[1] = halves(DAMPING * jnp.concatenate([l1_ref[...], l2_ref[...]], axis=1))

    chunk = fetcher([[(ups[i], 0, 0), (dns[i], 0, w)] for i in range(m)], buf, sem)
    y1, averaged = chunk[:rank], chunk[rank:]
    y2 = dot3((project[0], project[1]), halves(averaged))
    y_out[0] = y2
    y = halves(jnp.concatenate([y1, y2], axis=0))
    mom_out[0] = both_ref[0] - dot3((update[0], update[1]), y)
    squares = dot(jnp.ones((8, 2 * w), F32), y2 * y2, 1, 1)

    @pl.when(k == 0)
    def _():
        sq_out[...] = squares

    @pl.when(k > 0)
    def _():
        sq_out[...] += squares


def chunk_at(steps, n):
    def at(k, place):
        step = steps[0]
        for i in range(1, len(steps)):
            step = jnp.where(k == i, steps[i], step)
        return lax.rem(place[0] + n - step, n)

    return at


def advance(place, steps, n, ups, dns, both, l1, l2, l2t):
    m = len(ups)
    _, rows, _ = both.shape
    rank = l1.shape[1]
    w = 2 * ups[0].shape[1]
    at = chunk_at(steps, n)
    block = pl.BlockSpec((1, rows, w), lambda k, place: (0, 0, at(k, place)))
    return pl.pallas_call(
        functools.partial(advance_kernel, m),
        out_shape=[
            jax.ShapeDtypeStruct(both.shape, F32),
            jax.ShapeDtypeStruct((m, rank, w), F32),
            jax.ShapeDtypeStruct((8, rank), F32),
        ],
        grid_spec=pltpu.PrefetchScalarGridSpec(
            num_scalar_prefetch=1,
            grid=(m,),
            in_specs=[VMEM] * (2 * m) + [block, whole((rows, rank)), whole((rows, rank)), whole((rank, rows))],
            out_specs=[block, pl.BlockSpec((1, rank, w), lambda k, order: (k, 0, 0)), whole((8, rank))],
            scratch_shapes=[
                pltpu.VMEM((2, rank + rows, w), F32),
                pltpu.SemaphoreType.DMA((2, 2)),
                pltpu.VMEM((2, rank, rows), BF16),
                pltpu.VMEM((2, rows, 2 * rank), BF16),
            ],
        ),
        input_output_aliases={1 + 2 * m: 0},
        cost_estimate=cost(m * w * 30 * rows * rank, m * w * rows * 24),
        compiler_params=grant(14),
        name="advance",
    )(place, *ups, *dns, both, l1, l2, l2t)


def weights_kernel(n, groups, rate, order_ref, *refs):
    ups, dns, ys = refs[:n], refs[n : 2 * n], refs[2 * n : 2 * n + len(groups)]
    w_ref, l1_ref, l2_ref, norm_ref, *totals, w_out, right_out, buf, sem, update = refs[2 * n + len(groups) :]
    rank = right_out.shape[1]
    w = buf.shape[2] // 2
    total = totals[0][0:1]
    for ref in totals[1:]:
        total = total + ref[0:1]
    norm = jnp.sqrt(total + EPS)

    @pl.when(pl.program_id(0) == 0)
    def _():
        left = jnp.concatenate([l1_ref[...] / norm_ref[...], l2_ref[...] / norm], axis=1)
        update[0], update[1] = halves(rate * left)

    pieces = []
    for y_ref, group in zip(ys, groups):
        for j in range(group):
            i = len(pieces)
            rows = pl.ds(0, rank)
            pieces.append([(ups[i].at[rows, :], 0, 0), (dns[i].at[rows, :], 0, w), (y_ref.at[j], rank, 0)])
    y = fetcher(pieces, buf, sem)
    w_out[...] = w_ref[...] - dot3((update[0], update[1]), halves(y))
    right_out[...] = y[rank:].T / norm


def finish(place, steps, ups, dns, ys, weights, l1, l2, norm, totals, rate):
    n = len(ups)
    rows, cols = weights.shape
    rank = l1.shape[1]
    w = cols // n
    groups = tuple(y.shape[0] for y in ys)
    at = chunk_at(steps, n)
    block = pl.BlockSpec((rows, w), lambda k, place: (0, at(k, place)))
    return pl.pallas_call(
        functools.partial(weights_kernel, n, groups, rate),
        out_shape=[
            jax.ShapeDtypeStruct((rows, cols), F32),
            jax.ShapeDtypeStruct((cols, rank), F32),
        ],
        grid_spec=pltpu.PrefetchScalarGridSpec(
            num_scalar_prefetch=1,
            grid=(n,),
            in_specs=[VMEM] * (2 * n + len(ys))
            + [block, whole((rows, rank)), whole((rows, rank)), whole((1, rank))]
            + [whole((8, rank))] * len(totals),
            out_specs=[block, pl.BlockSpec((w, rank), lambda k, place: (at(k, place), 0))],
            scratch_shapes=[
                pltpu.VMEM((2, 2 * rank, w), F32),
                pltpu.SemaphoreType.DMA((2, 3)),
                pltpu.VMEM((2, rows, 2 * rank), BF16),
            ],
        ),
        cost_estimate=cost(12 * rows * cols * rank, 32 * rows * cols),
        compiler_params=grant(28),
        name="finish",
    )(place, *ups, *dns, *ys, weights, l1, l2, norm, *totals)


def whole(shape):
    return pl.BlockSpec(shape, lambda k, order: (0,) * len(shape))


def flip(x, axis, bits):
    size = lax.axis_size(axis)
    return lax.ppermute(x, axis, [(i, i ^ bits) for i in range(size)])


def all_sum_stages(box):
    cols, reps = lax.axis_size("col"), lax.axis_size("rep")
    last = reps.bit_length() - 2

    def send(bit):
        box["pending"] = flip(box["x"], "rep", 1 << bit)

    def scatter():
        got = [flip(box["parts"][d], "col", d) for d in range(1, cols)]
        box["x"] = alike([box["parts"][0]] + got)
        send(0)

    def exchange(bit):
        def stage():
            box["x"] = alike([box["x"], box.pop("pending")])
            if bit < last:
                send(bit + 1)
                return
            box["parts"] = [box["x"]] + [flip(box["x"], "col", d) for d in range(1, cols)]

        return stage

    return [scatter] + [exchange(b) for b in range(last + 1)]


def ring_shards(rate, momentum, grads, weights, right_factor):
    n, count = lax.axis_size("rep"), lax.axis_size("col")
    _, rows, _ = momentum.shape
    rank = right_factor.shape[1]
    ring = list(range(0, n, 2)) + list(range(n - 1, 0, -2))
    rep = lax.axis_index("rep")
    place = jnp.where(rep % 2 == 0, rep // 2, n - 1 - rep // 2).astype(jnp.int32)[None]
    ahead = [(ring[i], ring[(i + 1) % n]) for i in range(n)]
    back = [(b, a) for a, b in ahead]
    me = lax.axis_index("col").astype(jnp.int32)[None]

    def tie(box, *arrays):
        keys = [k for k in box if k != "pending"]
        tied = lax.optimization_barrier(([box[k] for k in keys], list(arrays)))
        box.update(zip(keys, tied[0]))
        return tied[1]

    def step(up, dn):
        return lax.ppermute(up, "rep", ahead), lax.ppermute(dn, "rep", back)

    def first(scaled):
        def stage():
            out = orth_first(me, box.pop("parts"), rows, scaled)
            box.pop("x")
            box["left"], box["rest"] = out[:2]
            if scaled:
                box["norm"] = out[2]

        return stage

    box = {}
    stages = all_sum_stages(box)

    def begin():
        out = combine(me, momentum, grads, right_factor, n, count)
        box["up_all"], box["dn_all"], box["both"] = out[:3]
        box["parts"] = list(out[3])

    def second():
        box["left"], box["leftt"] = orth_second(box.pop("left"), box.pop("rest"))

    work = [[begin]] + [[stage] for stage in stages] + [[first(False)], [second]]
    up, dn = lead(place, momentum, grads, n)
    for k in range(1, n):
        up, dn = step(up, dn)
        if work:
            for stage in work.pop(0):
                stage()
            up, dn = tie(box, up, dn)
        if k < n - 1:
            up, dn = ring_add(place, k, up, dn, box["up_all"], box["dn_all"])
    l1 = box["left"]
    both = box["both"]
    up, dn = reduced(place, up, dn, box["up_all"], box["dn_all"], l1, box["leftt"], n)

    box = {}
    mine = (up, dn)
    stages = all_sum_stages(box)

    def begin_again():
        box["parts"] = list(partial_raw(me, *mine, rank, count))

    ups, dns = [up], [dn]
    ready, ys, totals = [], [], []

    def advance_ready():
        new = [c for c in range(n) if c not in ready and c < len(ups) and (n - c) % n < len(dns)]
        ready.extend(new)
        sides = ([ups[c] for c in new], [dns[(n - c) % n] for c in new])
        box["both"], y, squares = advance(place, new, n, *sides, box["both"], l1, box["left"], box["leftt"])
        ys.append(y)
        totals.append(squares)

    work = [[begin_again, stages[0]]] + [[stage] for stage in stages[1:]] + [[first(True)], [second]]
    for _ in range(1, n):
        up, dn = step(up, dn)
        if work:
            for stage in work.pop(0):
                stage()
            up, dn = tie(box, up, dn)
        else:
            box.setdefault("both", both)
            advance_ready()
            up, dn = tie(box, up, dn)
        ups.append(up)
        dns.append(dn)
    box.setdefault("both", both)
    advance_ready()
    total = alike_total(totals, count)
    sides = ([ups[c] for c in ready], [dns[(n - c) % n] for c in ready])
    new_weights, new_right = finish(place, ready, *sides, ys, weights, l1, box["left"], box["norm"], [total], rate)
    return new_weights, box["both"], new_right


def alike_total(totals, count):
    total = totals[0]
    for other in totals[1:]:
        total = alike([total, other])
    got = [flip(total, "col", d) for d in range(1, count)]
    return alike([total] + got)


def plain_orthonormal(left_raw):
    zero = jnp.zeros((1,), jnp.int32)
    left, rest = orth_first(zero, [left_raw], left_raw.shape[0], False)
    return orth_second(left, rest)[0]


def plain_shards(rate, momentum, grads, weights, right_factor):
    n = lax.axis_size("rep")
    moment = momentum[0]
    combined = moment + grads[0, 0].astype(F32)
    averaged, later = lax.psum((combined / n, grads[1, 0].astype(F32) / n), "rep")
    for step in range(STEPS):
        if step > 0:
            combined = moment + grads[step, 0].astype(F32)
            averaged = averaged + later
        left = plain_orthonormal(lax.psum(dot(averaged, right_factor), "col"))
        right_raw = dot(averaged, left, 0, 0)
        correction = DAMPING * dot(left, right_raw, 1, 1)
        moment = combined - correction
        averaged = averaged - correction
        totals = lax.psum(jnp.sum(right_raw * right_raw, axis=0), "col")
        right_factor = right_raw / jnp.sqrt(totals + EPS)
        weights = weights - rate * dot(left, right_factor, 1, 1)
    return weights, moment[None], right_factor


def solution(mesh):
    def body(momentum, grads, weights, right_factor):
        rep, col = mesh.shape["rep"], mesh.shape["col"]
        _, rows, cols = momentum.shape
        rank = right_factor.shape[1]
        rate = RATE * math.sqrt(rows * cols / rank)
        powers = rep & (rep - 1) == 0 and col & (col - 1) == 0 and col > 1
        fits = cols % (2 * LANES * rep * col) == 0 and rows % (8 * col) == 0
        ring = powers and 4 < rep <= 16 and col <= 8 and fits

        def shards(*args):
            return (ring_shards if ring else plain_shards)(rate, *args)

        step = jax.shard_map(
            shards,
            mesh=mesh,
            in_specs=(
                P("rep", None, "col"),
                P(None, "rep", None, "col"),
                P(None, "col"),
                P("col", None),
            ),
            out_specs=(P(None, "col"), P("rep", None, "col"), P("col", None)),
            check_vma=False,
        )
        return step(momentum, grads, weights, right_factor)

    return body
```

```python
import functools
import math

import jax
import jax.numpy as jnp
from jax import lax
from jax.experimental import pallas as pl
from jax.experimental.pallas import tpu as pltpu
from jax.sharding import PartitionSpec as P


STEPS = 2
DAMPING = 0.1
RATE = 0.2
EPS = 1e-06
LANES = 128
GROUP = 8

precise = lax.Precision.HIGHEST
VMEM = pl.BlockSpec(memory_space=pltpu.VMEM)
SMEM = pl.BlockSpec(memory_space=pltpu.SMEM)
F32 = jnp.float32
BF16 = jnp.bfloat16


def dot(a, b, ca=1, cb=0):
    return lax.dot_general(
        a, b, (((ca,), (cb,)), ((), ())), precision=precise, preferred_element_type=F32
    )


def halves(x):
    high = x.astype(BF16)
    return high, (x - high.astype(F32)).astype(BF16)


def dot3(a, b, ca=1, cb=0):
    def one(x, y):
        return lax.dot_general(x, y, (((ca,), (cb,)), ((), ())), preferred_element_type=F32)

    return one(a[0], b[0]) + (one(a[0], b[1]) + one(a[1], b[0]))


def grant(mib):
    return pltpu.CompilerParams(vmem_limit_bytes=mib << 20)


def cost(flops, moved):
    return pl.CostEstimate(flops=int(flops), bytes_accessed=int(moved), transcendentals=0)


def eliminate(rows, group):
    count, n = len(rows), len(rows) * 8
    lane = lax.broadcasted_iota(jnp.int32, (8, n), 1)
    sub = lax.broadcasted_iota(jnp.int32, (8, n), 0)
    rows = list(rows)
    for j in range(0, n, group):
        rb, s = j // 8, j % 8

        def across(x, k):
            return jnp.broadcast_to(x[:, k : k + 1], (8, n))

        def down(x, k):
            return jnp.broadcast_to(x[k : k + 1, :], (8, n))

        column = [{i: across(rows[i], j + k) for i in range(rb, count)} for k in range(group)]
        unit = [[None] * group for _ in range(group)]
        scaled = [[None] * group for _ in range(group)]
        inverse = [None] * group
        for a in range(group):
            for b in range(a + 1):
                v = down(column[b][rb], s + a)
                for e in range(b):
                    v = v - unit[a][e] * scaled[b][e]
                scaled[a][b] = v
                if b < a:
                    unit[a][b] = v * inverse[b]
            inverse[a] = 1.0 / scaled[a][a]
        inside = (lane >= j) & (lane < j + group)
        pivot_rows = []
        for k in range(group):
            r = jnp.where(lane == j + k, 1.0, jnp.where(inside, 0.0, down(rows[rb], s + k)))
            for e in range(k):
                r = r - unit[k][e] * pivot_rows[e]
            pivot_rows.append(r)
        for i in range(rb, count):
            if i == rb and s + group == 8 and s == 0:
                out = rows[i]
                for k in range(group):
                    r = jnp.where(lane == j + k, scaled[k][k], pivot_rows[k])
                    out = jnp.where(sub == k, r, out)
                rows[i] = out
                continue
            left = []
            for k in range(group):
                v = column[k][i]
                for e in range(k):
                    v = v - unit[k][e] * left[e]
                left.append(v)
            y = jnp.where(inside, 0.0, rows[i])
            for k in range(group):
                m = left[k] * inverse[k]
                if i == rb:
                    m = jnp.where(sub > s + k, m, 0.0)
                y = y - m * pivot_rows[k]
            if i == rb:
                out = jnp.where(sub < s, rows[i], y)
                for k in range(group):
                    r = jnp.where(lane == j + k, scaled[k][k], pivot_rows[k])
                    out = jnp.where(sub == s + k, r, out)
                y = out
            rows[i] = y
    return rows


def inverse_factor(matrix):
    n = matrix.shape[0]
    rows = eliminate([matrix[8 * i : 8 * i + 8, :] for i in range(n // 8)], GROUP)
    rows = jnp.concatenate(rows, axis=0)
    lane = lax.broadcasted_iota(jnp.int32, (n, n), 1)
    sub = lax.broadcasted_iota(jnp.int32, (n, n), 0)
    pivots = jnp.sum(jnp.where(lane == sub, rows, 0.0), axis=1, keepdims=True)
    unit = jnp.where(lane < sub, rows, jnp.where(lane == sub, 1.0, 0.0))
    return unit / jnp.sqrt(pivots)


def orthonormal_blocks(blocks):
    out = []
    for block in blocks:
        for q in out:
            block = block - dot(q, dot(q, block, 0, 0))
        out.append(dot(block, inverse_factor(dot(block, block, 0, 0)), 1, 1))
    return out


def column_blocks(x):
    return [x[:, i : i + LANES] for i in range(0, x.shape[1], LANES)]


def first_kernel(scaled, me_ref, *refs):
    count = len(refs) - 3 - scaled
    parts, (left_ref, rest_ref), raw = refs[:count], refs[count : count + 2], refs[-1]
    rows = raw.shape[0] // count
    for d in range(count):
        at = pl.multiple_of((me_ref[0] ^ d) * rows, 8)
        raw[pl.ds(at, rows), :] = parts[d][:rows]
    left_raw = raw[...]
    if scaled:
        norm = jnp.sqrt(parts[0][rows : rows + 1] + EPS)
        refs[count + 2][...] = norm
        left_raw = left_raw / norm
    blocks = column_blocks(left_raw)
    middle = len(blocks) // 2
    done = orthonormal_blocks(blocks[:middle])
    left_ref[...] = jnp.concatenate(done, axis=1)
    rest = blocks[middle:]
    for q in done:
        rest = [block - dot(q, dot(q, block, 0, 0)) for block in rest]
    rest_ref[...] = jnp.concatenate(rest, axis=1)


def second_kernel(left_ref, rest_ref, out_ref, outt_ref):
    done = orthonormal_blocks(column_blocks(rest_ref[...]))
    left = jnp.concatenate([left_ref[...]] + done, axis=1)
    out_ref[...] = left
    outt_ref[...] = left.T


def orth_first(me, parts, rows, scaled):
    rank = parts[0].shape[1]
    part = jax.ShapeDtypeStruct((rows, rank // 2), F32)
    shapes = [part, part] + [jax.ShapeDtypeStruct((1, rank), F32)] * scaled
    return pl.pallas_call(
        functools.partial(first_kernel, scaled),
        out_shape=shapes,
        in_specs=[SMEM] + [VMEM] * len(parts),
        out_specs=[VMEM] * len(shapes),
        scratch_shapes=[pltpu.VMEM((rows, rank), F32)],
        cost_estimate=cost(6e9, 1e6),
        compiler_params=grant(12),
        name="orth_first",
    )(me, *parts)


def orth_second(left, rest):
    rows, rank = left.shape[0], left.shape[1] + rest.shape[1]
    return pl.pallas_call(
        second_kernel,
        out_shape=[
            jax.ShapeDtypeStruct((rows, rank), F32),
            jax.ShapeDtypeStruct((rank, rows), F32),
        ],
        in_specs=[VMEM] * 2,
        out_specs=[VMEM] * 2,
        cost_estimate=cost(6e9, 1e6),
        compiler_params=grant(12),
        name="orth_second",
    )(left, rest)


def chunk_rows(mom, grads):
    return jnp.concatenate([mom[0] + grads[0, 0].astype(F32), grads[1, 0].astype(F32)], axis=0)


def lead_kernel(n, place_ref, mom, grads, up_ref, dn_ref, mom_buf, grads_buf, sem):
    w = up_ref.shape[1]
    copies = []
    for side, offset in enumerate((n - 1, 1)):
        chunk = lax.rem(place_ref[0] + offset, n)
        at = pl.ds(pl.multiple_of((2 * chunk + side) * w, w), w)
        copies.append(
            (
                pltpu.make_async_copy(mom.at[:, :, at], mom_buf.at[side], sem.at[side, 0]),
                pltpu.make_async_copy(grads.at[:, :, :, at], grads_buf.at[side], sem.at[side, 1]),
            )
        )
    for pair in copies:
        for copy in pair:
            copy.start()
    for side, ref in enumerate((up_ref, dn_ref)):
        for copy in copies[side]:
            copy.wait()
        ref[...] = chunk_rows(mom_buf[side], grads_buf[side])


def lead(place, momentum, grads, n):
    _, rows, cols = momentum.shape
    w = cols // n // 2
    part = jax.ShapeDtypeStruct((2 * rows, w), F32)
    return pl.pallas_call(
        functools.partial(lead_kernel, n),
        out_shape=[part, part],
        in_specs=[SMEM, pl.BlockSpec(memory_space=pltpu.HBM), pl.BlockSpec(memory_space=pltpu.HBM)],
        out_specs=[VMEM] * 2,
        scratch_shapes=[
            pltpu.VMEM((2, 1, rows, w), F32),
            pltpu.VMEM((2, 2, 1, rows, w), BF16),
            pltpu.SemaphoreType.DMA((2, 2)),
        ],
        cost_estimate=cost(4 * rows * w, 32 * rows * w),
        compiler_params=grant(58),
        name="lead",
    )(place, momentum, grads)


def combine_kernel(count, inv, me_ref, mom_ref, grads_ref, right_ref, up_ref, dn_ref, both_ref, *refs):
    parts, acc_ref = refs[:count], refs[count]
    k = pl.program_id(0)
    rows = mom_ref.shape[1]
    chunks, _, w = up_ref.shape
    total = mom_ref[0] + grads_ref[0, 0].astype(F32)
    later = grads_ref[1, 0].astype(F32)
    both_ref[0] = total + later
    for c in range(chunks):
        for side, ref in enumerate((up_ref, dn_ref)):
            at = (2 * c + side) * w
            ref[c, :rows] = total[:, at : at + w]
            ref[c, rows:] = later[:, at : at + w]
    part = dot(total, right_ref[...])

    @pl.when(k == 0)
    def _():
        acc_ref[...] = part

    @pl.when(k > 0)
    def _():
        acc_ref[...] += part

    @pl.when(k == pl.num_programs(0) - 1)
    def _():
        acc_ref[...] *= inv
        block = rows // count
        for d in range(count):
            at = pl.multiple_of((me_ref[0] ^ d) * block, 8)
            parts[d][...] = acc_ref[pl.ds(at, block), :]


def combine(me, momentum, grads, right_factor, n, count):
    _, rows, cols = momentum.shape
    rank = right_factor.shape[1]
    steps = n // 2
    w = cols // steps
    chunks = jax.ShapeDtypeStruct((n, 2 * rows, w // 4), F32)
    part = jax.ShapeDtypeStruct((rows // count, rank), F32)
    out = pl.pallas_call(
        functools.partial(combine_kernel, count, 1.0 / n),
        out_shape=[chunks, chunks, jax.ShapeDtypeStruct((1, rows, cols), F32)] + [part] * count,
        grid=(steps,),
        in_specs=[
            SMEM,
            pl.BlockSpec((1, rows, w), lambda k: (0, 0, k)),
            pl.BlockSpec((2, 1, rows, w), lambda k: (0, 0, 0, k)),
            pl.BlockSpec((w, rank), lambda k: (k, 0)),
        ],
        out_specs=[
            pl.BlockSpec((2, 2 * rows, w // 4), lambda k: (k, 0, 0)),
            pl.BlockSpec((2, 2 * rows, w // 4), lambda k: (k, 0, 0)),
            pl.BlockSpec((1, rows, w), lambda k: (0, 0, k)),
        ]
        + [pl.BlockSpec((rows // count, rank), lambda k: (0, 0))] * count,
        scratch_shapes=[pltpu.VMEM((rows, rank), F32)],
        cost_estimate=cost(12 * rows * cols * rank, 28 * rows * cols),
        compiler_params=grant(47),
        name="combine",
    )(me, momentum, grads, right_factor)
    return out[0], out[1], out[2], out[3:]


def ring_add_kernel(at_ref, up_ref, dn_ref, up_all, dn_all, up_out, dn_out):
    up_out[...] = up_ref[...] + up_all[0]
    dn_out[...] = dn_ref[...] + dn_all[0]


def ring_add(place, step, up, dn, up_all, dn_all):
    n = up_all.shape[0]
    shape = jax.ShapeDtypeStruct(up.shape, F32)
    return pl.pallas_call(
        ring_add_kernel,
        out_shape=[shape, shape],
        grid_spec=pltpu.PrefetchScalarGridSpec(
            num_scalar_prefetch=1,
            grid=(1,),
            in_specs=[
                whole(up.shape),
                whole(dn.shape),
                pl.BlockSpec((1,) + up.shape, lambda i, at: (lax.rem(at[0] + n - 1 - step, n), 0, 0)),
                pl.BlockSpec((1,) + dn.shape, lambda i, at: (lax.rem(at[0] + 1 + step, n), 0, 0)),
            ],
            out_specs=[whole(up.shape), whole(dn.shape)],
        ),
        cost_estimate=cost(2 * up.size, 24 * up.size),
        compiler_params=grant(8),
        name="ring_add",
    )(place, up, dn, up_all, dn_all)


def alike_kernel(*refs):
    terms = [ref[...] for ref in refs[:-1]]
    while len(terms) > 1:
        terms = [a + b for a, b in zip(terms[::2], terms[1::2])]
    refs[-1][...] = terms[0]


def alike(terms):
    return pl.pallas_call(
        alike_kernel,
        out_shape=jax.ShapeDtypeStruct(terms[0].shape, F32),
        in_specs=[VMEM] * len(terms),
        out_specs=VMEM,
        cost_estimate=cost(len(terms) * terms[0].size, 4 * (len(terms) + 1) * terms[0].size),
        compiler_params=grant(4),
        name="alike",
    )(*terms)


def reduced_kernel(inv, at_ref, up_ref, dn_ref, up_all, dn_all, left_ref, leftt_ref, up_out, dn_out):
    rows, rank = left_ref.shape
    w = up_ref.shape[1]
    up, dn = up_ref[...] + up_all[0], dn_ref[...] + dn_all[0]
    mean = jnp.concatenate([up, dn], axis=1) * inv
    averaged, later = mean[:rows], mean[rows:]
    right = dot(leftt_ref[...], averaged)
    averaged = averaged - DAMPING * dot(left_ref[...], right) + later
    up_out[:rank] = right[:, :w]
    dn_out[:rank] = right[:, w:]
    up_out[rank:] = averaged[:, :w]
    dn_out[rank:] = averaged[:, w:]


def reduced(place, up, dn, up_all, dn_all, left, leftt, n):
    rows, rank = left.shape
    w = up.shape[1]
    ring = jax.ShapeDtypeStruct((rank + rows, w), F32)
    mine = pl.BlockSpec((1, 2 * rows, w), lambda i, at: (at[0], 0, 0))
    return pl.pallas_call(
        functools.partial(reduced_kernel, 1.0 / n),
        out_shape=[ring, ring],
        grid_spec=pltpu.PrefetchScalarGridSpec(
            num_scalar_prefetch=1,
            grid=(1,),
            in_specs=[whole(up.shape), whole(dn.shape), mine, mine, whole((rows, rank)), whole((rank, rows))],
            out_specs=[whole(ring.shape)] * 2,
        ),
        cost_estimate=cost(24 * rows * rank * rank, 4e6),
        compiler_params=grant(12),
        name="reduced",
    )(place, up, dn, up_all, dn_all, left, leftt)


def partial_kernel(rank, me_ref, up_ref, dn_ref, *refs):
    parts, scratch = refs[:-1], refs[-1]
    rows = up_ref.shape[0] - rank
    both = jnp.concatenate([up_ref[...], dn_ref[...]], axis=1)
    right, averaged = both[:rank], both[rank:]
    scratch[...] = dot(averaged, right, 1, 1)
    squares = dot(jnp.ones((8, both.shape[1]), F32), right * right, 1, 1)
    block = rows // len(parts)
    for d, ref in enumerate(parts):
        at = pl.multiple_of((me_ref[0] ^ d) * block, 8)
        ref[:block] = scratch[pl.ds(at, block), :]
        ref[block:] = squares


def partial_raw(me, up, dn, rank, count):
    rows = up.shape[0] - rank
    part = jax.ShapeDtypeStruct((rows // count + 8, rank), F32)
    return pl.pallas_call(
        functools.partial(partial_kernel, rank),
        out_shape=[part] * count,
        in_specs=[SMEM] + [VMEM] * 2,
        out_specs=[VMEM] * count,
        scratch_shapes=[pltpu.VMEM((rows, rank), F32)],
        cost_estimate=cost(12 * rows * rank * rank, 2e6),
        compiler_params=grant(8),
        name="partial",
    )(me, up, dn)


def fetcher(pieces, buf, sem):
    k = pl.program_id(0)

    def copies(i, slot):
        out = []
        for j, (ref, row, col) in enumerate(pieces[i]):
            at = buf.at[slot, pl.ds(row, ref.shape[0]), pl.ds(col, ref.shape[1])]
            out.append(pltpu.make_async_copy(ref, at, sem.at[slot, j]))
        return out

    @pl.when(k == 0)
    def _():
        for c in copies(0, 0):
            c.start()

    for i in range(1, len(pieces)):

        @pl.when(k == i - 1)
        def _():
            for c in copies(i, i % 2):
                c.start()

    slot = lax.rem(k, 2)
    for c in copies(0, slot):
        c.wait()
    return buf[slot]


def advance_kernel(m, order_ref, *refs):
    ups, dns = refs[:m], refs[m : 2 * m]
    both_ref, l1_ref, l2_ref, l2t_ref, mom_out, y_out, sq_out, buf, sem, project, update = refs[2 * m :]
    k = pl.program_id(0)
    rank = l2t_ref.shape[0]
    w = buf.shape[2] // 2

    @pl.when(k == 0)
    def _():
        project[0], project[1] = halves(l2t_ref[...])
        update[0], update[1] = halves(DAMPING * jnp.concatenate([l1_ref[...], l2_ref[...]], axis=1))

    chunk = fetcher([[(ups[i], 0, 0), (dns[i], 0, w)] for i in range(m)], buf, sem)
    y1, averaged = chunk[:rank], chunk[rank:]
    y2 = dot3((project[0], project[1]), halves(averaged))
    y_out[0] = y2
    y = halves(jnp.concatenate([y1, y2], axis=0))
    mom_out[0] = both_ref[0] - dot3((update[0], update[1]), y)
    add_squares(k, y2, sq_out)


def add_squares(k, y, out):
    squares = dot(jnp.ones((8, y.shape[1]), F32), y * y, 1, 1)

    @pl.when(k == 0)
    def _():
        out[...] = squares

    @pl.when(k > 0)
    def _():
        out[...] += squares


def project_kernel(m, order_ref, *refs):
    ups, dns = refs[:m], refs[m : 2 * m]
    l2t_ref, y_out, sq_out, buf, sem, project = refs[2 * m :]
    k = pl.program_id(0)
    rank, rows = l2t_ref.shape
    w = buf.shape[2] // 2

    @pl.when(k == 0)
    def _():
        project[0], project[1] = halves(l2t_ref[...])

    at = pl.ds(rank, rows)
    averaged = fetcher([[(ups[i].at[at, :], 0, 0), (dns[i].at[at, :], 0, w)] for i in range(m)], buf, sem)
    y2 = dot3((project[0], project[1]), halves(averaged))
    y_out[0] = y2
    add_squares(k, y2, sq_out)


def moment_kernel(m, order_ref, *refs):
    ups, dns = refs[:m], refs[m : 2 * m]
    both_ref, y_ref, l1_ref, l2_ref, mom_out, buf, sem, update = refs[2 * m :]
    rank = y_ref.shape[1]
    w = buf.shape[2] // 2

    @pl.when(pl.program_id(0) == 0)
    def _():
        update[0], update[1] = halves(DAMPING * jnp.concatenate([l1_ref[...], l2_ref[...]], axis=1))

    at = pl.ds(0, rank)
    y1 = fetcher([[(ups[i].at[at, :], 0, 0), (dns[i].at[at, :], 0, w)] for i in range(m)], buf, sem)
    y = halves(jnp.concatenate([y1, y_ref[0]], axis=0))
    mom_out[0] = both_ref[0] - dot3((update[0], update[1]), y)


def chunk_at(steps, n):
    def at(k, place):
        step = steps[0]
        for i in range(1, len(steps)):
            step = jnp.where(k == i, steps[i], step)
        return lax.rem(place[0] + n - step, n)

    return at


def advance(mode, place, steps, n, ups, dns, both, y, l1, l2, l2t):
    m = len(ups)
    _, rows, _ = both.shape
    rank = l1.shape[1]
    w = 2 * ups[0].shape[1]
    at = chunk_at(steps, n)
    block = pl.BlockSpec((1, rows, w), lambda k, place: (0, 0, at(k, place)))
    y_block = pl.BlockSpec((1, rank, w), lambda k, place: (k, 0, 0))
    factors = [whole((rows, rank)), whole((rows, rank))]
    projected = [jax.ShapeDtypeStruct((m, rank, w), F32), jax.ShapeDtypeStruct((8, rank), F32)]
    moment = [jax.ShapeDtypeStruct(both.shape, F32)]
    project_scratch = pltpu.VMEM((2, rank, rows), BF16)
    moment_scratch = pltpu.VMEM((2, rows, 2 * rank), BF16)
    kernel, args, specs, outs, out_specs, scratch, fetched, aliases = {
        "both": (
            advance_kernel, [both, l1, l2, l2t], [block] + factors + [whole((rank, rows))],
            moment + projected, [block, y_block, whole((8, rank))],
            [project_scratch, moment_scratch], rank + rows, {1 + 2 * m: 0},
        ),
        "project": (
            project_kernel, [l2t], [whole((rank, rows))],
            projected, [y_block, whole((8, rank))], [project_scratch], rows, {},
        ),
        "moment": (
            moment_kernel, [both, y, l1, l2], [block, y_block] + factors,
            moment, [block], [moment_scratch], rank, {1 + 2 * m: 0},
        ),
    }[mode]
    return pl.pallas_call(
        functools.partial(kernel, m),
        out_shape=outs,
        grid_spec=pltpu.PrefetchScalarGridSpec(
            num_scalar_prefetch=1,
            grid=(m,),
            in_specs=[VMEM] * (2 * m) + specs,
            out_specs=out_specs,
            scratch_shapes=[pltpu.VMEM((2, fetched, w), F32), pltpu.SemaphoreType.DMA((2, 2))] + scratch,
        ),
        input_output_aliases=aliases,
        cost_estimate=cost(m * w * 20 * rows * rank, m * w * rows * 24),
        compiler_params=grant(14),
    )(place, *ups, *dns, *args)


def weights_kernel(n, groups, rate, order_ref, *refs):
    ups, dns, ys = refs[:n], refs[n : 2 * n], refs[2 * n : 2 * n + len(groups)]
    w_ref, l1_ref, l2_ref, norm_ref, *totals, w_out, right_out, buf, sem, update = refs[2 * n + len(groups) :]
    rank = right_out.shape[1]
    w = buf.shape[2] // 2
    total = totals[0][0:1]
    for ref in totals[1:]:
        total = total + ref[0:1]
    norm = jnp.sqrt(total + EPS)

    @pl.when(pl.program_id(0) == 0)
    def _():
        left = jnp.concatenate([l1_ref[...] / norm_ref[...], l2_ref[...] / norm], axis=1)
        update[0], update[1] = halves(rate * left)

    pieces = []
    for y_ref, group in zip(ys, groups):
        for j in range(group):
            i = len(pieces)
            rows = pl.ds(0, rank)
            pieces.append([(ups[i].at[rows, :], 0, 0), (dns[i].at[rows, :], 0, w), (y_ref.at[j], rank, 0)])
    y = fetcher(pieces, buf, sem)
    w_out[...] = w_ref[...] - dot3((update[0], update[1]), halves(y))
    right_out[...] = y[rank:].T / norm


def finish(place, steps, ups, dns, ys, weights, l1, l2, norm, totals, rate):
    n = len(ups)
    rows, cols = weights.shape
    rank = l1.shape[1]
    w = cols // n
    groups = tuple(y.shape[0] for y in ys)
    at = chunk_at(steps, n)
    block = pl.BlockSpec((rows, w), lambda k, place: (0, at(k, place)))
    return pl.pallas_call(
        functools.partial(weights_kernel, n, groups, rate),
        out_shape=[
            jax.ShapeDtypeStruct((rows, cols), F32),
            jax.ShapeDtypeStruct((cols, rank), F32),
        ],
        grid_spec=pltpu.PrefetchScalarGridSpec(
            num_scalar_prefetch=1,
            grid=(n,),
            in_specs=[VMEM] * (2 * n + len(ys))
            + [block, whole((rows, rank)), whole((rows, rank)), whole((1, rank))]
            + [whole((8, rank))] * len(totals),
            out_specs=[block, pl.BlockSpec((w, rank), lambda k, place: (at(k, place), 0))],
            scratch_shapes=[
                pltpu.VMEM((2, 2 * rank, w), F32),
                pltpu.SemaphoreType.DMA((2, 3)),
                pltpu.VMEM((2, rows, 2 * rank), BF16),
            ],
        ),
        cost_estimate=cost(12 * rows * cols * rank, 32 * rows * cols),
        compiler_params=grant(28),
        name="finish",
    )(place, *ups, *dns, *ys, weights, l1, l2, norm, *totals)


def whole(shape):
    return pl.BlockSpec(shape, lambda k, order: (0,) * len(shape))


def flip(x, axis, bits):
    size = lax.axis_size(axis)
    return lax.ppermute(x, axis, [(i, i ^ bits) for i in range(size)])


def rep_masks(reps):
    return [[1, 2, 3]] + [[1 << b] for b in range(2, reps.bit_length() - 1)]


def all_sum_stages(box):
    cols = lax.axis_size("col")
    masks = rep_masks(lax.axis_size("rep"))

    def send(x, axis, partners):
        return [flip(part, axis, p) for part, p in zip(x, partners)]

    def scatter():
        parts = box.pop("parts")
        box["x"] = parts[0]
        box["pending"] = send(parts[1:], "col", range(1, cols))

    def exchange(i):
        def stage():
            x = box["x"] = alike([box["x"]] + box.pop("pending"))
            if i < len(masks):
                box["pending"] = send([x] * len(masks[i]), "rep", masks[i])
            else:
                box["pending"] = send([x] * (cols - 1), "col", range(1, cols))

        return stage

    return [scatter] + [exchange(i) for i in range(len(masks) + 1)]


def ring_shards(rate, momentum, grads, weights, right_factor):
    n, count = lax.axis_size("rep"), lax.axis_size("col")
    _, rows, _ = momentum.shape
    rank = right_factor.shape[1]
    ring = list(range(0, n, 2)) + list(range(n - 1, 0, -2))
    rep = lax.axis_index("rep")
    place = jnp.where(rep % 2 == 0, rep // 2, n - 1 - rep // 2).astype(jnp.int32)[None]
    ahead = [(ring[i], ring[(i + 1) % n]) for i in range(n)]
    back = [(b, a) for a, b in ahead]
    me = lax.axis_index("col").astype(jnp.int32)[None]

    def tie(box, *arrays):
        keys = [k for k in box if k != "pending"]
        tied = lax.optimization_barrier(([box[k] for k in keys], list(arrays)))
        box.update(zip(keys, tied[0]))
        return tied[1]

    def step(up, dn):
        return lax.ppermute(up, "rep", ahead), lax.ppermute(dn, "rep", back)

    def first(scaled):
        def stage():
            out = orth_first(me, [box.pop("x")] + box.pop("pending"), rows, scaled)
            box["left"], box["rest"] = out[:2]
            if scaled:
                box["norm"] = out[2]

        return stage

    box = {}
    stages = all_sum_stages(box)

    def begin():
        out = combine(me, momentum, grads, right_factor, n, count)
        box["up_all"], box["dn_all"], box["both"] = out[:3]
        box["parts"] = list(out[3])

    def second():
        box["left"], box["leftt"] = orth_second(box.pop("left"), box.pop("rest"))

    work = [[begin]] + [[stage] for stage in stages] + [[first(False)], [second]]
    up, dn = lead(place, momentum, grads, n)
    for k in range(1, n):
        up, dn = step(up, dn)
        if work:
            for stage in work.pop(0):
                stage()
            up, dn = tie(box, up, dn)
        if k < n - 1:
            up, dn = ring_add(place, k, up, dn, box["up_all"], box["dn_all"])
    l1 = box["left"]
    both = box["both"]
    up, dn = reduced(place, up, dn, box["up_all"], box["dn_all"], l1, box["leftt"], n)

    box = {}
    mine = (up, dn)
    stages = all_sum_stages(box)

    def begin_again():
        box["parts"] = list(partial_raw(me, *mine, rank, count))

    ups, dns = [up], [dn]
    ready, ys, totals = [], [], []

    def advance_ready(last=False):
        new = [c for c in range(n) if c not in ready and c < len(ups) and (n - c) % n < len(dns)]
        ready.extend(new)
        sides = ([ups[c] for c in new], [dns[(n - c) % n] for c in new])
        factors = (l1, box["left"], box["leftt"])
        if not last:
            box["both"], y, squares = advance("both", place, new, n, *sides, box["both"], None, *factors)
            ys.append(y)
            totals.append(squares)
            return None
        y, squares = advance("project", place, new, n, *sides, box["both"], None, *factors)
        ys.append(y)
        totals.append(squares)
        total = alike_total(totals, count)
        (box["both"],) = advance("moment", place, new, n, *sides, box["both"], y, *factors)
        return total

    work = [[begin_again, stages[0]]] + [[stage] for stage in stages[1:]] + [[first(True)], [second]]
    for _ in range(1, n):
        up, dn = step(up, dn)
        if work:
            for stage in work.pop(0):
                stage()
            up, dn = tie(box, up, dn)
        else:
            box.setdefault("both", both)
            advance_ready()
            up, dn = tie(box, up, dn)
        ups.append(up)
        dns.append(dn)
    box.setdefault("both", both)
    total = advance_ready(last=True)
    sides = ([ups[c] for c in ready], [dns[(n - c) % n] for c in ready])
    new_weights, new_right = finish(place, ready, *sides, ys, weights, l1, box["left"], box["norm"], [total], rate)
    return new_weights, box["both"], new_right


def alike_total(totals, count):
    total = totals[0]
    for other in totals[1:]:
        total = alike([total, other])
    got = [flip(total, "col", d) for d in range(1, count)]
    return alike([total] + got)


def plain_orthonormal(left_raw):
    zero = jnp.zeros((1,), jnp.int32)
    left, rest = orth_first(zero, [left_raw], left_raw.shape[0], False)
    return orth_second(left, rest)[0]


def plain_shards(rate, momentum, grads, weights, right_factor):
    n = lax.axis_size("rep")
    moment = momentum[0]
    combined = moment + grads[0, 0].astype(F32)
    averaged, later = lax.psum((combined / n, grads[1, 0].astype(F32) / n), "rep")
    for step in range(STEPS):
        if step > 0:
            combined = moment + grads[step, 0].astype(F32)
            averaged = averaged + later
        left = plain_orthonormal(lax.psum(dot(averaged, right_factor), "col"))
        right_raw = dot(averaged, left, 0, 0)
        correction = DAMPING * dot(left, right_raw, 1, 1)
        moment = combined - correction
        averaged = averaged - correction
        totals = lax.psum(jnp.sum(right_raw * right_raw, axis=0), "col")
        right_factor = right_raw / jnp.sqrt(totals + EPS)
        weights = weights - rate * dot(left, right_factor, 1, 1)
    return weights, moment[None], right_factor


def solution(mesh):
    def body(momentum, grads, weights, right_factor):
        rep, col = mesh.shape["rep"], mesh.shape["col"]
        _, rows, cols = momentum.shape
        rank = right_factor.shape[1]
        rate = RATE * math.sqrt(rows * cols / rank)
        powers = rep & (rep - 1) == 0 and col & (col - 1) == 0 and col > 1
        fits = cols % (2 * LANES * rep * col) == 0 and rows % (8 * col) == 0
        ring = powers and 4 < rep <= 16 and col <= 8 and fits

        def shards(*args):
            return (ring_shards if ring else plain_shards)(rate, *args)

        step = jax.shard_map(
            shards,
            mesh=mesh,
            in_specs=(
                P("rep", None, "col"),
                P(None, "rep", None, "col"),
                P(None, "col"),
                P("col", None),
            ),
            out_specs=(P(None, "col"), P("rep", None, "col"), P("col", None)),
            check_vma=False,
        )
        return step(momentum, grads, weights, right_factor)

    return body
```

```python
import functools
import math

import jax
import jax.numpy as jnp
from jax import lax
from jax.experimental import pallas as pl
from jax.experimental.pallas import tpu as pltpu
from jax.sharding import PartitionSpec as P


STEPS = 2
DAMPING = 0.1
RATE = 0.2
EPS = 1e-06
LANES = 128
GROUP = 8

precise = lax.Precision.HIGHEST
VMEM = pl.BlockSpec(memory_space=pltpu.VMEM)
SMEM = pl.BlockSpec(memory_space=pltpu.SMEM)
F32 = jnp.float32
BF16 = jnp.bfloat16


def dot(a, b, ca=1, cb=0):
    return lax.dot_general(
        a, b, (((ca,), (cb,)), ((), ())), precision=precise, preferred_element_type=F32
    )


def halves(x):
    high = x.astype(BF16)
    return high, (x - high.astype(F32)).astype(BF16)


def dot3(a, b, ca=1, cb=0):
    def one(x, y):
        return lax.dot_general(x, y, (((ca,), (cb,)), ((), ())), preferred_element_type=F32)

    return one(a[0], b[0]) + (one(a[0], b[1]) + one(a[1], b[0]))


def grant(mib):
    return pltpu.CompilerParams(vmem_limit_bytes=mib << 20)


def cost(flops, moved):
    return pl.CostEstimate(flops=int(flops), bytes_accessed=int(moved), transcendentals=0)


def eliminate(rows, group):
    count, n = len(rows), len(rows) * 8
    lane = lax.broadcasted_iota(jnp.int32, (8, n), 1)
    sub = lax.broadcasted_iota(jnp.int32, (8, n), 0)
    rows = list(rows)
    for j in range(0, n, group):
        rb, s = j // 8, j % 8

        def across(x, k):
            return jnp.broadcast_to(x[:, k : k + 1], (8, n))

        def down(x, k):
            return jnp.broadcast_to(x[k : k + 1, :], (8, n))

        column = [{i: across(rows[i], j + k) for i in range(rb, count)} for k in range(group)]
        unit = [[None] * group for _ in range(group)]
        scaled = [[None] * group for _ in range(group)]
        inverse = [None] * group
        for a in range(group):
            for b in range(a + 1):
                v = down(column[b][rb], s + a)
                for e in range(b):
                    v = v - unit[a][e] * scaled[b][e]
                scaled[a][b] = v
                if b < a:
                    unit[a][b] = v * inverse[b]
            inverse[a] = 1.0 / scaled[a][a]
        inside = (lane >= j) & (lane < j + group)
        pivot_rows = []
        for k in range(group):
            r = jnp.where(lane == j + k, 1.0, jnp.where(inside, 0.0, down(rows[rb], s + k)))
            for e in range(k):
                r = r - unit[k][e] * pivot_rows[e]
            pivot_rows.append(r)
        for i in range(rb, count):
            if i == rb and s + group == 8 and s == 0:
                out = rows[i]
                for k in range(group):
                    r = jnp.where(lane == j + k, scaled[k][k], pivot_rows[k])
                    out = jnp.where(sub == k, r, out)
                rows[i] = out
                continue
            left = []
            for k in range(group):
                v = column[k][i]
                for e in range(k):
                    v = v - unit[k][e] * left[e]
                left.append(v)
            y = jnp.where(inside, 0.0, rows[i])
            for k in range(group):
                m = left[k] * inverse[k]
                if i == rb:
                    m = jnp.where(sub > s + k, m, 0.0)
                y = y - m * pivot_rows[k]
            if i == rb:
                out = jnp.where(sub < s, rows[i], y)
                for k in range(group):
                    r = jnp.where(lane == j + k, scaled[k][k], pivot_rows[k])
                    out = jnp.where(sub == s + k, r, out)
                y = out
            rows[i] = y
    return rows


def inverse_factor(matrix):
    n = matrix.shape[0]
    rows = eliminate([matrix[8 * i : 8 * i + 8, :] for i in range(n // 8)], GROUP)
    rows = jnp.concatenate(rows, axis=0)
    lane = lax.broadcasted_iota(jnp.int32, (n, n), 1)
    sub = lax.broadcasted_iota(jnp.int32, (n, n), 0)
    pivots = jnp.sum(jnp.where(lane == sub, rows, 0.0), axis=1, keepdims=True)
    unit = jnp.where(lane < sub, rows, jnp.where(lane == sub, 1.0, 0.0))
    return unit / jnp.sqrt(pivots)


def orthonormal_blocks(blocks):
    out = []
    for block in blocks:
        for q in out:
            block = block - dot(q, dot(q, block, 0, 0))
        out.append(dot(block, inverse_factor(dot(block, block, 0, 0)), 1, 1))
    return out


def column_blocks(x):
    return [x[:, i : i + LANES] for i in range(0, x.shape[1], LANES)]


def first_kernel(scaled, me_ref, *refs):
    count = len(refs) - 3 - scaled
    parts, (left_ref, rest_ref), raw = refs[:count], refs[count : count + 2], refs[-1]
    rows = raw.shape[0] // count
    for d in range(count):
        at = pl.multiple_of((me_ref[0] ^ d) * rows, 8)
        raw[pl.ds(at, rows), :] = parts[d][:rows]
    left_raw = raw[...]
    if scaled:
        norm = jnp.sqrt(parts[0][rows : rows + 1] + EPS)
        refs[count + 2][...] = norm
        left_raw = left_raw / norm
    blocks = column_blocks(left_raw)
    middle = len(blocks) // 2
    done = orthonormal_blocks(blocks[:middle])
    left_ref[...] = jnp.concatenate(done, axis=1)
    rest = blocks[middle:]
    for q in done:
        rest = [block - dot(q, dot(q, block, 0, 0)) for block in rest]
    rest_ref[...] = jnp.concatenate(rest, axis=1)


def second_kernel(left_ref, rest_ref, out_ref, outt_ref):
    done = orthonormal_blocks(column_blocks(rest_ref[...]))
    left = jnp.concatenate([left_ref[...]] + done, axis=1)
    out_ref[...] = left
    outt_ref[...] = left.T


def orth_first(me, parts, rows, scaled):
    rank = parts[0].shape[1]
    part = jax.ShapeDtypeStruct((rows, rank // 2), F32)
    shapes = [part, part] + [jax.ShapeDtypeStruct((1, rank), F32)] * scaled
    return pl.pallas_call(
        functools.partial(first_kernel, scaled),
        out_shape=shapes,
        in_specs=[SMEM] + [VMEM] * len(parts),
        out_specs=[VMEM] * len(shapes),
        scratch_shapes=[pltpu.VMEM((rows, rank), F32)],
        cost_estimate=cost(6e9, 1e6),
        compiler_params=grant(12),
        name="orth_first",
    )(me, *parts)


def orth_second(left, rest):
    rows, rank = left.shape[0], left.shape[1] + rest.shape[1]
    return pl.pallas_call(
        second_kernel,
        out_shape=[
            jax.ShapeDtypeStruct((rows, rank), F32),
            jax.ShapeDtypeStruct((rank, rows), F32),
        ],
        in_specs=[VMEM] * 2,
        out_specs=[VMEM] * 2,
        cost_estimate=cost(6e9, 1e6),
        compiler_params=grant(12),
        name="orth_second",
    )(left, rest)


def chunk_rows(mom, grads):
    return jnp.concatenate([mom[0] + grads[0, 0].astype(F32), grads[1, 0].astype(F32)], axis=0)


def lead_kernel(n, place_ref, mom, grads, up_ref, dn_ref, mom_buf, grads_buf, sem):
    w = up_ref.shape[1]
    copies = []
    for side, offset in enumerate((n - 1, 1)):
        chunk = lax.rem(place_ref[0] + offset, n)
        at = pl.ds(pl.multiple_of((2 * chunk + side) * w, w), w)
        copies.append(
            (
                pltpu.make_async_copy(mom.at[:, :, at], mom_buf.at[side], sem.at[side, 0]),
                pltpu.make_async_copy(grads.at[:, :, :, at], grads_buf.at[side], sem.at[side, 1]),
            )
        )
    for pair in copies:
        for copy in pair:
            copy.start()
    for side, ref in enumerate((up_ref, dn_ref)):
        for copy in copies[side]:
            copy.wait()
        ref[...] = chunk_rows(mom_buf[side], grads_buf[side])


def lead(place, momentum, grads, n):
    _, rows, cols = momentum.shape
    w = cols // n // 2
    part = jax.ShapeDtypeStruct((2 * rows, w), F32)
    return pl.pallas_call(
        functools.partial(lead_kernel, n),
        out_shape=[part, part],
        in_specs=[SMEM, pl.BlockSpec(memory_space=pltpu.HBM), pl.BlockSpec(memory_space=pltpu.HBM)],
        out_specs=[VMEM] * 2,
        scratch_shapes=[
            pltpu.VMEM((2, 1, rows, w), F32),
            pltpu.VMEM((2, 2, 1, rows, w), BF16),
            pltpu.SemaphoreType.DMA((2, 2)),
        ],
        cost_estimate=cost(4 * rows * w, 32 * rows * w),
        compiler_params=grant(58),
        name="lead",
    )(place, momentum, grads)


def combine_kernel(count, inv, me_ref, mom_ref, grads_ref, right_ref, up_ref, dn_ref, both_ref, *refs):
    parts, acc_ref = refs[:count], refs[count]
    k = pl.program_id(0)
    rows = mom_ref.shape[1]
    chunks, _, w = up_ref.shape
    total = mom_ref[0] + grads_ref[0, 0].astype(F32)
    later = grads_ref[1, 0].astype(F32)
    both_ref[0] = total + later
    for c in range(chunks):
        for side, ref in enumerate((up_ref, dn_ref)):
            at = (2 * c + side) * w
            ref[c, :rows] = total[:, at : at + w]
            ref[c, rows:] = later[:, at : at + w]
    part = dot(total, right_ref[...])

    @pl.when(k == 0)
    def _():
        acc_ref[...] = part

    @pl.when(k > 0)
    def _():
        acc_ref[...] += part

    @pl.when(k == pl.num_programs(0) - 1)
    def _():
        acc_ref[...] *= inv
        block = rows // count
        for d in range(count):
            at = pl.multiple_of((me_ref[0] ^ d) * block, 8)
            parts[d][...] = acc_ref[pl.ds(at, block), :]


def combine(me, momentum, grads, right_factor, n, count):
    _, rows, cols = momentum.shape
    rank = right_factor.shape[1]
    steps = n // 2
    w = cols // steps
    chunks = jax.ShapeDtypeStruct((n, 2 * rows, w // 4), F32)
    part = jax.ShapeDtypeStruct((rows // count, rank), F32)
    out = pl.pallas_call(
        functools.partial(combine_kernel, count, 1.0 / n),
        out_shape=[chunks, chunks, jax.ShapeDtypeStruct((1, rows, cols), F32)] + [part] * count,
        grid=(steps,),
        in_specs=[
            SMEM,
            pl.BlockSpec((1, rows, w), lambda k: (0, 0, k)),
            pl.BlockSpec((2, 1, rows, w), lambda k: (0, 0, 0, k)),
            pl.BlockSpec((w, rank), lambda k: (k, 0)),
        ],
        out_specs=[
            pl.BlockSpec((2, 2 * rows, w // 4), lambda k: (k, 0, 0)),
            pl.BlockSpec((2, 2 * rows, w // 4), lambda k: (k, 0, 0)),
            pl.BlockSpec((1, rows, w), lambda k: (0, 0, k)),
        ]
        + [pl.BlockSpec((rows // count, rank), lambda k: (0, 0))] * count,
        scratch_shapes=[pltpu.VMEM((rows, rank), F32)],
        cost_estimate=cost(12 * rows * cols * rank, 28 * rows * cols),
        compiler_params=grant(47),
        name="combine",
    )(me, momentum, grads, right_factor)
    return out[0], out[1], out[2], out[3:]


def ring_add_kernel(place_ref, x_ref, chunks_ref, out_ref):
    out_ref[...] = x_ref[...] + chunks_ref[0]


def ring_add(place, offset, x, chunks):
    n = chunks.shape[0]
    return pl.pallas_call(
        ring_add_kernel,
        out_shape=jax.ShapeDtypeStruct(x.shape, F32),
        grid_spec=pltpu.PrefetchScalarGridSpec(
            num_scalar_prefetch=1,
            grid=(1,),
            in_specs=[
                whole(x.shape),
                pl.BlockSpec((1,) + x.shape, lambda i, place: (lax.rem(place[0] + offset, n), 0, 0)),
            ],
            out_specs=whole(x.shape),
        ),
        cost_estimate=cost(x.size, 12 * x.size),
        compiler_params=grant(6),
        name="ring_add",
    )(place, x, chunks)


def alike_kernel(*refs):
    terms = [ref[...] for ref in refs[:-1]]
    while len(terms) > 1:
        terms = [a + b for a, b in zip(terms[::2], terms[1::2])]
    refs[-1][...] = terms[0]


def alike(terms):
    return pl.pallas_call(
        alike_kernel,
        out_shape=jax.ShapeDtypeStruct(terms[0].shape, F32),
        in_specs=[VMEM] * len(terms),
        out_specs=VMEM,
        cost_estimate=cost(len(terms) * terms[0].size, 4 * (len(terms) + 1) * terms[0].size),
        compiler_params=grant(4),
        name="alike",
    )(*terms)


def reduced_kernel(inv, at_ref, up_ref, dn_ref, up_all, dn_all, left_ref, leftt_ref, up_out, dn_out):
    rows, rank = left_ref.shape
    w = up_ref.shape[1]
    up, dn = up_ref[...] + up_all[0], dn_ref[...] + dn_all[0]
    mean = jnp.concatenate([up, dn], axis=1) * inv
    averaged, later = mean[:rows], mean[rows:]
    right = dot(leftt_ref[...], averaged)
    averaged = averaged - DAMPING * dot(left_ref[...], right) + later
    up_out[:rank] = right[:, :w]
    dn_out[:rank] = right[:, w:]
    up_out[rank:] = averaged[:, :w]
    dn_out[rank:] = averaged[:, w:]


def reduced(place, up, dn, up_all, dn_all, left, leftt, n):
    rows, rank = left.shape
    w = up.shape[1]
    ring = jax.ShapeDtypeStruct((rank + rows, w), F32)
    mine = pl.BlockSpec((1, 2 * rows, w), lambda i, at: (at[0], 0, 0))
    return pl.pallas_call(
        functools.partial(reduced_kernel, 1.0 / n),
        out_shape=[ring, ring],
        grid_spec=pltpu.PrefetchScalarGridSpec(
            num_scalar_prefetch=1,
            grid=(1,),
            in_specs=[whole(up.shape), whole(dn.shape), mine, mine, whole((rows, rank)), whole((rank, rows))],
            out_specs=[whole(ring.shape)] * 2,
        ),
        cost_estimate=cost(24 * rows * rank * rank, 4e6),
        compiler_params=grant(12),
        name="reduced",
    )(place, up, dn, up_all, dn_all, left, leftt)


def partial_kernel(rank, me_ref, up_ref, dn_ref, *refs):
    parts, scratch = refs[:-1], refs[-1]
    rows = up_ref.shape[0] - rank
    both = jnp.concatenate([up_ref[...], dn_ref[...]], axis=1)
    right, averaged = both[:rank], both[rank:]
    scratch[...] = dot(averaged, right, 1, 1)
    squares = dot(jnp.ones((8, both.shape[1]), F32), right * right, 1, 1)
    block = rows // len(parts)
    for d, ref in enumerate(parts):
        at = pl.multiple_of((me_ref[0] ^ d) * block, 8)
        ref[:block] = scratch[pl.ds(at, block), :]
        ref[block:] = squares


def partial_raw(me, up, dn, rank, count):
    rows = up.shape[0] - rank
    part = jax.ShapeDtypeStruct((rows // count + 8, rank), F32)
    return pl.pallas_call(
        functools.partial(partial_kernel, rank),
        out_shape=[part] * count,
        in_specs=[SMEM] + [VMEM] * 2,
        out_specs=[VMEM] * count,
        scratch_shapes=[pltpu.VMEM((rows, rank), F32)],
        cost_estimate=cost(12 * rows * rank * rank, 2e6),
        compiler_params=grant(8),
        name="partial",
    )(me, up, dn)


def fetcher(pieces, buf, sem):
    k = pl.program_id(0)

    def copies(i, slot):
        out = []
        for j, (ref, row, col) in enumerate(pieces[i]):
            at = buf.at[slot, pl.ds(row, ref.shape[0]), pl.ds(col, ref.shape[1])]
            out.append(pltpu.make_async_copy(ref, at, sem.at[slot, j]))
        return out

    @pl.when(k == 0)
    def _():
        for c in copies(0, 0):
            c.start()

    for i in range(1, len(pieces)):

        @pl.when(k == i - 1)
        def _():
            for c in copies(i, i % 2):
                c.start()

    slot = lax.rem(k, 2)
    for c in copies(0, slot):
        c.wait()
    return buf[slot]


def advance_kernel(m, order_ref, *refs):
    ups, dns = refs[:m], refs[m : 2 * m]
    both_ref, l1_ref, l2_ref, l2t_ref, mom_out, y_out, sq_out, buf, sem, project, update = refs[2 * m :]
    k = pl.program_id(0)
    rank = l2t_ref.shape[0]
    w = buf.shape[2] // 2

    @pl.when(k == 0)
    def _():
        project[0], project[1] = halves(l2t_ref[...])
        update[0], update[1] = halves(DAMPING * jnp.concatenate([l1_ref[...], l2_ref[...]], axis=1))

    chunk = fetcher([[(ups[i], 0, 0), (dns[i], 0, w)] for i in range(m)], buf, sem)
    y1, averaged = chunk[:rank], chunk[rank:]
    y2 = dot3((project[0], project[1]), halves(averaged))
    y_out[0] = y2
    y = halves(jnp.concatenate([y1, y2], axis=0))
    mom_out[0] = both_ref[0] - dot3((update[0], update[1]), y)
    add_squares(k, y2, sq_out)


def add_squares(k, y, out):
    ones = jnp.ones((8, y.shape[1]), BF16)
    high, low = [lax.dot_general(ones, part, (((1,), (1,)), ((), ())), preferred_element_type=F32) for part in halves(y * y)]
    squares = high + low

    @pl.when(k == 0)
    def _():
        out[...] = squares

    @pl.when(k > 0)
    def _():
        out[...] += squares


def project_kernel(m, order_ref, *refs):
    ups, dns = refs[:m], refs[m : 2 * m]
    l2t_ref, y_out, sq_out, buf, sem, project = refs[2 * m :]
    k = pl.program_id(0)
    rank, rows = l2t_ref.shape
    w = buf.shape[2] // 2

    @pl.when(k == 0)
    def _():
        project[0], project[1] = halves(l2t_ref[...])

    at = pl.ds(rank, rows)
    averaged = fetcher([[(ups[i].at[at, :], 0, 0), (dns[i].at[at, :], 0, w)] for i in range(m)], buf, sem)
    y2 = dot3((project[0], project[1]), halves(averaged))
    y_out[0] = y2
    add_squares(k, y2, sq_out)


def moment_kernel(m, order_ref, *refs):
    ups, dns = refs[:m], refs[m : 2 * m]
    both_ref, y_ref, l1_ref, l2_ref, mom_out, buf, sem, update = refs[2 * m :]
    rank = y_ref.shape[1]
    w = buf.shape[2] // 2

    @pl.when(pl.program_id(0) == 0)
    def _():
        update[0], update[1] = halves(DAMPING * jnp.concatenate([l1_ref[...], l2_ref[...]], axis=1))

    at = pl.ds(0, rank)
    y1 = fetcher([[(ups[i].at[at, :], 0, 0), (dns[i].at[at, :], 0, w)] for i in range(m)], buf, sem)
    y = halves(jnp.concatenate([y1, y_ref[0]], axis=0))
    mom_out[0] = both_ref[0] - dot3((update[0], update[1]), y)


def chunk_at(steps, n):
    def at(k, place):
        step = steps[0]
        for i in range(1, len(steps)):
            step = jnp.where(k == i, steps[i], step)
        return lax.rem(place[0] + n - step, n)

    return at


def advance(mode, place, steps, n, ups, dns, both, y, l1, l2, l2t):
    m = len(ups)
    _, rows, _ = both.shape
    rank = l1.shape[1]
    w = 2 * ups[0].shape[1]
    at = chunk_at(steps, n)
    block = pl.BlockSpec((1, rows, w), lambda k, place: (0, 0, at(k, place)))
    y_block = pl.BlockSpec((1, rank, w), lambda k, place: (k, 0, 0))
    factors = [whole((rows, rank)), whole((rows, rank))]
    projected = [jax.ShapeDtypeStruct((m, rank, w), F32), jax.ShapeDtypeStruct((8, rank), F32)]
    moment = [jax.ShapeDtypeStruct(both.shape, F32)]
    project_scratch = pltpu.VMEM((2, rank, rows), BF16)
    moment_scratch = pltpu.VMEM((2, rows, 2 * rank), BF16)
    kernel, args, specs, outs, out_specs, scratch, fetched, aliases = {
        "both": (
            advance_kernel, [both, l1, l2, l2t], [block] + factors + [whole((rank, rows))],
            moment + projected, [block, y_block, whole((8, rank))],
            [project_scratch, moment_scratch], rank + rows, {1 + 2 * m: 0},
        ),
        "project": (
            project_kernel, [l2t], [whole((rank, rows))],
            projected, [y_block, whole((8, rank))], [project_scratch], rows, {},
        ),
        "moment": (
            moment_kernel, [both, y, l1, l2], [block, y_block] + factors,
            moment, [block], [moment_scratch], rank, {1 + 2 * m: 0},
        ),
    }[mode]
    return pl.pallas_call(
        functools.partial(kernel, m),
        out_shape=outs,
        grid_spec=pltpu.PrefetchScalarGridSpec(
            num_scalar_prefetch=1,
            grid=(m,),
            in_specs=[VMEM] * (2 * m) + specs,
            out_specs=out_specs,
            scratch_shapes=[pltpu.VMEM((2, fetched, w), F32), pltpu.SemaphoreType.DMA((2, 2))] + scratch,
        ),
        input_output_aliases=aliases,
        cost_estimate=cost(m * w * 20 * rows * rank, m * w * rows * 24),
        compiler_params=grant(14),
    )(place, *ups, *dns, *args)


def weights_kernel(n, groups, rate, order_ref, *refs):
    ups, dns, ys = refs[:n], refs[n : 2 * n], refs[2 * n : 2 * n + len(groups)]
    w_ref, l1_ref, l2_ref, norm_ref, *totals, w_out, right_out, buf, sem, update = refs[2 * n + len(groups) :]
    rank = right_out.shape[1]
    w = buf.shape[2] // 2
    total = totals[0][0:1]
    for ref in totals[1:]:
        total = total + ref[0:1]
    norm = jnp.sqrt(total + EPS)

    @pl.when(pl.program_id(0) == 0)
    def _():
        left = jnp.concatenate([l1_ref[...] / norm_ref[...], l2_ref[...] / norm], axis=1)
        update[0], update[1] = halves(rate * left)

    pieces = []
    for y_ref, group in zip(ys, groups):
        for j in range(group):
            i = len(pieces)
            rows = pl.ds(0, rank)
            pieces.append([(ups[i].at[rows, :], 0, 0), (dns[i].at[rows, :], 0, w), (y_ref.at[j], rank, 0)])
    y = fetcher(pieces, buf, sem)
    w_out[...] = w_ref[...] - dot3((update[0], update[1]), halves(y))
    right_out[...] = y[rank:].T / norm


def finish(place, steps, ups, dns, ys, weights, l1, l2, norm, totals, rate):
    n = len(ups)
    rows, cols = weights.shape
    rank = l1.shape[1]
    w = cols // n
    groups = tuple(y.shape[0] for y in ys)
    at = chunk_at(steps, n)
    block = pl.BlockSpec((rows, w), lambda k, place: (0, at(k, place)))
    return pl.pallas_call(
        functools.partial(weights_kernel, n, groups, rate),
        out_shape=[
            jax.ShapeDtypeStruct((rows, cols), F32),
            jax.ShapeDtypeStruct((cols, rank), F32),
        ],
        grid_spec=pltpu.PrefetchScalarGridSpec(
            num_scalar_prefetch=1,
            grid=(n,),
            in_specs=[VMEM] * (2 * n + len(ys))
            + [block, whole((rows, rank)), whole((rows, rank)), whole((1, rank))]
            + [whole((8, rank))] * len(totals),
            out_specs=[block, pl.BlockSpec((w, rank), lambda k, place: (at(k, place), 0))],
            scratch_shapes=[
                pltpu.VMEM((2, 2 * rank, w), F32),
                pltpu.SemaphoreType.DMA((2, 3)),
                pltpu.VMEM((2, rows, 2 * rank), BF16),
            ],
        ),
        cost_estimate=cost(12 * rows * cols * rank, 32 * rows * cols),
        compiler_params=grant(28),
        name="finish",
    )(place, *ups, *dns, *ys, weights, l1, l2, norm, *totals)


def whole(shape):
    return pl.BlockSpec(shape, lambda k, order: (0,) * len(shape))


def flip(x, axis, bits):
    size = lax.axis_size(axis)
    return lax.ppermute(x, axis, [(i, i ^ bits) for i in range(size)])


def rep_masks(reps):
    return [[1, 2, 3]] + [[1 << b] for b in range(2, reps.bit_length() - 1)]


def all_sum_stages(box):
    cols = lax.axis_size("col")
    masks = rep_masks(lax.axis_size("rep"))

    def send(x, axis, partners):
        return [flip(part, axis, p) for part, p in zip(x, partners)]

    def scatter():
        parts = box.pop("parts")
        box["x"] = parts[0]
        box["pending"] = send(parts[1:], "col", range(1, cols))

    def exchange(i):
        def stage():
            x = box["x"] = alike([box["x"]] + box.pop("pending"))
            if i < len(masks):
                box["pending"] = send([x] * len(masks[i]), "rep", masks[i])
            else:
                box["pending"] = send([x] * (cols - 1), "col", range(1, cols))

        return stage

    return [scatter] + [exchange(i) for i in range(len(masks) + 1)]


def ring_shards(rate, momentum, grads, weights, right_factor):
    n, count = lax.axis_size("rep"), lax.axis_size("col")
    _, rows, _ = momentum.shape
    rank = right_factor.shape[1]
    ring = list(range(0, n, 2)) + list(range(n - 1, 0, -2))
    rep = lax.axis_index("rep")
    place = jnp.where(rep % 2 == 0, rep // 2, n - 1 - rep // 2).astype(jnp.int32)[None]
    ahead = [(ring[i], ring[(i + 1) % n]) for i in range(n)]
    back = [(b, a) for a, b in ahead]
    me = lax.axis_index("col").astype(jnp.int32)[None]

    def tie(box, *arrays):
        keys = [k for k in box if k != "pending"]
        tied = lax.optimization_barrier(([box[k] for k in keys], list(arrays)))
        box.update(zip(keys, tied[0]))
        return tied[1]

    def step(up, dn):
        up = lax.ppermute(up, "rep", ahead)
        dn = lax.ppermute(dn, "rep", back)
        return up, dn

    def first(scaled):
        def stage():
            out = orth_first(me, [box.pop("x")] + box.pop("pending"), rows, scaled)
            box["left"], box["rest"] = out[:2]
            if scaled:
                box["norm"] = out[2]

        return stage

    box = {}
    stages = all_sum_stages(box)

    def begin():
        out = combine(me, momentum, grads, right_factor, n, count)
        box["up_all"], box["dn_all"], box["both"] = out[:3]
        box["parts"] = list(out[3])

    def second():
        box["left"], box["leftt"] = orth_second(box.pop("left"), box.pop("rest"))

    work = [[begin]] + [[stage] for stage in stages] + [[first(False)], [second]]
    up, dn = lead(place, momentum, grads, n)
    for k in range(1, n):
        up, dn = step(up, dn)
        if work:
            for stage in work.pop(0):
                stage()
            (up,) = tie(box, up)
        if k < n - 1:
            up = ring_add(place, n - 1 - k, up, box["up_all"])
            dn = ring_add(place, 1 + k, dn, box["dn_all"])
    l1 = box["left"]
    both = box["both"]
    up, dn = reduced(place, up, dn, box["up_all"], box["dn_all"], l1, box["leftt"], n)

    box = {}
    mine = (up, dn)
    stages = all_sum_stages(box)

    def begin_again():
        box["parts"] = list(partial_raw(me, *mine, rank, count))

    ups, dns = [up], [dn]
    ready, ys, totals = [], [], []

    def advance_ready(last=False):
        new = [c for c in range(n) if c not in ready and c < len(ups) and (n - c) % n < len(dns)]
        ready.extend(new)
        sides = ([ups[c] for c in new], [dns[(n - c) % n] for c in new])
        factors = (l1, box["left"], box["leftt"])
        if not last:
            box["both"], y, squares = advance("both", place, new, n, *sides, box["both"], None, *factors)
            ys.append(y)
            totals.append(squares)
            return None
        y, squares = advance("project", place, new, n, *sides, box["both"], None, *factors)
        ys.append(y)
        totals.append(squares)
        total = alike_total(totals, count)
        (box["both"],) = advance("moment", place, new, n, *sides, box["both"], y, *factors)
        return total

    work = [[begin_again, stages[0]]] + [[stage] for stage in stages[1:]] + [[first(True)], [second]]
    for _ in range(1, n):
        up, dn = step(up, dn)
        if work:
            for stage in work.pop(0):
                stage()
            (up,) = tie(box, up)
        else:
            box.setdefault("both", both)
            advance_ready()
            (up,) = tie(box, up)
        ups.append(up)
        dns.append(dn)
    box.setdefault("both", both)
    total = advance_ready(last=True)
    sides = ([ups[c] for c in ready], [dns[(n - c) % n] for c in ready])
    new_weights, new_right = finish(place, ready, *sides, ys, weights, l1, box["left"], box["norm"], [total], rate)
    return new_weights, box["both"], new_right


def alike_total(totals, count):
    total = totals[0]
    for other in totals[1:]:
        total = alike([total, other])
    got = [flip(total, "col", d) for d in range(1, count)]
    return alike([total] + got)


def plain_orthonormal(left_raw):
    zero = jnp.zeros((1,), jnp.int32)
    left, rest = orth_first(zero, [left_raw], left_raw.shape[0], False)
    return orth_second(left, rest)[0]


def plain_shards(rate, momentum, grads, weights, right_factor):
    n = lax.axis_size("rep")
    moment = momentum[0]
    combined = moment + grads[0, 0].astype(F32)
    averaged, later = lax.psum((combined / n, grads[1, 0].astype(F32) / n), "rep")
    for step in range(STEPS):
        if step > 0:
            combined = moment + grads[step, 0].astype(F32)
            averaged = averaged + later
        left = plain_orthonormal(lax.psum(dot(averaged, right_factor), "col"))
        right_raw = dot(averaged, left, 0, 0)
        correction = DAMPING * dot(left, right_raw, 1, 1)
        moment = combined - correction
        averaged = averaged - correction
        totals = lax.psum(jnp.sum(right_raw * right_raw, axis=0), "col")
        right_factor = right_raw / jnp.sqrt(totals + EPS)
        weights = weights - rate * dot(left, right_factor, 1, 1)
    return weights, moment[None], right_factor


def solution(mesh):
    def body(momentum, grads, weights, right_factor):
        rep, col = mesh.shape["rep"], mesh.shape["col"]
        _, rows, cols = momentum.shape
        rank = right_factor.shape[1]
        rate = RATE * math.sqrt(rows * cols / rank)
        powers = rep & (rep - 1) == 0 and col & (col - 1) == 0 and col > 1
        fits = cols % (2 * LANES * rep * col) == 0 and rows % (8 * col) == 0
        ring = powers and 4 < rep <= 16 and col <= 8 and fits

        def shards(*args):
            return (ring_shards if ring else plain_shards)(rate, *args)

        step = jax.shard_map(
            shards,
            mesh=mesh,
            in_specs=(
                P("rep", None, "col"),
                P(None, "rep", None, "col"),
                P(None, "col"),
                P("col", None),
            ),
            out_specs=(P(None, "col"), P("rep", None, "col"), P("col", None)),
            check_vma=False,
        )
        return step(momentum, grads, weights, right_factor)

    return body
```

```python
import functools
import math

import jax
import jax.numpy as jnp
from jax import lax
from jax.experimental import pallas as pl
from jax.experimental.pallas import tpu as pltpu
from jax.sharding import PartitionSpec as P


STEPS = 2
DAMPING = 0.1
RATE = 0.2
EPS = 1e-06
LANES = 128
GROUP = 8

precise = lax.Precision.HIGHEST
VMEM = pl.BlockSpec(memory_space=pltpu.VMEM)
SMEM = pl.BlockSpec(memory_space=pltpu.SMEM)
F32 = jnp.float32
BF16 = jnp.bfloat16


def dot(a, b, ca=1, cb=0):
    return lax.dot_general(
        a, b, (((ca,), (cb,)), ((), ())), precision=precise, preferred_element_type=F32
    )


def halves(x):
    high = x.astype(BF16)
    return high, (x - high.astype(F32)).astype(BF16)


def stacked(x):
    return jnp.concatenate(halves(x), axis=0)


def dot3(a, b):
    m = a.shape[0] // 2
    top = jnp.dot(a, b[0], preferred_element_type=F32)
    return top[:m] + (top[m:] + jnp.dot(a[:m], b[1], preferred_element_type=F32))


def grant(mib):
    return pltpu.CompilerParams(vmem_limit_bytes=mib << 20)


def cost(flops, moved):
    return pl.CostEstimate(flops=int(flops), bytes_accessed=int(moved), transcendentals=0)


def eliminate(rows, group):
    count, n = len(rows), len(rows) * 8
    lane = lax.broadcasted_iota(jnp.int32, (8, n), 1)
    sub = lax.broadcasted_iota(jnp.int32, (8, n), 0)
    rows = list(rows)
    for j in range(0, n, group):
        rb, s = j // 8, j % 8

        def across(x, k):
            return jnp.broadcast_to(x[:, k : k + 1], (8, n))

        def down(x, k):
            return jnp.broadcast_to(x[k : k + 1, :], (8, n))

        column = [{i: across(rows[i], j + k) for i in range(rb, count)} for k in range(group)]
        unit = [[None] * group for _ in range(group)]
        scaled = [[None] * group for _ in range(group)]
        inverse = [None] * group
        for a in range(group):
            for b in range(a + 1):
                v = down(column[b][rb], s + a)
                for e in range(b):
                    v = v - unit[a][e] * scaled[b][e]
                scaled[a][b] = v
                if b < a:
                    unit[a][b] = v * inverse[b]
            inverse[a] = 1.0 / scaled[a][a]
        inside = (lane >= j) & (lane < j + group)
        pivot_rows = []
        for k in range(group):
            r = jnp.where(lane == j + k, 1.0, jnp.where(inside, 0.0, down(rows[rb], s + k)))
            for e in range(k):
                r = r - unit[k][e] * pivot_rows[e]
            pivot_rows.append(r)
        for i in range(rb, count):
            if i == rb and s + group == 8 and s == 0:
                out = rows[i]
                for k in range(group):
                    r = jnp.where(lane == j + k, scaled[k][k], pivot_rows[k])
                    out = jnp.where(sub == k, r, out)
                rows[i] = out
                continue
            left = []
            for k in range(group):
                v = column[k][i]
                for e in range(k):
                    v = v - unit[k][e] * left[e]
                left.append(v)
            y = jnp.where(inside, 0.0, rows[i])
            for k in range(group):
                m = left[k] * inverse[k]
                if i == rb:
                    m = jnp.where(sub > s + k, m, 0.0)
                y = y - m * pivot_rows[k]
            if i == rb:
                out = jnp.where(sub < s, rows[i], y)
                for k in range(group):
                    r = jnp.where(lane == j + k, scaled[k][k], pivot_rows[k])
                    out = jnp.where(sub == s + k, r, out)
                y = out
            rows[i] = y
    return rows


def inverse_factor(matrix):
    n = matrix.shape[0]
    rows = eliminate([matrix[8 * i : 8 * i + 8, :] for i in range(n // 8)], GROUP)
    rows = jnp.concatenate(rows, axis=0)
    lane = lax.broadcasted_iota(jnp.int32, (n, n), 1)
    sub = lax.broadcasted_iota(jnp.int32, (n, n), 0)
    pivots = jnp.sum(jnp.where(lane == sub, rows, 0.0), axis=1, keepdims=True)
    unit = jnp.where(lane < sub, rows, jnp.where(lane == sub, 1.0, 0.0))
    return unit / jnp.sqrt(pivots)


def orthonormal_blocks(blocks):
    out = []
    for block in blocks:
        for q in out:
            block = block - dot(q, dot(q, block, 0, 0))
        out.append(dot(block, inverse_factor(dot(block, block, 0, 0)), 1, 1))
    return out


def column_blocks(x):
    return [x[:, i : i + LANES] for i in range(0, x.shape[1], LANES)]


def first_kernel(scaled, me_ref, *refs):
    count = len(refs) - 3 - scaled
    parts, (left_ref, rest_ref), raw = refs[:count], refs[count : count + 2], refs[-1]
    rows = raw.shape[0] // count
    for d in range(count):
        at = pl.multiple_of((me_ref[0] ^ d) * rows, 8)
        raw[pl.ds(at, rows), :] = parts[d][:rows]
    left_raw = raw[...]
    if scaled:
        norm = jnp.sqrt(parts[0][rows : rows + 1] + EPS)
        refs[count + 2][...] = norm
        left_raw = left_raw / norm
    blocks = column_blocks(left_raw)
    middle = len(blocks) // 2
    done = orthonormal_blocks(blocks[:middle])
    left_ref[...] = jnp.concatenate(done, axis=1)
    rest = blocks[middle:]
    for q in done:
        rest = [block - dot(q, dot(q, block, 0, 0)) for block in rest]
    rest_ref[...] = jnp.concatenate(rest, axis=1)


def second_kernel(left_ref, rest_ref, out_ref, outt_ref):
    done = orthonormal_blocks(column_blocks(rest_ref[...]))
    left = jnp.concatenate([left_ref[...]] + done, axis=1)
    out_ref[...] = left
    outt_ref[...] = left.T


def orth_first(me, parts, rows, scaled):
    rank = parts[0].shape[1]
    part = jax.ShapeDtypeStruct((rows, rank // 2), F32)
    shapes = [part, part] + [jax.ShapeDtypeStruct((1, rank), F32)] * scaled
    return pl.pallas_call(
        functools.partial(first_kernel, scaled),
        out_shape=shapes,
        in_specs=[SMEM] + [VMEM] * len(parts),
        out_specs=[VMEM] * len(shapes),
        scratch_shapes=[pltpu.VMEM((rows, rank), F32)],
        cost_estimate=cost(6e9, 1e6),
        compiler_params=grant(12),
        name="orth_first",
    )(me, *parts)


def orth_second(left, rest):
    rows, rank = left.shape[0], left.shape[1] + rest.shape[1]
    return pl.pallas_call(
        second_kernel,
        out_shape=[
            jax.ShapeDtypeStruct((rows, rank), F32),
            jax.ShapeDtypeStruct((rank, rows), F32),
        ],
        in_specs=[VMEM] * 2,
        out_specs=[VMEM] * 2,
        cost_estimate=cost(6e9, 1e6),
        compiler_params=grant(12),
        name="orth_second",
    )(left, rest)


def chunk_rows(mom, grads):
    return jnp.concatenate([mom[0] + grads[0, 0].astype(F32), grads[1, 0].astype(F32)], axis=0)


def lead_kernel(n, place_ref, mom, grads, up_ref, dn_ref, mom_buf, grads_buf, sem):
    w = up_ref.shape[1]
    copies = []
    for side, offset in enumerate((n - 1, 1)):
        chunk = lax.rem(place_ref[0] + offset, n)
        at = pl.ds(pl.multiple_of((2 * chunk + side) * w, w), w)
        copies.append(
            (
                pltpu.make_async_copy(mom.at[:, :, at], mom_buf.at[side], sem.at[side, 0]),
                pltpu.make_async_copy(grads.at[:, :, :, at], grads_buf.at[side], sem.at[side, 1]),
            )
        )
    for pair in copies:
        for copy in pair:
            copy.start()
    for side, ref in enumerate((up_ref, dn_ref)):
        for copy in copies[side]:
            copy.wait()
        ref[...] = chunk_rows(mom_buf[side], grads_buf[side])


def lead(place, momentum, grads, n):
    _, rows, cols = momentum.shape
    w = cols // n // 2
    part = jax.ShapeDtypeStruct((2 * rows, w), F32)
    return pl.pallas_call(
        functools.partial(lead_kernel, n),
        out_shape=[part, part],
        in_specs=[SMEM, pl.BlockSpec(memory_space=pltpu.HBM), pl.BlockSpec(memory_space=pltpu.HBM)],
        out_specs=[VMEM] * 2,
        scratch_shapes=[
            pltpu.VMEM((2, 1, rows, w), F32),
            pltpu.VMEM((2, 2, 1, rows, w), BF16),
            pltpu.SemaphoreType.DMA((2, 2)),
        ],
        cost_estimate=cost(4 * rows * w, 32 * rows * w),
        compiler_params=grant(58),
        name="lead",
    )(place, momentum, grads)


def combine_kernel(count, inv, me_ref, mom_ref, grads_ref, right_ref, up_ref, dn_ref, both_ref, *refs):
    parts, acc_ref = refs[:count], refs[count]
    k = pl.program_id(0)
    rows = mom_ref.shape[1]
    chunks, _, w = up_ref.shape
    total = mom_ref[0] + grads_ref[0, 0].astype(F32)
    later = grads_ref[1, 0].astype(F32)
    both_ref[0] = total + later
    for c in range(chunks):
        for side, ref in enumerate((up_ref, dn_ref)):
            at = (2 * c + side) * w
            ref[c, :rows] = total[:, at : at + w]
            ref[c, rows:] = later[:, at : at + w]
    part = dot(total, right_ref[...])

    @pl.when(k == 0)
    def _():
        acc_ref[...] = part

    @pl.when(k > 0)
    def _():
        acc_ref[...] += part

    @pl.when(k == pl.num_programs(0) - 1)
    def _():
        acc_ref[...] *= inv
        block = rows // count
        for d in range(count):
            at = pl.multiple_of((me_ref[0] ^ d) * block, 8)
            parts[d][...] = acc_ref[pl.ds(at, block), :]


def combine(me, momentum, grads, right_factor, n, count):
    _, rows, cols = momentum.shape
    rank = right_factor.shape[1]
    steps = n // 2
    w = cols // steps
    chunks = jax.ShapeDtypeStruct((n, 2 * rows, w // 4), F32)
    part = jax.ShapeDtypeStruct((rows // count, rank), F32)
    out = pl.pallas_call(
        functools.partial(combine_kernel, count, 1.0 / n),
        out_shape=[chunks, chunks, jax.ShapeDtypeStruct((1, rows, cols), F32)] + [part] * count,
        grid=(steps,),
        in_specs=[
            SMEM,
            pl.BlockSpec((1, rows, w), lambda k: (0, 0, k)),
            pl.BlockSpec((2, 1, rows, w), lambda k: (0, 0, 0, k)),
            pl.BlockSpec((w, rank), lambda k: (k, 0)),
        ],
        out_specs=[
            pl.BlockSpec((2, 2 * rows, w // 4), lambda k: (k, 0, 0)),
            pl.BlockSpec((2, 2 * rows, w // 4), lambda k: (k, 0, 0)),
            pl.BlockSpec((1, rows, w), lambda k: (0, 0, k)),
        ]
        + [pl.BlockSpec((rows // count, rank), lambda k: (0, 0))] * count,
        scratch_shapes=[pltpu.VMEM((rows, rank), F32)],
        cost_estimate=cost(12 * rows * cols * rank, 28 * rows * cols),
        compiler_params=grant(47),
        name="combine",
    )(me, momentum, grads, right_factor)
    return out[0], out[1], out[2], out[3:]


def ring_add_kernel(place_ref, x_ref, chunks_ref, out_ref):
    out_ref[...] = x_ref[...] + chunks_ref[0]


def ring_add(place, offset, x, chunks):
    n = chunks.shape[0]
    return pl.pallas_call(
        ring_add_kernel,
        out_shape=jax.ShapeDtypeStruct(x.shape, F32),
        grid_spec=pltpu.PrefetchScalarGridSpec(
            num_scalar_prefetch=1,
            grid=(1,),
            in_specs=[
                whole(x.shape),
                pl.BlockSpec((1,) + x.shape, lambda i, place: (lax.rem(place[0] + offset, n), 0, 0)),
            ],
            out_specs=whole(x.shape),
        ),
        cost_estimate=cost(x.size, 12 * x.size),
        compiler_params=grant(6),
        name="ring_add",
    )(place, x, chunks)


def alike_kernel(*refs):
    terms = [ref[...] for ref in refs[:-1]]
    while len(terms) > 1:
        terms = [a + b for a, b in zip(terms[::2], terms[1::2])]
    refs[-1][...] = terms[0]


def alike(terms):
    return pl.pallas_call(
        alike_kernel,
        out_shape=jax.ShapeDtypeStruct(terms[0].shape, F32),
        in_specs=[VMEM] * len(terms),
        out_specs=VMEM,
        cost_estimate=cost(len(terms) * terms[0].size, 4 * (len(terms) + 1) * terms[0].size),
        compiler_params=grant(4),
        name="alike",
    )(*terms)


def reduced_kernel(inv, at_ref, up_ref, dn_ref, up_all, dn_all, left_ref, leftt_ref, up_out, dn_out):
    rows, rank = left_ref.shape
    w = up_ref.shape[1]
    up, dn = up_ref[...] + up_all[0], dn_ref[...] + dn_all[0]
    mean = jnp.concatenate([up, dn], axis=1) * inv
    averaged, later = mean[:rows], mean[rows:]
    right = dot(leftt_ref[...], averaged)
    averaged = averaged - DAMPING * dot(left_ref[...], right) + later
    up_out[:rank] = right[:, :w]
    dn_out[:rank] = right[:, w:]
    up_out[rank:] = averaged[:, :w]
    dn_out[rank:] = averaged[:, w:]


def reduced(place, up, dn, up_all, dn_all, left, leftt, n):
    rows, rank = left.shape
    w = up.shape[1]
    ring = jax.ShapeDtypeStruct((rank + rows, w), F32)
    mine = pl.BlockSpec((1, 2 * rows, w), lambda i, at: (at[0], 0, 0))
    return pl.pallas_call(
        functools.partial(reduced_kernel, 1.0 / n),
        out_shape=[ring, ring],
        grid_spec=pltpu.PrefetchScalarGridSpec(
            num_scalar_prefetch=1,
            grid=(1,),
            in_specs=[whole(up.shape), whole(dn.shape), mine, mine, whole((rows, rank)), whole((rank, rows))],
            out_specs=[whole(ring.shape)] * 2,
        ),
        cost_estimate=cost(24 * rows * rank * rank, 4e6),
        compiler_params=grant(12),
        name="reduced",
    )(place, up, dn, up_all, dn_all, left, leftt)


def partial_kernel(rank, me_ref, up_ref, dn_ref, *refs):
    parts, scratch = refs[:-1], refs[-1]
    rows = up_ref.shape[0] - rank
    both = jnp.concatenate([up_ref[...], dn_ref[...]], axis=1)
    right, averaged = both[:rank], both[rank:]
    scratch[...] = dot(averaged, right, 1, 1)
    squares = dot(jnp.ones((8, both.shape[1]), F32), right * right, 1, 1)
    block = rows // len(parts)
    for d, ref in enumerate(parts):
        at = pl.multiple_of((me_ref[0] ^ d) * block, 8)
        ref[:block] = scratch[pl.ds(at, block), :]
        ref[block:] = squares


def partial_raw(me, up, dn, rank, count):
    rows = up.shape[0] - rank
    part = jax.ShapeDtypeStruct((rows // count + 8, rank), F32)
    return pl.pallas_call(
        functools.partial(partial_kernel, rank),
        out_shape=[part] * count,
        in_specs=[SMEM] + [VMEM] * 2,
        out_specs=[VMEM] * count,
        scratch_shapes=[pltpu.VMEM((rows, rank), F32)],
        cost_estimate=cost(12 * rows * rank * rank, 2e6),
        compiler_params=grant(8),
        name="partial",
    )(me, up, dn)


def fetcher(pieces, buf, sem):
    k = pl.program_id(0)

    def copies(i, slot):
        out = []
        for j, (ref, row, col) in enumerate(pieces[i]):
            at = buf.at[slot, pl.ds(row, ref.shape[0]), pl.ds(col, ref.shape[1])]
            out.append(pltpu.make_async_copy(ref, at, sem.at[slot, j]))
        return out

    @pl.when(k == 0)
    def _():
        for c in copies(0, 0):
            c.start()

    for i in range(1, len(pieces)):

        @pl.when(k == i - 1)
        def _():
            for c in copies(i, i % 2):
                c.start()

    slot = lax.rem(k, 2)
    for c in copies(0, slot):
        c.wait()
    return buf[slot]


def advance_kernel(m, order_ref, *refs):
    ups, dns = refs[:m], refs[m : 2 * m]
    both_ref, l1_ref, l2_ref, l2t_ref, mom_out, y_out, sq_out, buf, sem, project, update, acc = refs[2 * m :]
    k = pl.program_id(0)
    rank = l2t_ref.shape[0]
    w = buf.shape[2] // 2

    @pl.when(k == 0)
    def _():
        project[...] = stacked(l2t_ref[...])
        update[...] = stacked(DAMPING * jnp.concatenate([l1_ref[...], l2_ref[...]], axis=1))

    chunk = fetcher([[(ups[i], 0, 0), (dns[i], 0, w)] for i in range(m)], buf, sem)
    y1, averaged = chunk[:rank], chunk[rank:]
    y2 = dot3(project[...], halves(averaged))
    y_out[0] = y2
    y = halves(jnp.concatenate([y1, y2], axis=0))
    mom_out[0] = both_ref[0] - dot3(update[...], y)
    add_squares(k, m, y2, acc, sq_out)


def add_squares(k, m, y, acc, out):
    ones = jnp.ones((y.shape[1], LANES), BF16)
    high, low = [jnp.dot(part, ones, preferred_element_type=F32) for part in halves(y * y)]

    @pl.when(k == 0)
    def _():
        acc[...] = high + low

    @pl.when(k > 0)
    def _():
        acc[...] += high + low

    @pl.when(k == m - 1)
    def _():
        out[...] = acc[...].T[:8]


def project_kernel(m, order_ref, *refs):
    ups, dns = refs[:m], refs[m : 2 * m]
    l2t_ref, y_out, sq_out, buf, sem, project, acc = refs[2 * m :]
    k = pl.program_id(0)
    rank, rows = l2t_ref.shape
    w = buf.shape[2] // 2

    @pl.when(k == 0)
    def _():
        project[...] = stacked(l2t_ref[...])

    at = pl.ds(rank, rows)
    averaged = fetcher([[(ups[i].at[at, :], 0, 0), (dns[i].at[at, :], 0, w)] for i in range(m)], buf, sem)
    y2 = dot3(project[...], halves(averaged))
    y_out[0] = y2
    add_squares(k, m, y2, acc, sq_out)


def moment_kernel(m, order_ref, *refs):
    ups, dns = refs[:m], refs[m : 2 * m]
    both_ref, y_ref, l1_ref, l2_ref, mom_out, buf, sem, update = refs[2 * m :]
    rank = y_ref.shape[1]
    w = buf.shape[2] // 2

    @pl.when(pl.program_id(0) == 0)
    def _():
        update[...] = stacked(DAMPING * jnp.concatenate([l1_ref[...], l2_ref[...]], axis=1))

    at = pl.ds(0, rank)
    y1 = fetcher([[(ups[i].at[at, :], 0, 0), (dns[i].at[at, :], 0, w)] for i in range(m)], buf, sem)
    y = halves(jnp.concatenate([y1, y_ref[0]], axis=0))
    mom_out[0] = both_ref[0] - dot3(update[...], y)


def chunk_at(steps, n):
    def at(k, place):
        step = steps[0]
        for i in range(1, len(steps)):
            step = jnp.where(k == i, steps[i], step)
        return lax.rem(place[0] + n - step, n)

    return at


def advance(mode, place, steps, n, ups, dns, both, y, l1, l2, l2t):
    m = len(ups)
    _, rows, _ = both.shape
    rank = l1.shape[1]
    w = 2 * ups[0].shape[1]
    at = chunk_at(steps, n)
    block = pl.BlockSpec((1, rows, w), lambda k, place: (0, 0, at(k, place)))
    y_block = pl.BlockSpec((1, rank, w), lambda k, place: (k, 0, 0))
    factors = [whole((rows, rank)), whole((rows, rank))]
    projected = [jax.ShapeDtypeStruct((m, rank, w), F32), jax.ShapeDtypeStruct((8, rank), F32)]
    moment = [jax.ShapeDtypeStruct(both.shape, F32)]
    project_scratch = pltpu.VMEM((2 * rank, rows), BF16)
    squares_scratch = pltpu.VMEM((rank, LANES), F32)
    moment_scratch = pltpu.VMEM((2 * rows, 2 * rank), BF16)
    kernel, args, specs, outs, out_specs, scratch, fetched, aliases = {
        "both": (
            advance_kernel, [both, l1, l2, l2t], [block] + factors + [whole((rank, rows))],
            moment + projected, [block, y_block, whole((8, rank))],
            [project_scratch, moment_scratch, squares_scratch], rank + rows, {1 + 2 * m: 0},
        ),
        "project": (
            project_kernel, [l2t], [whole((rank, rows))],
            projected, [y_block, whole((8, rank))], [project_scratch, squares_scratch], rows, {},
        ),
        "moment": (
            moment_kernel, [both, y, l1, l2], [block, y_block] + factors,
            moment, [block], [moment_scratch], rank, {1 + 2 * m: 0},
        ),
    }[mode]
    return pl.pallas_call(
        functools.partial(kernel, m),
        out_shape=outs,
        grid_spec=pltpu.PrefetchScalarGridSpec(
            num_scalar_prefetch=1,
            grid=(m,),
            in_specs=[VMEM] * (2 * m) + specs,
            out_specs=out_specs,
            scratch_shapes=[pltpu.VMEM((2, fetched, w), F32), pltpu.SemaphoreType.DMA((2, 2))] + scratch,
        ),
        input_output_aliases=aliases,
        cost_estimate=cost(m * w * 20 * rows * rank, m * w * rows * 24),
        compiler_params=grant(14),
    )(place, *ups, *dns, *args)


def weights_kernel(n, groups, rate, order_ref, *refs):
    ups, dns, ys = refs[:n], refs[n : 2 * n], refs[2 * n : 2 * n + len(groups)]
    w_ref, l1_ref, l2_ref, norm_ref, *totals, w_out, right_out, buf, sem, update = refs[2 * n + len(groups) :]
    rank = right_out.shape[1]
    w = buf.shape[2] // 2
    total = totals[0][0:1]
    for ref in totals[1:]:
        total = total + ref[0:1]
    norm = jnp.sqrt(total + EPS)

    @pl.when(pl.program_id(0) == 0)
    def _():
        left = jnp.concatenate([l1_ref[...] / norm_ref[...], l2_ref[...] / norm], axis=1)
        update[...] = stacked(rate * left)

    pieces = []
    for y_ref, group in zip(ys, groups):
        for j in range(group):
            i = len(pieces)
            rows = pl.ds(0, rank)
            pieces.append([(ups[i].at[rows, :], 0, 0), (dns[i].at[rows, :], 0, w), (y_ref.at[j], rank, 0)])
    y = fetcher(pieces, buf, sem)
    w_out[...] = w_ref[...] - dot3(update[...], halves(y))
    right_out[...] = y[rank:].T / norm


def finish(place, steps, ups, dns, ys, weights, l1, l2, norm, totals, rate):
    n = len(ups)
    rows, cols = weights.shape
    rank = l1.shape[1]
    w = cols // n
    groups = tuple(y.shape[0] for y in ys)
    at = chunk_at(steps, n)
    block = pl.BlockSpec((rows, w), lambda k, place: (0, at(k, place)))
    return pl.pallas_call(
        functools.partial(weights_kernel, n, groups, rate),
        out_shape=[
            jax.ShapeDtypeStruct((rows, cols), F32),
            jax.ShapeDtypeStruct((cols, rank), F32),
        ],
        grid_spec=pltpu.PrefetchScalarGridSpec(
            num_scalar_prefetch=1,
            grid=(n,),
            in_specs=[VMEM] * (2 * n + len(ys))
            + [block, whole((rows, rank)), whole((rows, rank)), whole((1, rank))]
            + [whole((8, rank))] * len(totals),
            out_specs=[block, pl.BlockSpec((w, rank), lambda k, place: (at(k, place), 0))],
            scratch_shapes=[
                pltpu.VMEM((2, 2 * rank, w), F32),
                pltpu.SemaphoreType.DMA((2, 3)),
                pltpu.VMEM((2 * rows, 2 * rank), BF16),
            ],
        ),
        cost_estimate=cost(12 * rows * cols * rank, 32 * rows * cols),
        compiler_params=grant(28),
        name="finish",
    )(place, *ups, *dns, *ys, weights, l1, l2, norm, *totals)


def whole(shape):
    return pl.BlockSpec(shape, lambda k, order: (0,) * len(shape))


def flip(x, axis, bits):
    size = lax.axis_size(axis)
    return lax.ppermute(x, axis, [(i, i ^ bits) for i in range(size)])


def rep_masks(reps):
    return [[1, 2, 3]] + [[1 << b] for b in range(2, reps.bit_length() - 1)]


def all_sum_stages(box):
    cols = lax.axis_size("col")
    masks = rep_masks(lax.axis_size("rep"))

    def send(x, axis, partners):
        return [flip(part, axis, p) for part, p in zip(x, partners)]

    def scatter():
        parts = box.pop("parts")
        box["x"] = parts[0]
        box["pending"] = send(parts[1:], "col", range(1, cols))

    def exchange(i):
        def stage():
            x = box["x"] = alike([box["x"]] + box.pop("pending"))
            if i < len(masks):
                box["pending"] = send([x] * len(masks[i]), "rep", masks[i])
            else:
                box["pending"] = send([x] * (cols - 1), "col", range(1, cols))

        return stage

    return [scatter] + [exchange(i) for i in range(len(masks) + 1)]


def ring_shards(rate, momentum, grads, weights, right_factor):
    n, count = lax.axis_size("rep"), lax.axis_size("col")
    _, rows, _ = momentum.shape
    rank = right_factor.shape[1]
    ring = list(range(0, n, 2)) + list(range(n - 1, 0, -2))
    rep = lax.axis_index("rep")
    place = jnp.where(rep % 2 == 0, rep // 2, n - 1 - rep // 2).astype(jnp.int32)[None]
    ahead = [(ring[i], ring[(i + 1) % n]) for i in range(n)]
    back = [(b, a) for a, b in ahead]
    me = lax.axis_index("col").astype(jnp.int32)[None]

    def tie(box, *arrays):
        keys = [k for k in box if k != "pending"]
        tied = lax.optimization_barrier(([box[k] for k in keys], list(arrays)))
        box.update(zip(keys, tied[0]))
        return tied[1]

    def step(up, dn):
        up = lax.ppermute(up, "rep", ahead)
        dn = lax.ppermute(dn, "rep", back)
        return up, dn

    def first(scaled):
        def stage():
            out = orth_first(me, [box.pop("x")] + box.pop("pending"), rows, scaled)
            box["left"], box["rest"] = out[:2]
            if scaled:
                box["norm"] = out[2]

        return stage

    box = {}
    stages = all_sum_stages(box)

    def begin():
        out = combine(me, momentum, grads, right_factor, n, count)
        box["up_all"], box["dn_all"], box["both"] = out[:3]
        box["parts"] = list(out[3])

    def second():
        box["left"], box["leftt"] = orth_second(box.pop("left"), box.pop("rest"))

    work = [[begin]] + [[stage] for stage in stages] + [[first(False)], [second]]
    up, dn = lead(place, momentum, grads, n)
    for k in range(1, n):
        up, dn = step(up, dn)
        if work:
            for stage in work.pop(0):
                stage()
            (up,) = tie(box, up)
        if k < n - 1:
            up = ring_add(place, n - 1 - k, up, box["up_all"])
            dn = ring_add(place, 1 + k, dn, box["dn_all"])
    l1 = box["left"]
    both = box["both"]
    up, dn = reduced(place, up, dn, box["up_all"], box["dn_all"], l1, box["leftt"], n)

    box = {}
    mine = (up, dn)
    stages = all_sum_stages(box)

    def begin_again():
        box["parts"] = list(partial_raw(me, *mine, rank, count))

    ups, dns = [up], [dn]
    ready, ys, totals = [], [], []

    def advance_ready(last=False):
        new = [c for c in range(n) if c not in ready and c < len(ups) and (n - c) % n < len(dns)]
        ready.extend(new)
        sides = ([ups[c] for c in new], [dns[(n - c) % n] for c in new])
        factors = (l1, box["left"], box["leftt"])
        if not last:
            box["both"], y, squares = advance("both", place, new, n, *sides, box["both"], None, *factors)
            ys.append(y)
            totals.append(squares)
            return None
        y, squares = advance("project", place, new, n, *sides, box["both"], None, *factors)
        ys.append(y)
        totals.append(squares)
        total = alike_total(totals, count)
        (box["both"],) = advance("moment", place, new, n, *sides, box["both"], y, *factors)
        return total

    work = [[begin_again, stages[0]]] + [[stage] for stage in stages[1:]] + [[first(True)], [second]]
    for _ in range(1, n):
        up, dn = step(up, dn)
        if work:
            for stage in work.pop(0):
                stage()
            (up,) = tie(box, up)
        else:
            box.setdefault("both", both)
            advance_ready()
            (up,) = tie(box, up)
        ups.append(up)
        dns.append(dn)
    box.setdefault("both", both)
    total = advance_ready(last=True)
    sides = ([ups[c] for c in ready], [dns[(n - c) % n] for c in ready])
    new_weights, new_right = finish(place, ready, *sides, ys, weights, l1, box["left"], box["norm"], [total], rate)
    return new_weights, box["both"], new_right


def alike_total(totals, count):
    total = totals[0]
    for other in totals[1:]:
        total = alike([total, other])
    got = [flip(total, "col", d) for d in range(1, count)]
    return alike([total] + got)


def plain_orthonormal(left_raw):
    zero = jnp.zeros((1,), jnp.int32)
    left, rest = orth_first(zero, [left_raw], left_raw.shape[0], False)
    return orth_second(left, rest)[0]


def plain_shards(rate, momentum, grads, weights, right_factor):
    n = lax.axis_size("rep")
    moment = momentum[0]
    combined = moment + grads[0, 0].astype(F32)
    averaged, later = lax.psum((combined / n, grads[1, 0].astype(F32) / n), "rep")
    for step in range(STEPS):
        if step > 0:
            combined = moment + grads[step, 0].astype(F32)
            averaged = averaged + later
        left = plain_orthonormal(lax.psum(dot(averaged, right_factor), "col"))
        right_raw = dot(averaged, left, 0, 0)
        correction = DAMPING * dot(left, right_raw, 1, 1)
        moment = combined - correction
        averaged = averaged - correction
        totals = lax.psum(jnp.sum(right_raw * right_raw, axis=0), "col")
        right_factor = right_raw / jnp.sqrt(totals + EPS)
        weights = weights - rate * dot(left, right_factor, 1, 1)
    return weights, moment[None], right_factor


def solution(mesh):
    def body(momentum, grads, weights, right_factor):
        rep, col = mesh.shape["rep"], mesh.shape["col"]
        _, rows, cols = momentum.shape
        rank = right_factor.shape[1]
        rate = RATE * math.sqrt(rows * cols / rank)
        powers = rep & (rep - 1) == 0 and col & (col - 1) == 0 and col > 1
        fits = cols % (2 * LANES * rep * col) == 0 and rows % (8 * col) == 0
        ring = powers and 4 < rep <= 16 and col <= 8 and fits

        def shards(*args):
            return (ring_shards if ring else plain_shards)(rate, *args)

        step = jax.shard_map(
            shards,
            mesh=mesh,
            in_specs=(
                P("rep", None, "col"),
                P(None, "rep", None, "col"),
                P(None, "col"),
                P("col", None),
            ),
            out_specs=(P(None, "col"), P("rep", None, "col"), P("col", None)),
            check_vma=False,
        )
        return step(momentum, grads, weights, right_factor)

    return body
```

```python
import functools
import math

import jax
import jax.numpy as jnp
from jax import lax
from jax.experimental import pallas as pl
from jax.experimental.pallas import tpu as pltpu
from jax.sharding import PartitionSpec as P


STEPS = 2
DAMPING = 0.1
RATE = 0.2
EPS = 1e-06
LANES = 128
GROUP = 8

precise = lax.Precision.HIGHEST
VMEM = pl.BlockSpec(memory_space=pltpu.VMEM)
SMEM = pl.BlockSpec(memory_space=pltpu.SMEM)
F32 = jnp.float32
BF16 = jnp.bfloat16


def dot(a, b, ca=1, cb=0):
    return lax.dot_general(
        a, b, (((ca,), (cb,)), ((), ())), precision=precise, preferred_element_type=F32
    )


def halves(x):
    high = x.astype(BF16)
    return high, (x - high.astype(F32)).astype(BF16)


def stacked(x):
    return jnp.concatenate(halves(x), axis=0)


def dot3(a, b):
    m = a.shape[0] // 2
    top = jnp.dot(a, b[0], preferred_element_type=F32)
    return top[:m] + (top[m:] + jnp.dot(a[:m], b[1], preferred_element_type=F32))


def grant(mib):
    return pltpu.CompilerParams(vmem_limit_bytes=mib << 20)


def cost(flops, moved):
    return pl.CostEstimate(flops=int(flops), bytes_accessed=int(moved), transcendentals=0)


def eliminate(rows, group):
    count, n = len(rows), len(rows) * 8
    lane = lax.broadcasted_iota(jnp.int32, (8, n), 1)
    sub = lax.broadcasted_iota(jnp.int32, (8, n), 0)
    rows = list(rows)
    for j in range(0, n, group):
        rb, s = j // 8, j % 8

        def across(x, k):
            return jnp.broadcast_to(x[:, k : k + 1], (8, n))

        def down(x, k):
            return jnp.broadcast_to(x[k : k + 1, :], (8, n))

        column = [{i: across(rows[i], j + k) for i in range(rb, count)} for k in range(group)]
        unit = [[None] * group for _ in range(group)]
        scaled = [[None] * group for _ in range(group)]
        inverse = [None] * group
        for a in range(group):
            for b in range(a + 1):
                v = down(column[b][rb], s + a)
                for e in range(b):
                    v = v - unit[a][e] * scaled[b][e]
                scaled[a][b] = v
                if b < a:
                    unit[a][b] = v * inverse[b]
            inverse[a] = 1.0 / scaled[a][a]
        inside = (lane >= j) & (lane < j + group)
        pivot_rows = []
        for k in range(group):
            r = jnp.where(lane == j + k, 1.0, jnp.where(inside, 0.0, down(rows[rb], s + k)))
            for e in range(k):
                r = r - unit[k][e] * pivot_rows[e]
            pivot_rows.append(r)
        for i in range(rb, count):
            if i == rb and s + group == 8 and s == 0:
                out = rows[i]
                for k in range(group):
                    r = jnp.where(lane == j + k, scaled[k][k], pivot_rows[k])
                    out = jnp.where(sub == k, r, out)
                rows[i] = out
                continue
            left = []
            for k in range(group):
                v = column[k][i]
                for e in range(k):
                    v = v - unit[k][e] * left[e]
                left.append(v)
            y = jnp.where(inside, 0.0, rows[i])
            for k in range(group):
                m = left[k] * inverse[k]
                if i == rb:
                    m = jnp.where(sub > s + k, m, 0.0)
                y = y - m * pivot_rows[k]
            if i == rb:
                out = jnp.where(sub < s, rows[i], y)
                for k in range(group):
                    r = jnp.where(lane == j + k, scaled[k][k], pivot_rows[k])
                    out = jnp.where(sub == s + k, r, out)
                y = out
            rows[i] = y
    return rows


def inverse_factor(matrix):
    n = matrix.shape[0]
    rows = eliminate([matrix[8 * i : 8 * i + 8, :] for i in range(n // 8)], GROUP)
    rows = jnp.concatenate(rows, axis=0)
    lane = lax.broadcasted_iota(jnp.int32, (n, n), 1)
    sub = lax.broadcasted_iota(jnp.int32, (n, n), 0)
    pivots = jnp.sum(jnp.where(lane == sub, rows, 0.0), axis=1, keepdims=True)
    unit = jnp.where(lane < sub, rows, jnp.where(lane == sub, 1.0, 0.0))
    return unit / jnp.sqrt(pivots)


def orthonormal_blocks(blocks):
    out = []
    for block in blocks:
        for q in out:
            block = block - dot(q, dot(q, block, 0, 0))
        out.append(dot(block, inverse_factor(dot(block, block, 0, 0)), 1, 1))
    return out


def column_blocks(x):
    return [x[:, i : i + LANES] for i in range(0, x.shape[1], LANES)]


def first_kernel(scaled, me_ref, *refs):
    count = len(refs) - 3 - scaled
    parts, (left_ref, rest_ref), raw = refs[:count], refs[count : count + 2], refs[-1]
    rows = raw.shape[0] // count
    for d in range(count):
        at = pl.multiple_of((me_ref[0] ^ d) * rows, 8)
        raw[pl.ds(at, rows), :] = parts[d][:rows]
    left_raw = raw[...]
    if scaled:
        norm = jnp.sqrt(parts[0][rows : rows + 1] + EPS)
        refs[count + 2][...] = norm
        left_raw = left_raw / norm
    blocks = column_blocks(left_raw)
    middle = len(blocks) // 2
    done = orthonormal_blocks(blocks[:middle])
    left_ref[...] = jnp.concatenate(done, axis=1)
    rest = blocks[middle:]
    for q in done:
        rest = [block - dot(q, dot(q, block, 0, 0)) for block in rest]
    rest_ref[...] = jnp.concatenate(rest, axis=1)


def second_kernel(left_ref, rest_ref, out_ref, outt_ref):
    done = orthonormal_blocks(column_blocks(rest_ref[...]))
    left = jnp.concatenate([left_ref[...]] + done, axis=1)
    out_ref[...] = left
    outt_ref[...] = left.T


def orth_first(me, parts, rows, scaled):
    rank = parts[0].shape[1]
    part = jax.ShapeDtypeStruct((rows, rank // 2), F32)
    shapes = [part, part] + [jax.ShapeDtypeStruct((1, rank), F32)] * scaled
    return pl.pallas_call(
        functools.partial(first_kernel, scaled),
        out_shape=shapes,
        in_specs=[SMEM] + [VMEM] * len(parts),
        out_specs=[VMEM] * len(shapes),
        scratch_shapes=[pltpu.VMEM((rows, rank), F32)],
        cost_estimate=cost(6e9, 1e6),
        compiler_params=grant(12),
        name="orth_first",
    )(me, *parts)


def orth_second(left, rest):
    rows, rank = left.shape[0], left.shape[1] + rest.shape[1]
    return pl.pallas_call(
        second_kernel,
        out_shape=[
            jax.ShapeDtypeStruct((rows, rank), F32),
            jax.ShapeDtypeStruct((rank, rows), F32),
        ],
        in_specs=[VMEM] * 2,
        out_specs=[VMEM] * 2,
        cost_estimate=cost(6e9, 1e6),
        compiler_params=grant(12),
        name="orth_second",
    )(left, rest)


def chunk_rows(mom, grads):
    return jnp.concatenate([mom[0] + grads[0, 0].astype(F32), grads[1, 0].astype(F32)], axis=0)


def lead_kernel(n, place_ref, mom, grads, up_ref, dn_ref, mom_buf, grads_buf, sem):
    w = up_ref.shape[1]
    copies = []
    for side, offset in enumerate((n - 1, 1)):
        chunk = lax.rem(place_ref[0] + offset, n)
        at = pl.ds(pl.multiple_of((2 * chunk + side) * w, w), w)
        copies.append(
            (
                pltpu.make_async_copy(mom.at[:, :, at], mom_buf.at[side], sem.at[side, 0]),
                pltpu.make_async_copy(grads.at[:, :, :, at], grads_buf.at[side], sem.at[side, 1]),
            )
        )
    for pair in copies:
        for copy in pair:
            copy.start()
    for side, ref in enumerate((up_ref, dn_ref)):
        for copy in copies[side]:
            copy.wait()
        ref[...] = chunk_rows(mom_buf[side], grads_buf[side])


def lead(place, momentum, grads, n):
    _, rows, cols = momentum.shape
    w = cols // n // 2
    part = jax.ShapeDtypeStruct((2 * rows, w), F32)
    return pl.pallas_call(
        functools.partial(lead_kernel, n),
        out_shape=[part, part],
        in_specs=[SMEM, pl.BlockSpec(memory_space=pltpu.HBM), pl.BlockSpec(memory_space=pltpu.HBM)],
        out_specs=[VMEM] * 2,
        scratch_shapes=[
            pltpu.VMEM((2, 1, rows, w), F32),
            pltpu.VMEM((2, 2, 1, rows, w), BF16),
            pltpu.SemaphoreType.DMA((2, 2)),
        ],
        cost_estimate=cost(4 * rows * w, 32 * rows * w),
        compiler_params=grant(58),
        name="lead",
    )(place, momentum, grads)


def combine_kernel(count, inv, me_ref, mom_ref, grads_ref, right_ref, up_ref, dn_ref, both_ref, *refs):
    parts, acc_ref = refs[:count], refs[count]
    k = pl.program_id(0)
    rows = mom_ref.shape[1]
    chunks, _, w = up_ref.shape
    total = mom_ref[0] + grads_ref[0, 0].astype(F32)
    later = grads_ref[1, 0].astype(F32)
    both_ref[0] = total + later
    for c in range(chunks):
        for side, ref in enumerate((up_ref, dn_ref)):
            at = (2 * c + side) * w
            ref[c, :rows] = total[:, at : at + w]
            ref[c, rows:] = later[:, at : at + w]
    part = dot(total, right_ref[...])

    @pl.when(k == 0)
    def _():
        acc_ref[...] = part

    @pl.when(k > 0)
    def _():
        acc_ref[...] += part

    @pl.when(k == pl.num_programs(0) - 1)
    def _():
        acc_ref[...] *= inv
        block = rows // count
        for d in range(count):
            at = pl.multiple_of((me_ref[0] ^ d) * block, 8)
            parts[d][...] = acc_ref[pl.ds(at, block), :]


def combine(me, momentum, grads, right_factor, n, count):
    _, rows, cols = momentum.shape
    rank = right_factor.shape[1]
    steps = n // 2
    w = cols // steps
    chunks = jax.ShapeDtypeStruct((n, 2 * rows, w // 4), F32)
    part = jax.ShapeDtypeStruct((rows // count, rank), F32)
    out = pl.pallas_call(
        functools.partial(combine_kernel, count, 1.0 / n),
        out_shape=[chunks, chunks, jax.ShapeDtypeStruct((1, rows, cols), F32)] + [part] * count,
        grid=(steps,),
        in_specs=[
            SMEM,
            pl.BlockSpec((1, rows, w), lambda k: (0, 0, k)),
            pl.BlockSpec((2, 1, rows, w), lambda k: (0, 0, 0, k)),
            pl.BlockSpec((w, rank), lambda k: (k, 0)),
        ],
        out_specs=[
            pl.BlockSpec((2, 2 * rows, w // 4), lambda k: (k, 0, 0)),
            pl.BlockSpec((2, 2 * rows, w // 4), lambda k: (k, 0, 0)),
            pl.BlockSpec((1, rows, w), lambda k: (0, 0, k)),
        ]
        + [pl.BlockSpec((rows // count, rank), lambda k: (0, 0))] * count,
        scratch_shapes=[pltpu.VMEM((rows, rank), F32)],
        cost_estimate=cost(12 * rows * cols * rank, 28 * rows * cols),
        compiler_params=grant(47),
        name="combine",
    )(me, momentum, grads, right_factor)
    return out[0], out[1], out[2], out[3:]


def ring_add_kernel(place_ref, x_ref, chunks_ref, out_ref):
    out_ref[...] = x_ref[...] + chunks_ref[0]


def ring_add(place, offset, x, chunks):
    n = chunks.shape[0]
    return pl.pallas_call(
        ring_add_kernel,
        out_shape=jax.ShapeDtypeStruct(x.shape, F32),
        grid_spec=pltpu.PrefetchScalarGridSpec(
            num_scalar_prefetch=1,
            grid=(1,),
            in_specs=[
                whole(x.shape),
                pl.BlockSpec((1,) + x.shape, lambda i, place: (lax.rem(place[0] + offset, n), 0, 0)),
            ],
            out_specs=whole(x.shape),
        ),
        cost_estimate=cost(x.size, 12 * x.size),
        compiler_params=grant(6),
        name="ring_add",
    )(place, x, chunks)


def alike_kernel(*refs):
    terms = [ref[...] for ref in refs[:-1]]
    while len(terms) > 1:
        terms = [a + b for a, b in zip(terms[::2], terms[1::2])]
    refs[-1][...] = terms[0]


def alike(terms):
    return pl.pallas_call(
        alike_kernel,
        out_shape=jax.ShapeDtypeStruct(terms[0].shape, F32),
        in_specs=[VMEM] * len(terms),
        out_specs=VMEM,
        cost_estimate=cost(len(terms) * terms[0].size, 4 * (len(terms) + 1) * terms[0].size),
        compiler_params=grant(4),
        name="alike",
    )(*terms)


def reduced_kernel(inv, at_ref, up_ref, dn_ref, up_all, dn_all, left_ref, leftt_ref, up_out, dn_out):
    rows, rank = left_ref.shape
    w = up_ref.shape[1]
    up, dn = up_ref[...] + up_all[0], dn_ref[...] + dn_all[0]
    mean = jnp.concatenate([up, dn], axis=1) * inv
    averaged, later = mean[:rows], mean[rows:]
    right = dot(leftt_ref[...], averaged)
    averaged = averaged - DAMPING * dot3(stacked(left_ref[...]), halves(right)) + later
    up_out[:rank] = right[:, :w]
    dn_out[:rank] = right[:, w:]
    up_out[rank:] = averaged[:, :w]
    dn_out[rank:] = averaged[:, w:]


def reduced(place, up, dn, up_all, dn_all, left, leftt, n):
    rows, rank = left.shape
    w = up.shape[1]
    ring = jax.ShapeDtypeStruct((rank + rows, w), F32)
    mine = pl.BlockSpec((1, 2 * rows, w), lambda i, at: (at[0], 0, 0))
    return pl.pallas_call(
        functools.partial(reduced_kernel, 1.0 / n),
        out_shape=[ring, ring],
        grid_spec=pltpu.PrefetchScalarGridSpec(
            num_scalar_prefetch=1,
            grid=(1,),
            in_specs=[whole(up.shape), whole(dn.shape), mine, mine, whole((rows, rank)), whole((rank, rows))],
            out_specs=[whole(ring.shape)] * 2,
        ),
        cost_estimate=cost(24 * rows * rank * rank, 4e6),
        compiler_params=grant(12),
        name="reduced",
    )(place, up, dn, up_all, dn_all, left, leftt)


def partial_kernel(rank, me_ref, up_ref, dn_ref, *refs):
    parts, scratch = refs[:-1], refs[-1]
    rows = up_ref.shape[0] - rank
    both = jnp.concatenate([up_ref[...], dn_ref[...]], axis=1)
    right, averaged = both[:rank], both[rank:]
    scratch[...] = dot(averaged, right, 1, 1)
    squares = dot(jnp.ones((8, both.shape[1]), F32), right * right, 1, 1)
    block = rows // len(parts)
    for d, ref in enumerate(parts):
        at = pl.multiple_of((me_ref[0] ^ d) * block, 8)
        ref[:block] = scratch[pl.ds(at, block), :]
        ref[block:] = squares


def partial_raw(me, up, dn, rank, count):
    rows = up.shape[0] - rank
    part = jax.ShapeDtypeStruct((rows // count + 8, rank), F32)
    return pl.pallas_call(
        functools.partial(partial_kernel, rank),
        out_shape=[part] * count,
        in_specs=[SMEM] + [VMEM] * 2,
        out_specs=[VMEM] * count,
        scratch_shapes=[pltpu.VMEM((rows, rank), F32)],
        cost_estimate=cost(12 * rows * rank * rank, 2e6),
        compiler_params=grant(8),
        name="partial",
    )(me, up, dn)


def fetcher(pieces, buf, sem):
    k = pl.program_id(0)

    def copies(i, slot):
        out = []
        for j, (ref, row, col) in enumerate(pieces[i]):
            at = buf.at[slot, pl.ds(row, ref.shape[0]), pl.ds(col, ref.shape[1])]
            out.append(pltpu.make_async_copy(ref, at, sem.at[slot, j]))
        return out

    @pl.when(k == 0)
    def _():
        for c in copies(0, 0):
            c.start()

    for i in range(1, len(pieces)):

        @pl.when(k == i - 1)
        def _():
            for c in copies(i, i % 2):
                c.start()

    slot = lax.rem(k, 2)
    for c in copies(0, slot):
        c.wait()
    return buf[slot]


def advance_kernel(m, order_ref, *refs):
    ups, dns = refs[:m], refs[m : 2 * m]
    both_ref, l1_ref, l2_ref, l2t_ref, *_, mom_out, y_out, sq_out, buf, sem, project, update, acc = refs[2 * m :]
    k = pl.program_id(0)
    rank = l2t_ref.shape[0]
    w = buf.shape[2] // 2

    @pl.when(k == 0)
    def _():
        project[...] = stacked(l2t_ref[...])
        update[...] = stacked(DAMPING * jnp.concatenate([l1_ref[...], l2_ref[...]], axis=1))

    chunk = fetcher([[(ups[i], 0, 0), (dns[i], 0, w)] for i in range(m)], buf, sem)
    y1, averaged = chunk[:rank], chunk[rank:]
    y2 = dot3(project[...], halves(averaged))
    y_out[0] = y2
    y = halves(jnp.concatenate([y1, y2], axis=0))
    mom_out[0] = both_ref[0] - dot3(update[...], y)
    add_squares(k, m, y2, acc, sq_out)


def add_squares(k, m, y, acc, out):
    ones = jnp.ones((y.shape[1], LANES), BF16)
    high, low = [jnp.dot(part, ones, preferred_element_type=F32) for part in halves(y * y)]

    @pl.when(k == 0)
    def _():
        acc[...] = high + low

    @pl.when(k > 0)
    def _():
        acc[...] += high + low

    @pl.when(k == m - 1)
    def _():
        out[...] = acc[...].T[:8]


def project_kernel(m, order_ref, *refs):
    ups, dns = refs[:m], refs[m : 2 * m]
    l2t_ref, y_out, sq_out, buf, sem, project, acc = refs[2 * m :]
    k = pl.program_id(0)
    rank, rows = l2t_ref.shape
    w = buf.shape[2] // 2

    @pl.when(k == 0)
    def _():
        project[...] = stacked(l2t_ref[...])

    at = pl.ds(rank, rows)
    averaged = fetcher([[(ups[i].at[at, :], 0, 0), (dns[i].at[at, :], 0, w)] for i in range(m)], buf, sem)
    y2 = dot3(project[...], halves(averaged))
    y_out[0] = y2
    add_squares(k, m, y2, acc, sq_out)


def moment_kernel(m, order_ref, *refs):
    ups, dns = refs[:m], refs[m : 2 * m]
    both_ref, y_ref, l1_ref, l2_ref, *_, mom_out, buf, sem, update = refs[2 * m :]
    rank = y_ref.shape[1]
    w = buf.shape[2] // 2

    @pl.when(pl.program_id(0) == 0)
    def _():
        update[...] = stacked(DAMPING * jnp.concatenate([l1_ref[...], l2_ref[...]], axis=1))

    at = pl.ds(0, rank)
    y1 = fetcher([[(ups[i].at[at, :], 0, 0), (dns[i].at[at, :], 0, w)] for i in range(m)], buf, sem)
    y = halves(jnp.concatenate([y1, y_ref[0]], axis=0))
    mom_out[0] = both_ref[0] - dot3(update[...], y)


def chunk_at(steps, n):
    def at(k, place):
        step = steps[0]
        for i in range(1, len(steps)):
            step = jnp.where(k == i, steps[i], step)
        return lax.rem(place[0] + n - step, n)

    return at


def advance(mode, place, steps, n, ups, dns, both, done, y, l1, l2, l2t):
    m = len(ups)
    _, rows, _ = both.shape
    rank = l1.shape[1]
    w = 2 * ups[0].shape[1]
    at = chunk_at(steps, n)
    block = pl.BlockSpec((1, rows, w), lambda k, place: (0, 0, at(k, place)))
    y_block = pl.BlockSpec((1, rank, w), lambda k, place: (k, 0, 0))
    factors = [whole((rows, rank)), whole((rows, rank))]
    projected = [jax.ShapeDtypeStruct((m, rank, w), F32), jax.ShapeDtypeStruct((8, rank), F32)]
    moment = [jax.ShapeDtypeStruct(both.shape, F32)]
    project_scratch = pltpu.VMEM((2 * rank, rows), BF16)
    squares_scratch = pltpu.VMEM((rank, LANES), F32)
    moment_scratch = pltpu.VMEM((2 * rows, 2 * rank), BF16)
    kernel, args, specs, outs, out_specs, scratch, fetched = {
        "both": (
            advance_kernel, [both, l1, l2, l2t], [block] + factors + [whole((rank, rows))],
            moment + projected, [block, y_block, whole((8, rank))],
            [project_scratch, moment_scratch, squares_scratch], rank + rows,
        ),
        "project": (
            project_kernel, [l2t], [whole((rank, rows))],
            projected, [y_block, whole((8, rank))], [project_scratch, squares_scratch], rows,
        ),
        "moment": (
            moment_kernel, [both, y, l1, l2], [block, y_block] + factors,
            moment, [block], [moment_scratch], rank,
        ),
    }[mode]
    aliases = {}
    if done is not None:
        aliases = {1 + 2 * m + len(args): 0}
        args, specs = args + [done], specs + [pl.BlockSpec(memory_space=pl.ANY)]
    return pl.pallas_call(
        functools.partial(kernel, m),
        out_shape=outs,
        grid_spec=pltpu.PrefetchScalarGridSpec(
            num_scalar_prefetch=1,
            grid=(m,),
            in_specs=[VMEM] * (2 * m) + specs,
            out_specs=out_specs,
            scratch_shapes=[pltpu.VMEM((2, fetched, w), F32), pltpu.SemaphoreType.DMA((2, 2))] + scratch,
        ),
        input_output_aliases=aliases,
        cost_estimate=cost(m * w * 20 * rows * rank, m * w * rows * 24),
        compiler_params=grant(14),
    )(place, *ups, *dns, *args)


def weights_kernel(n, groups, rate, order_ref, *refs):
    ups, dns, ys = refs[:n], refs[n : 2 * n], refs[2 * n : 2 * n + len(groups)]
    w_ref, l1_ref, l2_ref, norm_ref, *totals, w_out, right_out, buf, sem, update = refs[2 * n + len(groups) :]
    rank = right_out.shape[1]
    w = buf.shape[2] // 2
    total = totals[0][0:1]
    for ref in totals[1:]:
        total = total + ref[0:1]
    norm = jnp.sqrt(total + EPS)

    @pl.when(pl.program_id(0) == 0)
    def _():
        left = jnp.concatenate([l1_ref[...] / norm_ref[...], l2_ref[...] / norm], axis=1)
        update[...] = stacked(rate * left)

    pieces = []
    for y_ref, group in zip(ys, groups):
        for j in range(group):
            i = len(pieces)
            rows = pl.ds(0, rank)
            pieces.append([(ups[i].at[rows, :], 0, 0), (dns[i].at[rows, :], 0, w), (y_ref.at[j], rank, 0)])
    y = fetcher(pieces, buf, sem)
    w_out[...] = w_ref[...] - dot3(update[...], halves(y))
    right_out[...] = y[rank:].T / norm


def finish(place, steps, ups, dns, ys, weights, l1, l2, norm, totals, rate):
    n = len(ups)
    rows, cols = weights.shape
    rank = l1.shape[1]
    w = cols // n
    groups = tuple(y.shape[0] for y in ys)
    at = chunk_at(steps, n)
    block = pl.BlockSpec((rows, w), lambda k, place: (0, at(k, place)))
    return pl.pallas_call(
        functools.partial(weights_kernel, n, groups, rate),
        out_shape=[
            jax.ShapeDtypeStruct((rows, cols), F32),
            jax.ShapeDtypeStruct((cols, rank), F32),
        ],
        grid_spec=pltpu.PrefetchScalarGridSpec(
            num_scalar_prefetch=1,
            grid=(n,),
            in_specs=[VMEM] * (2 * n + len(ys))
            + [block, whole((rows, rank)), whole((rows, rank)), whole((1, rank))]
            + [whole((8, rank))] * len(totals),
            out_specs=[block, pl.BlockSpec((w, rank), lambda k, place: (at(k, place), 0))],
            scratch_shapes=[
                pltpu.VMEM((2, 2 * rank, w), F32),
                pltpu.SemaphoreType.DMA((2, 3)),
                pltpu.VMEM((2 * rows, 2 * rank), BF16),
            ],
        ),
        cost_estimate=cost(12 * rows * cols * rank, 32 * rows * cols),
        compiler_params=grant(28),
        name="finish",
    )(place, *ups, *dns, *ys, weights, l1, l2, norm, *totals)


def whole(shape):
    return pl.BlockSpec(shape, lambda k, order: (0,) * len(shape))


def flip(x, axis, bits):
    size = lax.axis_size(axis)
    return lax.ppermute(x, axis, [(i, i ^ bits) for i in range(size)])


def rep_masks(reps):
    return [[1, 2, 3]] + [[1 << b] for b in range(2, reps.bit_length() - 1)]


def all_sum_stages(box):
    cols = lax.axis_size("col")
    masks = rep_masks(lax.axis_size("rep"))

    def send(x, axis, partners):
        return [flip(part, axis, p) for part, p in zip(x, partners)]

    def scatter():
        parts = box.pop("parts")
        box["x"] = parts[0]
        box["pending"] = send(parts[1:], "col", range(1, cols))

    def exchange(i):
        def stage():
            x = box["x"] = alike([box["x"]] + box.pop("pending"))
            if i < len(masks):
                box["pending"] = send([x] * len(masks[i]), "rep", masks[i])
            else:
                box["pending"] = send([x] * (cols - 1), "col", range(1, cols))

        return stage

    return [scatter] + [exchange(i) for i in range(len(masks) + 1)]


def ring_shards(rate, momentum, grads, weights, right_factor):
    n, count = lax.axis_size("rep"), lax.axis_size("col")
    _, rows, _ = momentum.shape
    rank = right_factor.shape[1]
    ring = list(range(0, n, 2)) + list(range(n - 1, 0, -2))
    rep = lax.axis_index("rep")
    place = jnp.where(rep % 2 == 0, rep // 2, n - 1 - rep // 2).astype(jnp.int32)[None]
    ahead = [(ring[i], ring[(i + 1) % n]) for i in range(n)]
    back = [(b, a) for a, b in ahead]
    me = lax.axis_index("col").astype(jnp.int32)[None]

    def tie(box, *arrays):
        keys = [k for k in box if k != "pending"]
        tied = lax.optimization_barrier(([box[k] for k in keys], list(arrays)))
        box.update(zip(keys, tied[0]))
        return tied[1]

    def step(up, dn):
        up = lax.ppermute(up, "rep", ahead)
        dn = lax.ppermute(dn, "rep", back)
        return up, dn

    def first(scaled):
        def stage():
            out = orth_first(me, [box.pop("x")] + box.pop("pending"), rows, scaled)
            box["left"], box["rest"] = out[:2]
            if scaled:
                box["norm"] = out[2]

        return stage

    box = {}
    stages = all_sum_stages(box)

    def begin():
        out = combine(me, momentum, grads, right_factor, n, count)
        box["up_all"], box["dn_all"], box["both"] = out[:3]
        box["parts"] = list(out[3])

    def second():
        box["left"], box["leftt"] = orth_second(box.pop("left"), box.pop("rest"))

    work = [[begin]] + [[stage] for stage in stages] + [[first(False)], [second]]
    up, dn = lead(place, momentum, grads, n)
    for k in range(1, n):
        up, dn = step(up, dn)
        if work:
            for stage in work.pop(0):
                stage()
            (up,) = tie(box, up)
        if k < n - 1:
            up = ring_add(place, n - 1 - k, up, box["up_all"])
            dn = ring_add(place, 1 + k, dn, box["dn_all"])
    l1 = box["left"]
    both = box["both"]
    up, dn = reduced(place, up, dn, box["up_all"], box["dn_all"], l1, box["leftt"], n)

    box = {}
    mine = (up, dn)
    stages = all_sum_stages(box)

    def begin_again():
        box["parts"] = list(partial_raw(me, *mine, rank, count))

    ups, dns = [up], [dn]
    ready, ys, totals = [], [], []

    def advance_ready(last=False):
        new = [c for c in range(n) if c not in ready and c < len(ups) and (n - c) % n < len(dns)]
        ready.extend(new)
        sides = ([ups[c] for c in new], [dns[(n - c) % n] for c in new])
        factors = (l1, box["left"], box["leftt"])
        if not last:
            done = box.get("done")
            box["done"], y, squares = advance("both", place, new, n, *sides, both, done, None, *factors)
            ys.append(y)
            totals.append(squares)
            return None
        y, squares = advance("project", place, new, n, *sides, both, None, None, *factors)
        ys.append(y)
        totals.append(squares)
        total = alike_total(totals, count)
        (box["done"],) = advance("moment", place, new, n, *sides, both, box.get("done"), y, *factors)
        return total

    work = [[begin_again, stages[0]]] + [[stage] for stage in stages[1:]] + [[first(True)], [second]]
    for _ in range(1, n):
        up, dn = step(up, dn)
        if work:
            for stage in work.pop(0):
                stage()
            (up,) = tie(box, up)
        else:
            advance_ready()
            (up,) = tie(box, up)
        ups.append(up)
        dns.append(dn)
    total = advance_ready(last=True)
    sides = ([ups[c] for c in ready], [dns[(n - c) % n] for c in ready])
    new_weights, new_right = finish(place, ready, *sides, ys, weights, l1, box["left"], box["norm"], [total], rate)
    return new_weights, box["done"], new_right


def alike_total(totals, count):
    total = totals[0]
    for other in totals[1:]:
        total = alike([total, other])
    got = [flip(total, "col", d) for d in range(1, count)]
    return alike([total] + got)


def plain_orthonormal(left_raw):
    zero = jnp.zeros((1,), jnp.int32)
    left, rest = orth_first(zero, [left_raw], left_raw.shape[0], False)
    return orth_second(left, rest)[0]


def plain_shards(rate, momentum, grads, weights, right_factor):
    n = lax.axis_size("rep")
    moment = momentum[0]
    combined = moment + grads[0, 0].astype(F32)
    averaged, later = lax.psum((combined / n, grads[1, 0].astype(F32) / n), "rep")
    for step in range(STEPS):
        if step > 0:
            combined = moment + grads[step, 0].astype(F32)
            averaged = averaged + later
        left = plain_orthonormal(lax.psum(dot(averaged, right_factor), "col"))
        right_raw = dot(averaged, left, 0, 0)
        correction = DAMPING * dot(left, right_raw, 1, 1)
        moment = combined - correction
        averaged = averaged - correction
        totals = lax.psum(jnp.sum(right_raw * right_raw, axis=0), "col")
        right_factor = right_raw / jnp.sqrt(totals + EPS)
        weights = weights - rate * dot(left, right_factor, 1, 1)
    return weights, moment[None], right_factor


def solution(mesh):
    def body(momentum, grads, weights, right_factor):
        rep, col = mesh.shape["rep"], mesh.shape["col"]
        _, rows, cols = momentum.shape
        rank = right_factor.shape[1]
        rate = RATE * math.sqrt(rows * cols / rank)
        powers = rep & (rep - 1) == 0 and col & (col - 1) == 0 and col > 1
        fits = cols % (2 * LANES * rep * col) == 0 and rows % (8 * col) == 0
        ring = powers and 4 < rep <= 16 and col <= 8 and fits

        def shards(*args):
            return (ring_shards if ring else plain_shards)(rate, *args)

        step = jax.shard_map(
            shards,
            mesh=mesh,
            in_specs=(
                P("rep", None, "col"),
                P(None, "rep", None, "col"),
                P(None, "col"),
                P("col", None),
            ),
            out_specs=(P(None, "col"), P("rep", None, "col"), P("col", None)),
            check_vma=False,
        )
        return step(momentum, grads, weights, right_factor)

    return body
```

```python
import functools
import math

import jax
import jax.numpy as jnp
from jax import lax
from jax.experimental import pallas as pl
from jax.experimental.pallas import tpu as pltpu
from jax.sharding import PartitionSpec as P


STEPS = 2
DAMPING = 0.1
RATE = 0.2
EPS = 1e-06
LANES = 128
GROUP = 8

precise = lax.Precision.HIGHEST
VMEM = pl.BlockSpec(memory_space=pltpu.VMEM)
SMEM = pl.BlockSpec(memory_space=pltpu.SMEM)
F32 = jnp.float32
BF16 = jnp.bfloat16


def dot(a, b, ca=1, cb=0):
    return lax.dot_general(
        a, b, (((ca,), (cb,)), ((), ())), precision=precise, preferred_element_type=F32
    )


def halves(x):
    high = x.astype(BF16)
    return high, (x - high.astype(F32)).astype(BF16)


def stacked(x):
    return jnp.concatenate(halves(x), axis=0)


def dot3(a, b):
    m = a.shape[0] // 2
    top = jnp.dot(a, b[0], preferred_element_type=F32)
    return top[:m] + (top[m:] + jnp.dot(a[:m], b[1], preferred_element_type=F32))


def grant(mib):
    return pltpu.CompilerParams(vmem_limit_bytes=mib << 20)


def cost(flops, moved):
    return pl.CostEstimate(flops=int(flops), bytes_accessed=int(moved), transcendentals=0)


def eliminate(rows, group):
    count, n = len(rows), len(rows) * 8
    lane = lax.broadcasted_iota(jnp.int32, (8, n), 1)
    sub = lax.broadcasted_iota(jnp.int32, (8, n), 0)
    rows = list(rows)
    for j in range(0, n, group):
        rb, s = j // 8, j % 8

        def across(x, k):
            return jnp.broadcast_to(x[:, k : k + 1], (8, n))

        def down(x, k):
            return jnp.broadcast_to(x[k : k + 1, :], (8, n))

        column = [{i: across(rows[i], j + k) for i in range(rb, count)} for k in range(group)]
        unit = [[None] * group for _ in range(group)]
        scaled = [[None] * group for _ in range(group)]
        inverse = [None] * group
        for a in range(group):
            for b in range(a + 1):
                v = down(column[b][rb], s + a)
                for e in range(b):
                    v = v - unit[a][e] * scaled[b][e]
                scaled[a][b] = v
                if b < a:
                    unit[a][b] = v * inverse[b]
            inverse[a] = 1.0 / scaled[a][a]
        inside = (lane >= j) & (lane < j + group)
        pivot_rows = []
        for k in range(group):
            r = jnp.where(lane == j + k, 1.0, jnp.where(inside, 0.0, down(rows[rb], s + k)))
            for e in range(k):
                r = r - unit[k][e] * pivot_rows[e]
            pivot_rows.append(r)
        for i in range(rb, count):
            if i == rb and s + group == 8 and s == 0:
                out = rows[i]
                for k in range(group):
                    r = jnp.where(lane == j + k, scaled[k][k], pivot_rows[k])
                    out = jnp.where(sub == k, r, out)
                rows[i] = out
                continue
            left = []
            for k in range(group):
                v = column[k][i]
                for e in range(k):
                    v = v - unit[k][e] * left[e]
                left.append(v)
            y = jnp.where(inside, 0.0, rows[i])
            for k in range(group):
                m = left[k] * inverse[k]
                if i == rb:
                    m = jnp.where(sub > s + k, m, 0.0)
                y = y - m * pivot_rows[k]
            if i == rb:
                out = jnp.where(sub < s, rows[i], y)
                for k in range(group):
                    r = jnp.where(lane == j + k, scaled[k][k], pivot_rows[k])
                    out = jnp.where(sub == s + k, r, out)
                y = out
            rows[i] = y
    return rows


def inverse_factor(matrix):
    n = matrix.shape[0]
    rows = eliminate([matrix[8 * i : 8 * i + 8, :] for i in range(n // 8)], GROUP)
    rows = jnp.concatenate(rows, axis=0)
    lane = lax.broadcasted_iota(jnp.int32, (n, n), 1)
    sub = lax.broadcasted_iota(jnp.int32, (n, n), 0)
    pivots = jnp.sum(jnp.where(lane == sub, rows, 0.0), axis=1, keepdims=True)
    unit = jnp.where(lane < sub, rows, jnp.where(lane == sub, 1.0, 0.0))
    return unit / jnp.sqrt(pivots)


def orthonormal_blocks(blocks):
    out = []
    for block in blocks:
        for q in out:
            block = block - dot(q, dot(q, block, 0, 0))
        out.append(dot(block, inverse_factor(dot(block, block, 0, 0)), 1, 1))
    return out


def column_blocks(x):
    return [x[:, i : i + LANES] for i in range(0, x.shape[1], LANES)]


def first_kernel(scaled, me_ref, *refs):
    count = len(refs) - 3 - scaled
    parts, (left_ref, rest_ref), raw = refs[:count], refs[count : count + 2], refs[-1]
    rows = raw.shape[0] // count
    for d in range(count):
        at = pl.multiple_of((me_ref[0] ^ d) * rows, 8)
        raw[pl.ds(at, rows), :] = parts[d][:rows]
    left_raw = raw[...]
    if scaled:
        norm = jnp.sqrt(parts[0][rows : rows + 1] + EPS)
        refs[count + 2][...] = norm
        left_raw = left_raw / norm
    blocks = column_blocks(left_raw)
    middle = len(blocks) // 2
    done = orthonormal_blocks(blocks[:middle])
    left_ref[...] = jnp.concatenate(done, axis=1)
    rest = blocks[middle:]
    for q in done:
        rest = [block - dot(q, dot(q, block, 0, 0)) for block in rest]
    rest_ref[...] = jnp.concatenate(rest, axis=1)


def second_kernel(left_ref, rest_ref, out_ref, outt_ref):
    done = orthonormal_blocks(column_blocks(rest_ref[...]))
    left = jnp.concatenate([left_ref[...]] + done, axis=1)
    out_ref[...] = left
    outt_ref[...] = left.T


def orth_first(me, parts, rows, scaled):
    rank = parts[0].shape[1]
    part = jax.ShapeDtypeStruct((rows, rank // 2), F32)
    shapes = [part, part] + [jax.ShapeDtypeStruct((1, rank), F32)] * scaled
    return pl.pallas_call(
        functools.partial(first_kernel, scaled),
        out_shape=shapes,
        in_specs=[SMEM] + [VMEM] * len(parts),
        out_specs=[VMEM] * len(shapes),
        scratch_shapes=[pltpu.VMEM((rows, rank), F32)],
        cost_estimate=cost(6e9, 1e6),
        compiler_params=grant(12),
        name="orth_first",
    )(me, *parts)


def orth_second(left, rest):
    rows, rank = left.shape[0], left.shape[1] + rest.shape[1]
    return pl.pallas_call(
        second_kernel,
        out_shape=[
            jax.ShapeDtypeStruct((rows, rank), F32),
            jax.ShapeDtypeStruct((rank, rows), F32),
        ],
        in_specs=[VMEM] * 2,
        out_specs=[VMEM] * 2,
        cost_estimate=cost(6e9, 1e6),
        compiler_params=grant(12),
        name="orth_second",
    )(left, rest)


def chunk_rows(mom, grads):
    return jnp.concatenate([mom[0] + grads[0, 0].astype(F32), grads[1, 0].astype(F32)], axis=0)


def lead_kernel(n, place_ref, mom, grads, up_ref, dn_ref, mom_buf, grads_buf, sem):
    w = up_ref.shape[1]
    copies = []
    for side, offset in enumerate((n - 1, 1)):
        chunk = lax.rem(place_ref[0] + offset, n)
        at = pl.ds(pl.multiple_of((2 * chunk + side) * w, w), w)
        copies.append(
            (
                pltpu.make_async_copy(mom.at[:, :, at], mom_buf.at[side], sem.at[side, 0]),
                pltpu.make_async_copy(grads.at[:, :, :, at], grads_buf.at[side], sem.at[side, 1]),
            )
        )
    for pair in copies:
        for copy in pair:
            copy.start()
    for side, ref in enumerate((up_ref, dn_ref)):
        for copy in copies[side]:
            copy.wait()
        ref[...] = chunk_rows(mom_buf[side], grads_buf[side])


def lead(place, momentum, grads, n):
    _, rows, cols = momentum.shape
    w = cols // n // 2
    part = jax.ShapeDtypeStruct((2 * rows, w), F32)
    return pl.pallas_call(
        functools.partial(lead_kernel, n),
        out_shape=[part, part],
        in_specs=[SMEM, pl.BlockSpec(memory_space=pltpu.HBM), pl.BlockSpec(memory_space=pltpu.HBM)],
        out_specs=[VMEM] * 2,
        scratch_shapes=[
            pltpu.VMEM((2, 1, rows, w), F32),
            pltpu.VMEM((2, 2, 1, rows, w), BF16),
            pltpu.SemaphoreType.DMA((2, 2)),
        ],
        cost_estimate=cost(4 * rows * w, 32 * rows * w),
        compiler_params=grant(58),
        name="lead",
    )(place, momentum, grads)


def combine_kernel(count, inv, me_ref, mom_ref, grads_ref, right_ref, up_ref, dn_ref, both_ref, *refs):
    parts, acc_ref = refs[:count], refs[count]
    k = pl.program_id(0)
    rows = mom_ref.shape[1]
    chunks, _, w = up_ref.shape
    total = mom_ref[0] + grads_ref[0, 0].astype(F32)
    later = grads_ref[1, 0].astype(F32)
    both_ref[0] = total + later
    for c in range(chunks):
        for side, ref in enumerate((up_ref, dn_ref)):
            at = (2 * c + side) * w
            ref[c, :rows] = total[:, at : at + w]
            ref[c, rows:] = later[:, at : at + w]
    part = dot(total, right_ref[...])

    @pl.when(k == 0)
    def _():
        acc_ref[...] = part

    @pl.when(k > 0)
    def _():
        acc_ref[...] += part

    @pl.when(k == pl.num_programs(0) - 1)
    def _():
        acc_ref[...] *= inv
        block = rows // count
        for d in range(count):
            at = pl.multiple_of((me_ref[0] ^ d) * block, 8)
            parts[d][...] = acc_ref[pl.ds(at, block), :]


def combine(me, momentum, grads, right_factor, n, count):
    _, rows, cols = momentum.shape
    rank = right_factor.shape[1]
    steps = n // 2
    w = cols // steps
    chunks = jax.ShapeDtypeStruct((n, 2 * rows, w // 4), F32)
    part = jax.ShapeDtypeStruct((rows // count, rank), F32)
    out = pl.pallas_call(
        functools.partial(combine_kernel, count, 1.0 / n),
        out_shape=[chunks, chunks, jax.ShapeDtypeStruct((1, rows, cols), F32)] + [part] * count,
        grid=(steps,),
        in_specs=[
            SMEM,
            pl.BlockSpec((1, rows, w), lambda k: (0, 0, k)),
            pl.BlockSpec((2, 1, rows, w), lambda k: (0, 0, 0, k)),
            pl.BlockSpec((w, rank), lambda k: (k, 0)),
        ],
        out_specs=[
            pl.BlockSpec((2, 2 * rows, w // 4), lambda k: (k, 0, 0)),
            pl.BlockSpec((2, 2 * rows, w // 4), lambda k: (k, 0, 0)),
            pl.BlockSpec((1, rows, w), lambda k: (0, 0, k)),
        ]
        + [pl.BlockSpec((rows // count, rank), lambda k: (0, 0))] * count,
        scratch_shapes=[pltpu.VMEM((rows, rank), F32)],
        cost_estimate=cost(12 * rows * cols * rank, 28 * rows * cols),
        compiler_params=grant(47),
        name="combine",
    )(me, momentum, grads, right_factor)
    return out[0], out[1], out[2], out[3:]


def ring_add_kernel(place_ref, x_ref, chunks_ref, out_ref):
    out_ref[...] = x_ref[...] + chunks_ref[0]


def ring_add(place, offset, x, chunks):
    n = chunks.shape[0]
    return pl.pallas_call(
        ring_add_kernel,
        out_shape=jax.ShapeDtypeStruct(x.shape, F32),
        grid_spec=pltpu.PrefetchScalarGridSpec(
            num_scalar_prefetch=1,
            grid=(1,),
            in_specs=[
                whole(x.shape),
                pl.BlockSpec((1,) + x.shape, lambda i, place: (lax.rem(place[0] + offset, n), 0, 0)),
            ],
            out_specs=whole(x.shape),
        ),
        cost_estimate=cost(x.size, 12 * x.size),
        compiler_params=grant(6),
        name="ring_add",
    )(place, x, chunks)


def alike_kernel(*refs):
    terms = [ref[...] for ref in refs[:-1]]
    while len(terms) > 1:
        terms = [a + b for a, b in zip(terms[::2], terms[1::2])]
    refs[-1][...] = terms[0]


def alike(terms):
    return pl.pallas_call(
        alike_kernel,
        out_shape=jax.ShapeDtypeStruct(terms[0].shape, F32),
        in_specs=[VMEM] * len(terms),
        out_specs=VMEM,
        cost_estimate=cost(len(terms) * terms[0].size, 4 * (len(terms) + 1) * terms[0].size),
        compiler_params=grant(4),
        name="alike",
    )(*terms)


def reduced_kernel(inv, at_ref, up_ref, dn_ref, up_all, dn_all, left_ref, leftt_ref, up_out, dn_out):
    rows, rank = left_ref.shape
    w = up_ref.shape[1]
    up, dn = up_ref[...] + up_all[0], dn_ref[...] + dn_all[0]
    mean = jnp.concatenate([up, dn], axis=1) * inv
    averaged, later = mean[:rows], mean[rows:]
    right = dot(leftt_ref[...], averaged)
    averaged = averaged - DAMPING * dot3(stacked(left_ref[...]), halves(right)) + later
    up_out[:rank] = right[:, :w]
    dn_out[:rank] = right[:, w:]
    up_out[rank:] = averaged[:, :w]
    dn_out[rank:] = averaged[:, w:]


def reduced(place, up, dn, up_all, dn_all, left, leftt, n):
    rows, rank = left.shape
    w = up.shape[1]
    ring = jax.ShapeDtypeStruct((rank + rows, w), F32)
    mine = pl.BlockSpec((1, 2 * rows, w), lambda i, at: (at[0], 0, 0))
    return pl.pallas_call(
        functools.partial(reduced_kernel, 1.0 / n),
        out_shape=[ring, ring],
        grid_spec=pltpu.PrefetchScalarGridSpec(
            num_scalar_prefetch=1,
            grid=(1,),
            in_specs=[whole(up.shape), whole(dn.shape), mine, mine, whole((rows, rank)), whole((rank, rows))],
            out_specs=[whole(ring.shape)] * 2,
        ),
        cost_estimate=cost(24 * rows * rank * rank, 4e6),
        compiler_params=grant(12),
        name="reduced",
    )(place, up, dn, up_all, dn_all, left, leftt)


def partial_kernel(rank, me_ref, up_ref, dn_ref, *refs):
    parts, scratch = refs[:-1], refs[-1]
    rows = up_ref.shape[0] - rank
    both = jnp.concatenate([up_ref[...], dn_ref[...]], axis=1)
    right, averaged = both[:rank], both[rank:]
    scratch[...] = dot(averaged, right, 1, 1)
    squares = dot(jnp.ones((8, both.shape[1]), F32), right * right, 1, 1)
    block = rows // len(parts)
    for d, ref in enumerate(parts):
        at = pl.multiple_of((me_ref[0] ^ d) * block, 8)
        ref[:block] = scratch[pl.ds(at, block), :]
        ref[block:] = squares


def partial_raw(me, up, dn, rank, count):
    rows = up.shape[0] - rank
    part = jax.ShapeDtypeStruct((rows // count + 8, rank), F32)
    return pl.pallas_call(
        functools.partial(partial_kernel, rank),
        out_shape=[part] * count,
        in_specs=[SMEM] + [VMEM] * 2,
        out_specs=[VMEM] * count,
        scratch_shapes=[pltpu.VMEM((rows, rank), F32)],
        cost_estimate=cost(12 * rows * rank * rank, 2e6),
        compiler_params=grant(8),
        name="partial",
    )(me, up, dn)


def fetcher(pieces, buf, sem):
    k = pl.program_id(0)

    def copies(i, slot):
        out = []
        for j, (ref, row, col) in enumerate(pieces[i]):
            at = buf.at[slot, pl.ds(row, ref.shape[0]), pl.ds(col, ref.shape[1])]
            out.append(pltpu.make_async_copy(ref, at, sem.at[slot, j]))
        return out

    @pl.when(k == 0)
    def _():
        for c in copies(0, 0):
            c.start()

    for i in range(1, len(pieces)):

        @pl.when(k == i - 1)
        def _():
            for c in copies(i, i % 2):
                c.start()

    slot = lax.rem(k, 2)
    for c in copies(0, slot):
        c.wait()
    return buf[slot]


def advance_kernel(m, order_ref, *refs):
    ups, dns = refs[:m], refs[m : 2 * m]
    both_ref, l1_ref, l2_ref, l2t_ref, *_, mom_out, y_out, sq_out, buf, sem, project, update, acc = refs[2 * m :]
    k = pl.program_id(0)
    rank = l2t_ref.shape[0]
    w = buf.shape[2] // 2

    @pl.when(k == 0)
    def _():
        project[...] = stacked(l2t_ref[...])
        update[...] = stacked(DAMPING * jnp.concatenate([l1_ref[...], l2_ref[...]], axis=1))

    chunk = fetcher([[(ups[i], 0, 0), (dns[i], 0, w)] for i in range(m)], buf, sem)
    y1, averaged = chunk[:rank], chunk[rank:]
    y2 = dot3(project[...], halves(averaged))
    y_out[0] = y2
    y = halves(jnp.concatenate([y1, y2], axis=0))
    mom_out[0] = both_ref[0] - dot3(update[...], y)
    add_squares(k, m, y2, acc, sq_out)


def add_squares(k, m, y, acc, out):
    ones = jnp.ones((y.shape[1], LANES), BF16)
    high, low = [jnp.dot(part, ones, preferred_element_type=F32) for part in halves(y * y)]

    @pl.when(k == 0)
    def _():
        acc[...] = high + low

    @pl.when(k > 0)
    def _():
        acc[...] += high + low

    @pl.when(k == m - 1)
    def _():
        out[...] = acc[...].T[:8]


def project_kernel(m, order_ref, *refs):
    ups, dns = refs[:m], refs[m : 2 * m]
    l2t_ref, y_out, sq_out, buf, sem, project, acc = refs[2 * m :]
    k = pl.program_id(0)
    rank, rows = l2t_ref.shape
    w = buf.shape[2] // 2

    @pl.when(k == 0)
    def _():
        project[...] = stacked(l2t_ref[...])

    at = pl.ds(rank, rows)
    averaged = fetcher([[(ups[i].at[at, :], 0, 0), (dns[i].at[at, :], 0, w)] for i in range(m)], buf, sem)
    y2 = dot3(project[...], halves(averaged))
    y_out[0] = y2
    add_squares(k, m, y2, acc, sq_out)


def moment_kernel(m, order_ref, *refs):
    ups, dns = refs[:m], refs[m : 2 * m]
    both_ref, y_ref, l1_ref, l2_ref, *_, mom_out, buf, sem, update = refs[2 * m :]
    rank = y_ref.shape[1]
    w = buf.shape[2] // 2

    @pl.when(pl.program_id(0) == 0)
    def _():
        update[...] = stacked(DAMPING * jnp.concatenate([l1_ref[...], l2_ref[...]], axis=1))

    at = pl.ds(0, rank)
    y1 = fetcher([[(ups[i].at[at, :], 0, 0), (dns[i].at[at, :], 0, w)] for i in range(m)], buf, sem)
    y = halves(jnp.concatenate([y1, y_ref[0]], axis=0))
    mom_out[0] = both_ref[0] - dot3(update[...], y)


def chunk_at(steps, n):
    def at(k, place):
        step = steps[0]
        for i in range(1, len(steps)):
            step = jnp.where(k == i, steps[i], step)
        return lax.rem(place[0] + n - step, n)

    return at


def advance(mode, place, steps, n, ups, dns, both, done, y, l1, l2, l2t):
    m = len(ups)
    _, rows, _ = both.shape
    rank = l1.shape[1]
    w = 2 * ups[0].shape[1]
    at = chunk_at(steps, n)
    block = pl.BlockSpec((1, rows, w), lambda k, place: (0, 0, at(k, place)))
    y_block = pl.BlockSpec((1, rank, w), lambda k, place: (k, 0, 0))
    factors = [whole((rows, rank)), whole((rows, rank))]
    projected = [jax.ShapeDtypeStruct((m, rank, w), F32), jax.ShapeDtypeStruct((8, rank), F32)]
    moment = [jax.ShapeDtypeStruct(both.shape, F32)]
    project_scratch = pltpu.VMEM((2 * rank, rows), BF16)
    squares_scratch = pltpu.VMEM((rank, LANES), F32)
    moment_scratch = pltpu.VMEM((2 * rows, 2 * rank), BF16)
    kernel, args, specs, outs, out_specs, scratch, fetched = {
        "both": (
            advance_kernel, [both, l1, l2, l2t], [block] + factors + [whole((rank, rows))],
            moment + projected, [block, y_block, whole((8, rank))],
            [project_scratch, moment_scratch, squares_scratch], rank + rows,
        ),
        "project": (
            project_kernel, [l2t], [whole((rank, rows))],
            projected, [y_block, whole((8, rank))], [project_scratch, squares_scratch], rows,
        ),
        "moment": (
            moment_kernel, [both, y, l1, l2], [block, y_block] + factors,
            moment, [block], [moment_scratch], rank,
        ),
    }[mode]
    aliases = {}
    if done is not None:
        aliases = {1 + 2 * m + len(args): 0}
        args, specs = args + [done], specs + [pl.BlockSpec(memory_space=pl.ANY)]
    return pl.pallas_call(
        functools.partial(kernel, m),
        out_shape=outs,
        grid_spec=pltpu.PrefetchScalarGridSpec(
            num_scalar_prefetch=1,
            grid=(m,),
            in_specs=[VMEM] * (2 * m) + specs,
            out_specs=out_specs,
            scratch_shapes=[pltpu.VMEM((2, fetched, w), F32), pltpu.SemaphoreType.DMA((2, 2))] + scratch,
        ),
        input_output_aliases=aliases,
        cost_estimate=cost(m * w * 20 * rows * rank, m * w * rows * 24),
        compiler_params=grant(14),
    )(place, *ups, *dns, *args)


def weights_kernel(n, groups, rate, order_ref, *refs):
    ups, dns, ys = refs[:n], refs[n : 2 * n], refs[2 * n : 2 * n + len(groups)]
    w_ref, l1_ref, l2_ref, norm_ref, *totals, w_out, right_out, buf, sem, update = refs[2 * n + len(groups) :]
    rank = right_out.shape[1]
    w = buf.shape[2] // 2
    total = totals[0][0:1]
    for ref in totals[1:]:
        total = total + ref[0:1]
    norm = jnp.sqrt(total + EPS)

    @pl.when(pl.program_id(0) == 0)
    def _():
        left = jnp.concatenate([l1_ref[...] / norm_ref[...], l2_ref[...] / norm], axis=1)
        update[...] = stacked(rate * left)

    pieces = []
    for y_ref, group in zip(ys, groups):
        for j in range(group):
            i = len(pieces)
            rows = pl.ds(0, rank)
            pieces.append([(ups[i].at[rows, :], 0, 0), (dns[i].at[rows, :], 0, w), (y_ref.at[j], rank, 0)])
    y = fetcher(pieces, buf, sem)
    w_out[...] = w_ref[...] - dot3(update[...], halves(y))
    right_out[...] = y[rank:].T / norm


def finish(place, steps, ups, dns, ys, weights, l1, l2, norm, totals, rate):
    n = len(ups)
    rows, cols = weights.shape
    rank = l1.shape[1]
    w = cols // n
    groups = tuple(y.shape[0] for y in ys)
    at = chunk_at(steps, n)
    block = pl.BlockSpec((rows, w), lambda k, place: (0, at(k, place)))
    return pl.pallas_call(
        functools.partial(weights_kernel, n, groups, rate),
        out_shape=[
            jax.ShapeDtypeStruct((rows, cols), F32),
            jax.ShapeDtypeStruct((cols, rank), F32),
        ],
        grid_spec=pltpu.PrefetchScalarGridSpec(
            num_scalar_prefetch=1,
            grid=(n,),
            in_specs=[VMEM] * (2 * n + len(ys))
            + [block, whole((rows, rank)), whole((rows, rank)), whole((1, rank))]
            + [whole((8, rank))] * len(totals),
            out_specs=[block, pl.BlockSpec((w, rank), lambda k, place: (at(k, place), 0))],
            scratch_shapes=[
                pltpu.VMEM((2, 2 * rank, w), F32),
                pltpu.SemaphoreType.DMA((2, 3)),
                pltpu.VMEM((2 * rows, 2 * rank), BF16),
            ],
        ),
        cost_estimate=cost(12 * rows * cols * rank, 32 * rows * cols),
        compiler_params=grant(28),
        name="finish",
    )(place, *ups, *dns, *ys, weights, l1, l2, norm, *totals)


def whole(shape):
    return pl.BlockSpec(shape, lambda k, order: (0,) * len(shape))


def flip(x, axis, bits):
    size = lax.axis_size(axis)
    return lax.ppermute(x, axis, [(i, i ^ bits) for i in range(size)])


def rep_masks(reps, phase):
    single = [[1 << b] for b in range(reps.bit_length() - 1)]
    return single if phase == "reduce" else [[1, 2, 3]] + single[2:]


def all_sum_stages(box, phase):
    cols = lax.axis_size("col")
    masks = rep_masks(lax.axis_size("rep"), phase)

    def send(x, axis, partners):
        return [flip(part, axis, p) for part, p in zip(x, partners)]

    def scatter():
        parts = box.pop("parts")
        box["x"] = parts[0]
        box["pending"] = send(parts[1:], "col", range(1, cols))

    def exchange(i):
        def stage():
            x = box["x"] = alike([box["x"]] + box.pop("pending"))
            if i < len(masks):
                box["pending"] = send([x] * len(masks[i]), "rep", masks[i])
            else:
                box["pending"] = send([x] * (cols - 1), "col", range(1, cols))

        return stage

    return [scatter] + [exchange(i) for i in range(len(masks) + 1)]


def ring_shards(rate, momentum, grads, weights, right_factor):
    n, count = lax.axis_size("rep"), lax.axis_size("col")
    _, rows, _ = momentum.shape
    rank = right_factor.shape[1]
    ring = list(range(0, n, 2)) + list(range(n - 1, 0, -2))
    rep = lax.axis_index("rep")
    place = jnp.where(rep % 2 == 0, rep // 2, n - 1 - rep // 2).astype(jnp.int32)[None]
    ahead = [(ring[i], ring[(i + 1) % n]) for i in range(n)]
    back = [(b, a) for a, b in ahead]
    me = lax.axis_index("col").astype(jnp.int32)[None]

    def tie(box, *arrays):
        keys = [k for k in box if k != "pending"]
        tied = lax.optimization_barrier(([box[k] for k in keys], list(arrays)))
        box.update(zip(keys, tied[0]))
        return tied[1]

    def step(up, dn):
        up = lax.ppermute(up, "rep", ahead)
        dn = lax.ppermute(dn, "rep", back)
        return up, dn

    def first(scaled):
        def stage():
            out = orth_first(me, [box.pop("x")] + box.pop("pending"), rows, scaled)
            box["left"], box["rest"] = out[:2]
            if scaled:
                box["norm"] = out[2]

        return stage

    box = {}
    stages = all_sum_stages(box, "reduce")

    def begin():
        out = combine(me, momentum, grads, right_factor, n, count)
        box["up_all"], box["dn_all"], box["both"] = out[:3]
        box["parts"] = list(out[3])

    def second():
        box["left"], box["leftt"] = orth_second(box.pop("left"), box.pop("rest"))

    work = [[begin], stages[:2]] + [[stage] for stage in stages[2:]] + [[first(False)], [second]]
    up, dn = lead(place, momentum, grads, n)
    for k in range(1, n):
        up, dn = step(up, dn)
        if work:
            for stage in work.pop(0):
                stage()
            (up,) = tie(box, up)
        if k < n - 1:
            up = ring_add(place, n - 1 - k, up, box["up_all"])
            dn = ring_add(place, 1 + k, dn, box["dn_all"])
    l1 = box["left"]
    both = box["both"]
    up, dn = reduced(place, up, dn, box["up_all"], box["dn_all"], l1, box["leftt"], n)

    box = {}
    mine = (up, dn)
    stages = all_sum_stages(box, "gather")

    def begin_again():
        box["parts"] = list(partial_raw(me, *mine, rank, count))

    ups, dns = [up], [dn]
    ready, ys, totals = [], [], []

    def advance_ready(last=False):
        new = [c for c in range(n) if c not in ready and c < len(ups) and (n - c) % n < len(dns)]
        ready.extend(new)
        sides = ([ups[c] for c in new], [dns[(n - c) % n] for c in new])
        factors = (l1, box["left"], box["leftt"])
        if not last:
            done = box.get("done")
            box["done"], y, squares = advance("both", place, new, n, *sides, both, done, None, *factors)
            ys.append(y)
            totals.append(squares)
            return None
        y, squares = advance("project", place, new, n, *sides, both, None, None, *factors)
        ys.append(y)
        totals.append(squares)
        total = alike_total(totals, count)
        (box["done"],) = advance("moment", place, new, n, *sides, both, box.get("done"), y, *factors)
        return total

    work = [[begin_again, stages[0]]] + [[stage] for stage in stages[1:]] + [[first(True)], [second]]
    for _ in range(1, n):
        up, dn = step(up, dn)
        if work:
            for stage in work.pop(0):
                stage()
            (up,) = tie(box, up)
        else:
            advance_ready()
            (up,) = tie(box, up)
        ups.append(up)
        dns.append(dn)
    total = advance_ready(last=True)
    sides = ([ups[c] for c in ready], [dns[(n - c) % n] for c in ready])
    new_weights, new_right = finish(place, ready, *sides, ys, weights, l1, box["left"], box["norm"], [total], rate)
    return new_weights, box["done"], new_right


def alike_total(totals, count):
    total = totals[0]
    for other in totals[1:]:
        total = alike([total, other])
    got = [flip(total, "col", d) for d in range(1, count)]
    return alike([total] + got)


def plain_orthonormal(left_raw):
    zero = jnp.zeros((1,), jnp.int32)
    left, rest = orth_first(zero, [left_raw], left_raw.shape[0], False)
    return orth_second(left, rest)[0]


def plain_shards(rate, momentum, grads, weights, right_factor):
    n = lax.axis_size("rep")
    moment = momentum[0]
    combined = moment + grads[0, 0].astype(F32)
    averaged, later = lax.psum((combined / n, grads[1, 0].astype(F32) / n), "rep")
    for step in range(STEPS):
        if step > 0:
            combined = moment + grads[step, 0].astype(F32)
            averaged = averaged + later
        left = plain_orthonormal(lax.psum(dot(averaged, right_factor), "col"))
        right_raw = dot(averaged, left, 0, 0)
        correction = DAMPING * dot(left, right_raw, 1, 1)
        moment = combined - correction
        averaged = averaged - correction
        totals = lax.psum(jnp.sum(right_raw * right_raw, axis=0), "col")
        right_factor = right_raw / jnp.sqrt(totals + EPS)
        weights = weights - rate * dot(left, right_factor, 1, 1)
    return weights, moment[None], right_factor


def solution(mesh):
    def body(momentum, grads, weights, right_factor):
        rep, col = mesh.shape["rep"], mesh.shape["col"]
        _, rows, cols = momentum.shape
        rank = right_factor.shape[1]
        rate = RATE * math.sqrt(rows * cols / rank)
        powers = rep & (rep - 1) == 0 and col & (col - 1) == 0 and col > 1
        fits = cols % (2 * LANES * rep * col) == 0 and rows % (8 * col) == 0
        ring = powers and 4 < rep <= 16 and col <= 8 and fits

        def shards(*args):
            return (ring_shards if ring else plain_shards)(rate, *args)

        step = jax.shard_map(
            shards,
            mesh=mesh,
            in_specs=(
                P("rep", None, "col"),
                P(None, "rep", None, "col"),
                P(None, "col"),
                P("col", None),
            ),
            out_specs=(P(None, "col"), P("rep", None, "col"), P("col", None)),
            check_vma=False,
        )
        return step(momentum, grads, weights, right_factor)

    return body
```
